32 devices in a mesh: dp: 2 (over x), ctx: 4 (over y, core), tensor: 4 (over z).
Axes of the slice: x: 2, y: 2, z: 4, core: 2. Of those that a mesh axis runs over, the one named last changes fastest.
Arguments:
- tokens: bfloat16 [2, 4096, 768], P('dp', 'ctx'), may hold values from -6 to 6
- segment_ids: int32 [2, 4096], P('dp'), may hold values from 0 to 4, never falling along the last dimension, each value on 1 to 2000 neighbouring positions
- routes: int32 [2, 4096, 2], P('dp', 'ctx'), may hold values from 0 to 15, all different within a row
- pair_order: int32 [2, 4, 2048], P('dp', 'ctx'), may hold values from 0 to 2047, each once within a row
- gain_attn: bfloat16 [768], P(('dp', 'ctx')), may hold values from 0.099609375 to 1.8984375
- qkv_weight: bfloat16 [3, 768, 768], P(None, ('dp', 'ctx'), 'tensor'), may hold values from -0.21875 to 0.21875
- out_weight: bfloat16 [768, 768], P(('dp', 'ctx'), 'tensor'), may hold values from -2 to 2
- gain_ffn: bfloat16 [768], P(('dp', 'ctx')), may hold values from 0.099609375 to 1.8984375
- router_weight: bfloat16 [768, 16], P(('dp', 'ctx')), may hold values from -0.15625 to 0.15625
- shared_in: bfloat16 [2, 768, 2048], P(None, ('dp', 'ctx'), 'tensor'), may hold values from -0.21875 to 0.21875
- shared_out: bfloat16 [768, 2048], P(('dp', 'ctx'), 'tensor'), may hold values from -0.125 to 0.125
- expert_in: bfloat16 [16, 2, 768, 2048], P('dp', None, 'ctx', 'tensor'), may hold values from -0.21875 to 0.21875
- expert_out: bfloat16 [16, 768, 2048], P('dp', 'ctx', 'tensor'), may hold values from -0.125 to 0.125
- out_grad: bfloat16 [2, 4096, 768], P('dp', 'ctx'), may hold values from -6 to 6
Outputs:
- layer_out: bfloat16 [2, 4096, 768], P('dp', 'ctx')
- grad_tokens: float32 [2, 4096, 768], P('dp', 'ctx')
- grad_gain_attn: float32 [768], P(('dp', 'ctx'))
- grad_qkv: float32 [3, 768, 768], P(None, ('dp', 'ctx'), 'tensor')
- grad_out_weight: float32 [768, 768], P(('dp', 'ctx'), 'tensor')
- grad_gain_ffn: float32 [768], P(('dp', 'ctx'))
- grad_router: float32 [768, 16], P(('dp', 'ctx'))
- grad_shared_in: float32 [2, 768, 2048], P(None, ('dp', 'ctx'), 'tensor')
- grad_shared_out: float32 [768, 2048], P(('dp', 'ctx'), 'tensor')
- grad_expert_in: float32 [16, 2, 768, 2048], P('dp', None, 'ctx', 'tensor')
- grad_expert_out: float32 [16, 768, 2048], P('dp', 'ctx', 'tensor')
The draws below stay inside these ranges and needn't reach their ends.
Inputs may be any that keep to these rules, and one draw needn't show every extreme that they name: `segment_ids`: along a sequence the document numbers never fall; a document spans at most 2000 consecutive tokens, and in every sequence one spans exactly that many. The two routes of a token name different experts. `pair_order`: for every sequence and routing group, a permutation of the numbers of its 2048 pairs.
All inputs are finite; a program needn't handle non-finite values.
Results may differ from the reference program's by a relative error of at most 0.015.
Values may be sent and summed in bfloat16 or wider, within the bound.
No kernel may reach another device: no remote copies, remote signals or barrier semaphores. Data moves between devices by JAX's collectives and lax.ppermute only.
A program may use at most 256 MiB of HBM per device.

```python
import math
import jax
import jax.numpy as jnp
import numpy as np
from jax import lax

D = 768
HEADS = 12
HD = 64
EXPERTS = 16
EFF = 2048
SFF = 2048
LEN = 4096
SEQS = 2
GROUPS = 4
GROUP = 1024
CAP = 160
DOC_MOST = 2000
DOCS = 5


def block_levels(rng, dims, split, smallest, high):
    loudness, own = 1.0, jax.random.fold_in(rng, 6)
    for dim, shards_of in split:
        steps = jnp.exp(jax.random.uniform(jax.random.fold_in(own, dim), (shards_of,), jnp.float32, smallest / len(split), high / len(split)))
        loudness = loudness * jnp.repeat(steps, dims[dim] // shards_of).reshape([-1 if axis == dim else 1 for axis in range(len(dims))])
    return loudness


def choose_distinct(stream_key, rows, amount, top, lift):
    order = jax.random.permutation(jax.random.fold_in(stream_key, 1), amount)
    boost = order
    for power in range(3):
        boost = boost * boost // amount
    boost = boost * lift // amount
    chance = jax.random.randint(jax.random.fold_in(stream_key, 2), (rows, amount), 0, 4096) + boost
    fixed_rows = jax.random.permutation(jax.random.fold_in(stream_key, 3), rows)[jnp.arange(amount) % rows]
    chance = jnp.where(jnp.arange(rows)[:, None] == fixed_rows[None, :], 1 << 14, chance)
    merit = chance * amount + jnp.arange(amount)
    return lax.top_k(merit.astype(jnp.int32), top)[1].astype(jnp.int32)


def length_profile(count, total, most, lean):
    weights = [(1 << 20) // math.isqrt(rank ** lean) + 1 for rank in range(2, count + 1)]
    surplus, holding = total - most - (count - 1), [1] * (count - 1)
    while surplus > 0:
        movable = [i for i in range(count - 1) if holding[i] < most]
        mass, left = sum([weights[i] for i in movable]), surplus
        for i in movable:
            more = min(most - holding[i], max(1, left * weights[i] // mass), surplus)
            holding[i] = holding[i] + more
            surplus = surplus - more
    return np.array([most] + holding)


def ragged(rng, number_of, total, most, slope):
    if number_of == 2:
        one = jax.random.randint(rng, (), max(1, total - most), min(most, total - 1) + 1)
        return jnp.stack([one, total - one])
    lengths = jnp.asarray(length_profile(number_of, total, most, slope), jnp.int32)
    twos = (number_of - 1) // 2
    giver, receiver = lengths[1:1 + 2 * twos:2], lengths[2:2 + 2 * twos:2]
    slack = jnp.minimum(giver - 1, most - receiver)
    moved = jax.random.randint(jax.random.fold_in(rng, 1), (twos,), 0, 1 << 20) % (slack + 1)
    lengths = lengths.at[1:1 + 2 * twos:2].set(giver - moved).at[2:2 + 2 * twos:2].set(receiver + moved)
    return lengths[jax.random.permutation(jax.random.fold_in(rng, 2), number_of)]


def centred(stream_key, dims, scale, limit, split=(), kind=jnp.bfloat16):
    values = jax.random.normal(stream_key, dims, jnp.float32) * scale
    if len(split) > 0:
        values = block_levels(stream_key, dims, split, -0.22, 0.18) * values
    return jnp.clip(values, min=-limit, max=limit).astype(kind)


def setup_inputs(seed: int = 0) -> dict:
    key_list = jax.random.split(jax.random.key(seed), 15)
    tokens = centred(key_list[0], (SEQS, LEN, D), 1.0, 6.0, ((0, 2), (1, 4)))
    segment_ids = jax.vmap(lambda own: jnp.searchsorted(jnp.cumsum(ragged(own, DOCS, LEN, DOC_MOST, 1)), jnp.arange(LEN), side="right"))(jax.random.split(key_list[1], SEQS)).reshape((SEQS, LEN)).astype(jnp.int32)
    routes = choose_distinct(key_list[2], SEQS * LEN, EXPERTS, 2, 1024).reshape((SEQS, LEN, 2))
    pair_order = jax.vmap(lambda own: jax.random.permutation(own, 2 * GROUP))(jax.random.split(key_list[3], SEQS * GROUPS)).reshape((SEQS, GROUPS, 2 * GROUP)).astype(jnp.int32)
    gain_attn = jnp.clip(1.0 + 0.18 * jax.random.normal(key_list[4], (D,), jnp.float32), 0.099609375, 1.8984375).astype(jnp.bfloat16)
    qkv_weight = centred(key_list[5], (3, D, HEADS * HD), D ** -0.5, 0.21875, ((1, 8), (2, 4)))
    out_weight = centred(key_list[6], (D, HEADS * HD), 8 ** -0.5, 2.0, ((0, 8), (1, 4)))
    gain_ffn = jnp.clip(1.0 + 0.18 * jax.random.normal(key_list[7], (D,), jnp.float32), 0.099609375, 1.8984375).astype(jnp.bfloat16)
    router_weight = centred(key_list[8], (D, EXPERTS), (2 * D) ** -0.5, 0.15625, ((0, 8),))
    shared_in = centred(key_list[9], (2, D, SFF), D ** -0.5, 0.21875, ((1, 8), (2, 4)))
    shared_out = centred(key_list[10], (D, SFF), SFF ** -0.5, 0.125, ((0, 8), (1, 4)))
    expert_in = centred(key_list[11], (EXPERTS, 2, D, EFF), D ** -0.5, 0.21875, ((0, 2), (2, 4), (3, 4)))
    expert_out = centred(key_list[12], (EXPERTS, D, EFF), EFF ** -0.5, 0.125, ((0, 2), (1, 4), (2, 4)))
    out_grad = centred(key_list[13], (SEQS, LEN, D), 1.0, 6.0, ((0, 2), (1, 4)))
    return dict(tokens=tokens, segment_ids=segment_ids, routes=routes, pair_order=pair_order, gain_attn=gain_attn, qkv_weight=qkv_weight, out_weight=out_weight, gain_ffn=gain_ffn, router_weight=router_weight, shared_in=shared_in, shared_out=shared_out, expert_in=expert_in, expert_out=expert_out, out_grad=out_grad)


EPSILON = 1e-06
PRECISION = lax.Precision.HIGHEST

@jax.custom_vjp
def low(v):
    return lax.optimization_barrier(v.astype(jnp.bfloat16)).astype(jnp.float32)

@jax.custom_vjp
def low_back(v):
    return v

def low_keep(v):
    return (low(v), None)

def low_pass(kept, grad):
    return (grad,)

def back_keep(v):
    return (v, None)

def back_low(kept, grad):
    return (low(grad),)
low.defvjp(low_keep, low_pass)
low_back.defvjp(back_keep, back_low)

def rms_norm(values, norm_gain):
    return values * lax.rsqrt(lax.optimization_barrier(jnp.mean(values * values, axis=-1, keepdims=True)) + EPSILON) * norm_gain

def rope_tables(positions, head_size):
    half_size = head_size // 2
    inverse = 1.0 / 10000.0 ** (jnp.arange(half_size, dtype=jnp.float32) * (2.0 / head_size))
    angles = positions.astype(jnp.float32)[:, None] * inverse[None, :]
    return (jnp.cos(angles)[:, None, :], jnp.sin(angles)[:, None, :])

def rotate(values, cos_table, sin_table):
    half_size = values.shape[-1] // 2
    first_half = values[..., :half_size]
    second_half = values[..., half_size:]
    return jnp.concatenate([first_half * cos_table - second_half * sin_table, second_half * cos_table + first_half * sin_table], axis=-1)

def slot_tables(group_routes, group_order, experts, capacity):
    pair_count = group_order.shape[0]
    pair_expert = group_routes.reshape(pair_count).astype(jnp.int32)
    ranked = pair_expert[group_order]
    onehot = (ranked[:, None] == jnp.arange(experts, dtype=jnp.int32)[None, :]).astype(jnp.int32)
    earlier = jnp.cumsum(onehot, axis=0, dtype=jnp.int32) - onehot
    ranked_slot = lax.optimization_barrier(jnp.sum(earlier * onehot, axis=1, dtype=jnp.int32))
    slot_index = jnp.zeros((pair_count,), jnp.int32).at[group_order].set(ranked_slot)
    pair_place = jnp.where(slot_index < capacity, pair_expert * capacity + slot_index, experts * capacity).astype(jnp.int32)
    slot_pair = jnp.full((experts * capacity,), pair_count, jnp.int32).at[pair_place].set(jnp.arange(pair_count, dtype=jnp.int32), mode='drop')
    return (pair_place, slot_pair)

def attend_block(query_block, query_pos, query_seg, key_rows, value_rows, key_seg):
    raw_scores = jnp.einsum('qhd,khd->hqk', query_block, key_rows, precision=PRECISION) * (1.0 / math.sqrt(HD))
    key_pos = jnp.arange(key_rows.shape[0], dtype=jnp.int32)
    allowed = (key_pos[None, :] <= query_pos[:, None]) & (key_seg[None, :] == query_seg[:, None])
    scores = jnp.where(allowed[None, :, :], low_back(raw_scores), -1e+30)
    row_peak = lax.optimization_barrier(jnp.max(scores, axis=-1, keepdims=True))
    exponent = jnp.exp(scores - row_peak)
    attn_probs = low(exponent / lax.optimization_barrier(jnp.sum(exponent, axis=-1, keepdims=True)))
    return jnp.einsum('hqk,khd->qhd', attn_probs, value_rows, precision=PRECISION)

def group_moe(normed_group, gate_group, routes_group, order_group, expert_in, expert_out):
    pair_place, slot_pair = slot_tables(routes_group, order_group, EXPERTS, CAP)
    padded = jnp.concatenate([normed_group, jnp.zeros((1, D), jnp.float32)], axis=0)
    slot_rows = padded[slot_pair // 2].reshape(EXPERTS, CAP, D)
    gate_pre = low_back(jnp.einsum('ecd,edf->ecf', slot_rows, expert_in[:, 0], precision=PRECISION))
    up_pre = low_back(jnp.einsum('ecd,edf->ecf', slot_rows, expert_in[:, 1], precision=PRECISION))
    hidden = low(jax.nn.silu(gate_pre) * up_pre)
    expert_y = low_back(jnp.einsum('ecf,edf->ecd', hidden, expert_out, precision=PRECISION))
    flat_rows = jnp.concatenate([expert_y.reshape(EXPERTS * CAP, D), jnp.zeros((1, D), jnp.float32)], axis=0)
    paired = flat_rows[pair_place].reshape(GROUP, 2, D)
    return lax.optimization_barrier(jnp.sum(gate_group[:, :, None] * paired, axis=1))

def layer_sequence(inputs, seg_ids, seq_routes, seq_order, weights):
    gain_attn, qkv_weight, out_weight, gain_ffn, router_weight, shared_in, shared_out, expert_in, expert_out = weights
    seq_len = inputs.shape[0]
    normed = low(rms_norm(inputs, gain_attn))
    q_raw = low_back(jnp.dot(normed, qkv_weight[0], precision=PRECISION)).reshape(seq_len, HEADS, HD)
    k_raw = low_back(jnp.dot(normed, qkv_weight[1], precision=PRECISION)).reshape(seq_len, HEADS, HD)
    v_raw = low_back(jnp.dot(normed, qkv_weight[2], precision=PRECISION)).reshape(seq_len, HEADS, HD)
    positions = jnp.arange(seq_len, dtype=jnp.int32)
    cos_table, sin_table = rope_tables(positions, HD)
    query_rot = low(rotate(q_raw, cos_table, sin_table))
    key_rows = low(rotate(k_raw, cos_table, sin_table))
    value_rows = low(v_raw)
    block_rows = 512 if seq_len % 512 == 0 else seq_len
    block_count = seq_len // block_rows
    attend = jax.checkpoint(attend_block)
    attended = lax.map(lambda blocks: attend(blocks[0], blocks[1], blocks[2], key_rows, value_rows, seg_ids), (query_rot.reshape(block_count, block_rows, HEADS, HD), positions.reshape(block_count, block_rows), seg_ids.reshape(block_count, block_rows)))
    attended = low(low_back(attended.reshape(seq_len, HEADS * HD)))
    branch = low_back(jnp.dot(attended, out_weight.T, precision=PRECISION))
    residual = inputs + branch
    normed2 = low(rms_norm(residual, gain_ffn))
    logits = low_back(jnp.dot(normed2, router_weight, precision=PRECISION))
    chosen = jnp.take_along_axis(logits, seq_routes, axis=1)
    chosen_peak = lax.optimization_barrier(jnp.max(chosen, axis=1, keepdims=True))
    chosen_exp = jnp.exp(chosen - chosen_peak)
    gate_probs = chosen_exp / lax.optimization_barrier(jnp.sum(chosen_exp, axis=1, keepdims=True))
    combined = jax.vmap(group_moe, in_axes=(0, 0, 0, 0, None, None))(normed2.reshape(GROUPS, GROUP, D), gate_probs.reshape(GROUPS, GROUP, 2), seq_routes.reshape(GROUPS, GROUP, 2), seq_order, expert_in, expert_out).reshape(seq_len, D)
    s_gate = low_back(jnp.dot(normed2, shared_in[0], precision=PRECISION))
    s_up = low_back(jnp.dot(normed2, shared_in[1], precision=PRECISION))
    shared_hidden = low(jax.nn.silu(s_gate) * s_up)
    shared_y = low_back(jnp.dot(shared_hidden, shared_out.T, precision=PRECISION))
    return residual + (combined + shared_y)

def reference(tokens, segment_ids, routes, pair_order, gain_attn, qkv_weight, out_weight, gain_ffn, router_weight, shared_in, shared_out, expert_in, expert_out, out_grad):
    weights = tuple((weight_array.astype(jnp.float32) for weight_array in (gain_attn, qkv_weight, out_weight, gain_ffn, router_weight, shared_in, shared_out, expert_in, expert_out)))

    def forward(inputs, weight_list):
        return lax.map(lambda seq_items: layer_sequence(seq_items[0], seq_items[1], seq_items[2], seq_items[3], weight_list), (inputs, segment_ids, routes, pair_order))
    layer_out, pullback = jax.vjp(forward, tokens.astype(jnp.float32), weights)
    grad_tokens, grad_weights = pullback(out_grad.astype(jnp.float32))
    return (layer_out.astype(jnp.bfloat16), grad_tokens, grad_weights[0], grad_weights[1], grad_weights[2], grad_weights[3], grad_weights[4], grad_weights[5], grad_weights[6], grad_weights[7], grad_weights[8])
```

```python
import functools
import math

import jax
import jax.numpy as jnp
from jax import lax
from jax.experimental import pallas as pl
from jax.experimental.pallas import tpu as pltpu
from jax.sharding import PartitionSpec as P

HD = 64
HALF = HD // 2
EPSILON = 1e-06
LONGEST = 2000
DOCS = 5
BQ = 256
BK = 256
BF = jnp.bfloat16
F32 = jnp.float32
NEG = -1e30
DC = ("dp", "ctx")


def mm(a, b, ca, cb):
    return lax.dot_general(a, b, (((ca,), (cb,)), ((), ())), preferred_element_type=F32)


def attn_mask(scores_t, key_start, query_start, doc_row):
    rows, cols = scores_t.shape
    kpos = key_start + lax.broadcasted_iota(jnp.int32, (rows, cols), 0)
    qpos = query_start + lax.broadcasted_iota(jnp.int32, (rows, cols), 1)
    return (kpos <= qpos) & (kpos >= doc_row)


def attn_fwd_kernel(lo_ref, q_ref, k_ref, v_ref, doc_ref, o_ref, lse_ref, *, shift):
    rows = q_ref.shape[1]
    for qb in range(rows // BQ):
        qt = q_ref[:, qb * BQ : (qb + 1) * BQ]
        doc = doc_ref[:, qb * BQ : (qb + 1) * BQ]
        q0 = shift + qb * BQ

        def step(b, carry, qt=qt, doc=doc, q0=q0):
            peak, total, acc = carry
            off = pl.multiple_of(b * BK, BK)
            kt = k_ref[:, pl.ds(off, BK)]
            vt = v_ref[:, pl.ds(off, BK)]
            s = mm(kt, qt, 0, 0) * 0.125
            s = jnp.where(attn_mask(s, off, q0, doc), s, NEG)
            new = jnp.maximum(peak, jnp.max(s, axis=0, keepdims=True))
            p = jnp.exp(s - new)
            fix = jnp.exp(peak - new)
            total = total * fix + jnp.sum(p, axis=0, keepdims=True)
            acc = acc * fix + mm(vt, p.astype(BF), 1, 0)
            return new, total, acc

        init = (
            jnp.full((1, BQ), NEG, F32),
            jnp.zeros((1, BQ), F32),
            jnp.zeros((HD, BQ), F32),
        )
        last = (q0 + BQ - 1) // BK
        carry = step(last, init)
        peak, total, acc = lax.fori_loop(lo_ref[qb], last, step, carry)
        o_ref[:, qb * BQ : (qb + 1) * BQ] = (acc / total).astype(BF)
        lse_ref[0, :, qb * BQ : (qb + 1) * BQ] = peak + jnp.log(total)


def attn_bwd_kernel(
    lo_ref, q_ref, k_ref, v_ref, o_ref, do_ref, lse_ref, doc_ref, dq_ref, dk_ref, dv_ref, *, shift
):
    rows = q_ref.shape[1]
    dk_ref[...] = jnp.zeros_like(dk_ref)
    dv_ref[...] = jnp.zeros_like(dv_ref)
    for qb in range(rows // BQ):
        cols = slice(qb * BQ, (qb + 1) * BQ)
        qt = q_ref[:, cols]
        dot = do_ref[:, cols]
        doc = doc_ref[:, cols]
        lse = lse_ref[0, :, cols]
        delta = jnp.sum(dot.astype(F32) * o_ref[:, cols].astype(F32), axis=0, keepdims=True)
        q0 = shift + qb * BQ

        def step(b, dq, qt=qt, dot=dot, doc=doc, lse=lse, delta=delta, q0=q0):
            off = pl.multiple_of(b * BK, BK)
            kt = k_ref[:, pl.ds(off, BK)]
            vt = v_ref[:, pl.ds(off, BK)]
            s = mm(kt, qt, 0, 0) * 0.125
            s = jnp.where(attn_mask(s, off, q0, doc), s, NEG)
            p = jnp.exp(s - lse)
            dp = mm(vt, dot, 0, 0)
            ds = (p * (dp - delta)).astype(BF)
            dk_ref[:, pl.ds(off, BK)] += mm(qt, ds, 1, 1)
            dv_ref[:, pl.ds(off, BK)] += mm(dot, p.astype(BF), 1, 1)
            return dq + mm(kt, ds, 1, 0)

        last = (q0 + BQ - 1) // BK
        dq = lax.fori_loop(lo_ref[qb], last + 1, step, jnp.zeros((HD, BQ), F32))
        dq_ref[:, cols] = dq * 0.125
    dk_ref[...] = dk_ref[...] * 0.125


def head_spec(width):
    return pl.BlockSpec((HD, width), lambda h, lo: (h, 0))


def attn_forward(lo, q_t, k_t, v_t, doc, shift):
    cols, rows = q_t.shape
    window = k_t.shape[1]
    heads = cols // HD
    return pl.pallas_call(
        functools.partial(attn_fwd_kernel, shift=shift),
        out_shape=(
            jax.ShapeDtypeStruct((cols, rows), BF),
            jax.ShapeDtypeStruct((heads, 1, rows), F32),
        ),
        grid_spec=pltpu.PrefetchScalarGridSpec(
            num_scalar_prefetch=1,
            grid=(heads,),
            in_specs=[
                head_spec(rows),
                head_spec(window),
                head_spec(window),
                pl.BlockSpec((1, rows), lambda h, lo: (0, 0)),
            ],
            out_specs=[
                head_spec(rows),
                pl.BlockSpec((1, 1, rows), lambda h, lo: (h, 0, 0)),
            ],
        ),
        name="attn_fwd",
    )(lo, q_t, k_t, v_t, doc)


def attn_backward(lo, q_t, k_t, v_t, o_t, do_t, lse, doc, shift):
    cols, rows = q_t.shape
    window = k_t.shape[1]
    heads = cols // HD
    return pl.pallas_call(
        functools.partial(attn_bwd_kernel, shift=shift),
        out_shape=(
            jax.ShapeDtypeStruct((cols, rows), F32),
            jax.ShapeDtypeStruct((cols, window), F32),
            jax.ShapeDtypeStruct((cols, window), F32),
        ),
        grid_spec=pltpu.PrefetchScalarGridSpec(
            num_scalar_prefetch=1,
            grid=(heads,),
            in_specs=[
                head_spec(rows),
                head_spec(window),
                head_spec(window),
                head_spec(rows),
                head_spec(rows),
                pl.BlockSpec((1, 1, rows), lambda h, lo: (h, 0, 0)),
                pl.BlockSpec((1, rows), lambda h, lo: (0, 0)),
            ],
            out_specs=[head_spec(rows), head_spec(window), head_spec(window)],
        ),
        name="attn_bwd",
    )(lo, q_t, k_t, v_t, o_t, do_t, lse, doc)


def ffn_kernel(*refs, gated):
    if gated:
        x_ref, g_ref, gate_ref, win_ref, wout_ref = refs[:5]
        y_ref, dx_ref, dgate_ref, gin_ref, gout_ref, acc_in, acc_out = refs[5:]
    else:
        x_ref, g_ref, win_ref, wout_ref = refs[:4]
        y_ref, dx_ref, gin_ref, gout_ref, acc_in, acc_out = refs[4:]
    src, _, rows, width = x_ref.shape
    step = pl.program_id(1)

    @pl.when(step == 0)
    def _():
        acc_in[...] = jnp.zeros_like(acc_in)
        acc_out[...] = jnp.zeros_like(acc_out)

    x = x_ref[...].reshape(src * rows, width)
    g = g_ref[...].reshape(src * rows, width)
    w_gate = win_ref[0, 0]
    w_up = win_ref[0, 1]
    w_out = wout_ref[0]
    gate_pre = mm(x, w_gate, 1, 0)
    up_pre = mm(x, w_up, 1, 0)
    sig = 1.0 / (1.0 + jnp.exp(-gate_pre))
    silu = gate_pre * sig
    hidden = (silu * up_pre).astype(BF)
    y = mm(hidden, w_out, 1, 1)
    if gated:
        gf = g.astype(F32)
        gate = gate_ref[...].reshape(src * rows, 1)
        dgate_ref[...] = jnp.sum(gf * y, axis=1, keepdims=True).reshape(src, 1, rows, 1)
        dy = (gate * gf).astype(BF)
    else:
        dy = g
    y_ref[...] = y.astype(BF).reshape(src, 1, rows, width)
    dh = mm(dy, w_out, 1, 0)
    dgp = (dh * up_pre * (sig * (1.0 + gate_pre * (1.0 - sig)))).astype(BF)
    dup = (dh * silu).astype(BF)
    dx = mm(dgp, w_gate, 1, 1) + mm(dup, w_up, 1, 1)
    dx_ref[...] = dx.astype(BF).reshape(src, 1, rows, width)
    acc_in[0] += mm(x, dgp, 0, 0)
    acc_in[1] += mm(x, dup, 0, 0)
    acc_out[...] += mm(dy, hidden, 0, 0)

    @pl.when(step == pl.num_programs(1) - 1)
    def _():
        gin_ref[0] = acc_in[...].astype(BF)
        gout_ref[0] = acc_out[...].astype(BF)


def ffn(x, g, gate, w_in, w_out, block):
    sources, experts, rows, width = x.shape
    units = w_out.shape[2]
    gated = gate is not None
    block = math.gcd(sources, block)
    big = pl.BlockSpec((block, 1, rows, width), lambda e, s: (s, e, 0, 0))
    thin = pl.BlockSpec((block, 1, rows, 1), lambda e, s: (s, e, 0, 0))
    w_in_spec = pl.BlockSpec((1, 2, width, units), lambda e, s: (e, 0, 0, 0))
    w_out_spec = pl.BlockSpec((1, width, units), lambda e, s: (e, 0, 0))
    wide = jax.ShapeDtypeStruct(x.shape, BF)
    outs = [wide, wide]
    out_specs = [big, big]
    if gated:
        outs.append(jax.ShapeDtypeStruct(gate.shape, F32))
        out_specs.append(thin)
    outs += [
        jax.ShapeDtypeStruct((experts, 2, width, units), BF),
        jax.ShapeDtypeStruct((experts, width, units), BF),
    ]
    out_specs += [w_in_spec, w_out_spec]
    return pl.pallas_call(
        functools.partial(ffn_kernel, gated=gated),
        out_shape=outs,
        grid=(experts, sources // block),
        in_specs=[big, big] + ([thin] if gated else []) + [w_in_spec, w_out_spec],
        out_specs=out_specs,
        scratch_shapes=[
            pltpu.VMEM((2, width, units), F32),
            pltpu.VMEM((width, units), F32),
        ],
        compiler_params=pltpu.CompilerParams(
            dimension_semantics=("arbitrary", "arbitrary"), vmem_limit_bytes=56 * 1024 * 1024
        ),
        name="ffn_experts" if gated else "ffn_shared",
    )(*([x, g] + ([gate] if gated else []) + [w_in, w_out]))


def pair_slots(pair_route, order, experts, capacity):
    count = order.shape[0]
    flat = pair_route.reshape(count)
    number = jnp.arange(count, dtype=jnp.int32)
    ids = jnp.arange(experts, dtype=jnp.int32)
    owner = (flat[:, None] == ids[None, :]).astype(BF)
    ranked = jnp.dot(
        (order[:, None] == number[None, :]).astype(BF), owner, preferred_element_type=F32
    ).astype(BF)
    earlier = jnp.dot(
        (number[None, :] < number[:, None]).astype(BF), ranked, preferred_element_type=F32
    )
    ranked_slot = (jnp.minimum(earlier, float(capacity)) * ranked).astype(BF)
    slot = jnp.sum(
        jnp.dot(
            (order[None, :] == number[:, None]).astype(BF),
            ranked_slot,
            preferred_element_type=F32,
        ),
        axis=1,
    ).astype(jnp.int32)
    place = jnp.where(slot < capacity, flat * capacity + slot, experts * capacity)
    return place.reshape(pair_route.shape)


def own_sum(parts, axis):
    devices = lax.axis_size(DC)
    shape = parts.shape
    cut = shape[:axis] + (devices, shape[axis] // devices) + shape[axis + 1 :]
    swapped = lax.all_to_all(
        parts.astype(BF).reshape(cut), DC, split_axis=axis, concat_axis=axis, tiled=True
    )
    return jnp.sum(swapped.astype(F32), axis=axis)


def half_turn(values_t, cos_t, sin_t):
    cols, rows = values_t.shape
    split = values_t.reshape(cols // HD, 2, HALF, rows)
    a, b = split[:, 0], split[:, 1]
    return jnp.stack([a * cos_t - b * sin_t, b * cos_t + a * sin_t], axis=1).reshape(cols, rows)


def shards(
    tokens,
    segment_ids,
    routes,
    pair_order,
    gain_attn,
    qkv_weight,
    out_weight,
    gain_ffn,
    router_weight,
    shared_in,
    shared_out,
    expert_in,
    expert_out,
    out_grad,
):
    rows, width = tokens.shape[1], tokens.shape[2]
    ctx_count = lax.axis_size("ctx")
    ctx_at = lax.axis_index("ctx")
    inputs = tokens[0].astype(F32)
    grad_low = out_grad[0]
    grad_layer = grad_low.astype(F32)
    seg_all = segment_ids[0]
    my_routes = routes[0]

    gains = jnp.stack([gain_attn, gain_ffn], axis=1)
    heads_cols = qkv_weight.shape[2]
    experts = router_weight.shape[1]
    qkv_full = lax.all_gather(qkv_weight, DC, axis=1, tiled=True)
    rest = jnp.concatenate([out_weight, router_weight, gains], axis=1)
    gains_full = lax.all_gather(gains, DC, axis=0, tiled=True).astype(F32)
    rest_full = lax.all_gather(rest, DC, axis=0, tiled=True)
    out_full = rest_full[:, :heads_cols]
    router_full = rest_full[:, heads_cols : heads_cols + experts]
    attn_gain = gains_full[:, 0]
    ffn_gain = gains_full[:, 1]
    shin_full = lax.all_gather(shared_in, DC, axis=1, tiled=True)
    shout_full = lax.all_gather(shared_out, DC, axis=0, tiled=True)

    local_experts = expert_in.shape[0]
    spread = local_experts % ctx_count == 0
    if spread:
        expert_axes = DC
        ein = lax.all_to_all(expert_in, "ctx", split_axis=0, concat_axis=2, tiled=True)
        eout = lax.all_to_all(expert_out, "ctx", split_axis=0, concat_axis=1, tiled=True)
    else:
        expert_axes = ("dp",)
        ein = lax.all_gather(expert_in, "ctx", axis=2, tiled=True)
        eout = lax.all_gather(expert_out, "ctx", axis=1, tiled=True)
    owners = lax.axis_size(expert_axes)
    own = experts // owners
    capacity = 10 * rows // (4 * experts)
    slots = experts * capacity

    def swap(values):
        return lax.all_to_all(values, expert_axes, split_axis=0, concat_axis=0, tiled=True)

    place = pair_slots(my_routes, pair_order[0, 0], experts, capacity)
    slot_ids = jnp.arange(slots, dtype=jnp.int32)
    hit0 = place[None, :, 0] == slot_ids[:, None]
    hit1 = place[None, :, 1] == slot_ids[:, None]
    to_slot = (hit0 | hit1).astype(BF)
    slot_g = jnp.dot(to_slot, grad_low, preferred_element_type=F32).astype(BF)
    got_g = swap(slot_g.reshape(owners, own, capacity, width))

    inv1 = lax.rsqrt(jnp.mean(inputs * inputs, axis=-1, keepdims=True) + EPSILON)
    n1 = inputs * inv1
    normed = (n1 * attn_gain).astype(BF)
    row_start = ctx_at * rows
    query_pos = row_start + jnp.arange(rows, dtype=jnp.int32)
    inverse = 1.0 / 10000.0 ** (jnp.arange(HALF, dtype=F32) * (2.0 / HD))
    angles = inverse[:, None] * query_pos.astype(F32)[None, :]
    cos_t, sin_t = jnp.cos(angles), jnp.sin(angles)
    raw_t = jnp.einsum("pdc,ld->pcl", qkv_full, normed, preferred_element_type=F32)
    q_t = half_turn(raw_t[0], cos_t, sin_t).astype(BF)
    k_t = half_turn(raw_t[1], cos_t, sin_t).astype(BF)
    v_t = raw_t[2].astype(BF)
    kv_t = jnp.concatenate([k_t, v_t], axis=0)
    before = min(ctx_count - 1, -(-(LONGEST - 1) // rows))
    shift = before * rows
    pieces = [kv_t]
    for hop in range(1, before + 1):
        links = [(i, i + hop) for i in range(ctx_count - hop)]
        pieces.insert(0, lax.ppermute(kv_t, "ctx", links))
    kv_win = jnp.concatenate(pieces, axis=1)
    k_win, v_win = kv_win[:heads_cols], kv_win[heads_cols:]
    starts = jnp.sum(
        seg_all[:, None] < jnp.arange(DOCS, dtype=jnp.int32)[None, :], axis=0, dtype=jnp.int32
    )
    query_seg = lax.dynamic_slice_in_dim(seg_all, row_start, rows)
    doc = jnp.sum(
        jnp.where(
            query_seg[:, None] == jnp.arange(DOCS, dtype=jnp.int32)[None, :], starts[None, :], 0
        ),
        axis=1,
    ) - (row_start - shift)
    lo = jnp.maximum(doc[::BQ], 0) // BK
    doc = doc[None, :]
    att_t, lse = attn_forward(lo, q_t, k_win, v_win, doc, shift)
    branch_part = jnp.einsum("cl,dc->ld", att_t, out_full, preferred_element_type=F32)
    branch = lax.psum(branch_part.astype(BF), "tensor").astype(F32)
    resid = inputs + branch

    inv2 = lax.rsqrt(jnp.mean(resid * resid, axis=-1, keepdims=True) + EPSILON)
    n2 = resid * inv2
    normed2 = (n2 * ffn_gain).astype(BF)
    slot_x = jnp.dot(to_slot, normed2, preferred_element_type=F32).astype(BF)
    got_x = swap(slot_x.reshape(owners, own, capacity, width))
    logits = jnp.dot(normed2, router_full, preferred_element_type=F32)
    picked = my_routes[:, :, None] == jnp.arange(experts, dtype=jnp.int32)[None, None, :]
    chosen = jnp.sum(jnp.where(picked, logits[:, None, :], 0.0), axis=2)
    chosen_exp = jnp.exp(chosen - jnp.max(chosen, axis=1, keepdims=True))
    gates = chosen_exp / jnp.sum(chosen_exp, axis=1, keepdims=True)
    slot_gate = jnp.sum(
        jnp.where(hit0, gates[None, :, 0], 0.0) + jnp.where(hit1, gates[None, :, 1], 0.0), axis=1
    )
    got_gate = swap(slot_gate.reshape(owners, own * capacity))

    parts = 4
    shared_shape = (parts, 1, rows // parts, width)
    sh_y, sh_dx, sh_gin, sh_gout = ffn(
        normed2.reshape(shared_shape),
        grad_low.reshape(shared_shape),
        None,
        shin_full[None],
        shout_full[None],
        2,
    )
    total_shin = own_sum(sh_gin[0], 1)
    total_shout = own_sum(sh_gout[0], 0)

    y, dx, dgate, g_ein, g_eout = ffn(
        got_x, got_g, got_gate.reshape(owners, own, capacity, 1), ein, eout, 4
    )
    back_dx = swap(dx).reshape(slots, width)
    back_dgate = swap(dgate.reshape(owners, own * capacity)).reshape(slots)
    back_y = swap(y).reshape(slots, width)
    if spread:
        grad_ein = lax.all_to_all(g_ein, "ctx", split_axis=2, concat_axis=0, tiled=True)
        grad_eout = lax.all_to_all(g_eout, "ctx", split_axis=1, concat_axis=0, tiled=True)
    else:
        grad_ein = lax.psum_scatter(g_ein, "ctx", scatter_dimension=2, tiled=True)
        grad_eout = lax.psum_scatter(g_eout, "ctx", scatter_dimension=1, tiled=True)

    at0 = place[:, 0, None] == slot_ids[None, :]
    at1 = place[:, 1, None] == slot_ids[None, :]
    dn2_part = jnp.dot((at0 | at1).astype(BF), back_dx, preferred_element_type=F32)
    dgates = jnp.stack(
        [
            jnp.sum(jnp.where(at0, back_dgate[None, :], 0.0), axis=1),
            jnp.sum(jnp.where(at1, back_dgate[None, :], 0.0), axis=1),
        ],
        axis=1,
    )
    dchosen = gates * (dgates - jnp.sum(gates * dgates, axis=1, keepdims=True))
    dlogits = jnp.sum(jnp.where(picked, dchosen[:, :, None], 0.0), axis=1).astype(BF)
    dn2_part = (
        dn2_part
        + sh_dx.reshape(rows, width).astype(F32)
        + jnp.einsum("le,de->ld", dlogits, router_full, preferred_element_type=F32)
    )
    dn2 = lax.psum(dn2_part.astype(BF), "tensor").astype(F32)
    router_part = jnp.einsum("ld,le->de", normed2, dlogits, preferred_element_type=F32)
    gain2_part = jnp.sum(dn2_part * n2, axis=0)

    scaled2 = ffn_gain * dn2
    dresid = grad_layer + inv2 * (scaled2 - n2 * jnp.mean(scaled2 * n2, axis=-1, keepdims=True))
    dbranch = dresid.astype(BF)
    datt_t = jnp.einsum("dc,ld->cl", out_full, dbranch, preferred_element_type=F32).astype(BF)

    weight0 = jnp.where(at0, gates[:, 0, None], 0.0)
    weight1 = jnp.where(at1, gates[:, 1, None], 0.0)
    ffn_part = jnp.dot(
        (weight0 + weight1).astype(BF), back_y, preferred_element_type=F32
    ) + sh_y.reshape(rows, width).astype(F32)
    ffn_total = lax.psum(ffn_part.astype(BF), "tensor").astype(F32)
    layer_out = (resid + ffn_total).astype(BF)

    dq_t, dk_win, dv_win = attn_backward(
        lo, q_t, k_win, v_win, att_t, datt_t, lse, doc, shift
    )
    dkv_win = jnp.concatenate([dk_win, dv_win], axis=0)
    dkv = dkv_win[:, shift:]
    for hop in range(1, before + 1):
        links = [(i + hop, i) for i in range(ctx_count - hop)]
        piece = dkv_win[:, shift - hop * rows : shift - (hop - 1) * rows]
        dkv = dkv + lax.ppermute(piece.astype(BF), "ctx", links).astype(F32)
    dq_raw = half_turn(dq_t, cos_t, -sin_t)
    dk_raw = half_turn(dkv[:heads_cols], cos_t, -sin_t)
    draw_t = jnp.stack([dq_raw, dk_raw, dkv[heads_cols:]], axis=0).astype(BF)
    dn1_part = jnp.einsum("pcl,pdc->ld", draw_t, qkv_full, preferred_element_type=F32)
    dn1 = lax.psum(dn1_part.astype(BF), "tensor").astype(F32)
    gain1_part = jnp.sum(dn1_part * n1, axis=0)
    scaled1 = attn_gain * dn1
    grad_tokens = dresid + inv1 * (
        scaled1 - n1 * jnp.mean(scaled1 * n1, axis=-1, keepdims=True)
    )

    grad_qkv = jnp.einsum("ld,pcl->dpc", normed, draw_t, preferred_element_type=F32)
    grad_outw = jnp.einsum("ld,cl->dc", dbranch, att_t, preferred_element_type=F32)
    small = jnp.concatenate([router_part, gain1_part[:, None], gain2_part[:, None]], axis=1)
    tail = own_sum(
        jnp.concatenate([grad_qkv.reshape(width, 3 * heads_cols), grad_outw, small], axis=1), 0
    )
    total_qkv = tail[:, : 3 * heads_cols].reshape(-1, 3, heads_cols).transpose(1, 0, 2)
    total_outw = tail[:, 3 * heads_cols : 4 * heads_cols]
    small = lax.psum(tail[:, 4 * heads_cols :], "tensor")
    return (
        layer_out[None],
        grad_tokens[None],
        small[:, experts],
        total_qkv,
        total_outw,
        small[:, experts + 1],
        small[:, :experts],
        total_shin,
        total_shout,
        grad_ein.astype(F32),
        grad_eout.astype(F32),
    )


def solution(mesh):
    return jax.shard_map(
        shards,
        mesh=mesh,
        in_specs=(
            P("dp", "ctx", None),
            P("dp", None),
            P("dp", "ctx", None),
            P("dp", "ctx", None),
            P(DC),
            P(None, DC, "tensor"),
            P(DC, "tensor"),
            P(DC),
            P(DC, None),
            P(None, DC, "tensor"),
            P(DC, "tensor"),
            P("dp", None, "ctx", "tensor"),
            P("dp", "ctx", "tensor"),
            P("dp", "ctx", None),
        ),
        out_specs=(
            P("dp", "ctx", None),
            P("dp", "ctx", None),
            P(DC),
            P(None, DC, "tensor"),
            P(DC, "tensor"),
            P(DC),
            P(DC, None),
            P(None, DC, "tensor"),
            P(DC, "tensor"),
            P("dp", None, "ctx", "tensor"),
            P("dp", "ctx", "tensor"),
        ),
        check_vma=False,
    )
```

```python
import functools
import math

import jax
import jax.numpy as jnp
from jax import lax
from jax.experimental import pallas as pl
from jax.experimental.pallas import tpu as pltpu
from jax.sharding import PartitionSpec as P

HD = 64
HALF = HD // 2
EPSILON = 1e-06
LONGEST = 2000
DOCS = 5
BQ = 256
BK = 256
BF = jnp.bfloat16
F32 = jnp.float32
NEG = -1e30
DC = ("dp", "ctx")


def mm(a, b, ca, cb):
    return lax.dot_general(a, b, (((ca,), (cb,)), ((), ())), preferred_element_type=F32)


def attn_mask(scores_t, key_start, query_start, doc_row):
    rows, cols = scores_t.shape
    kpos = key_start + lax.broadcasted_iota(jnp.int32, (rows, cols), 0)
    qpos = query_start + lax.broadcasted_iota(jnp.int32, (rows, cols), 1)
    return (kpos <= qpos) & (kpos >= doc_row)


def attn_fwd_kernel(lo_ref, q_ref, k_ref, v_ref, doc_ref, o_ref, lse_ref, *, shift):
    rows = q_ref.shape[1]
    for qb in range(rows // BQ):
        qt = q_ref[:, qb * BQ : (qb + 1) * BQ]
        doc = doc_ref[:, qb * BQ : (qb + 1) * BQ]
        q0 = shift + qb * BQ

        def step(b, carry, qt=qt, doc=doc, q0=q0):
            peak, total, acc = carry
            off = pl.multiple_of(b * BK, BK)
            kt = k_ref[:, pl.ds(off, BK)]
            vt = v_ref[:, pl.ds(off, BK)]
            s = mm(kt, qt, 0, 0) * 0.125
            s = jnp.where(attn_mask(s, off, q0, doc), s, NEG)
            new = jnp.maximum(peak, jnp.max(s, axis=0, keepdims=True))
            p = jnp.exp(s - new)
            fix = jnp.exp(peak - new)
            total = total * fix + jnp.sum(p, axis=0, keepdims=True)
            acc = acc * fix + mm(vt, p.astype(BF), 1, 0)
            return new, total, acc

        init = (
            jnp.full((1, BQ), NEG, F32),
            jnp.zeros((1, BQ), F32),
            jnp.zeros((HD, BQ), F32),
        )
        last = (q0 + BQ - 1) // BK
        carry = step(last, init)
        peak, total, acc = lax.fori_loop(lo_ref[qb], last, step, carry)
        o_ref[:, qb * BQ : (qb + 1) * BQ] = (acc / total).astype(BF)
        lse_ref[0, :, qb * BQ : (qb + 1) * BQ] = peak + jnp.log(total)


def attn_bwd_kernel(
    lo_ref, q_ref, k_ref, v_ref, o_ref, do_ref, lse_ref, doc_ref, dq_ref, dk_ref, dv_ref, *, shift
):
    rows = q_ref.shape[1]
    dk_ref[...] = jnp.zeros_like(dk_ref)
    dv_ref[...] = jnp.zeros_like(dv_ref)
    for qb in range(rows // BQ):
        cols = slice(qb * BQ, (qb + 1) * BQ)
        qt = q_ref[:, cols]
        dot = do_ref[:, cols]
        doc = doc_ref[:, cols]
        lse = lse_ref[0, :, cols]
        delta = jnp.sum(dot.astype(F32) * o_ref[:, cols].astype(F32), axis=0, keepdims=True)
        q0 = shift + qb * BQ

        def step(b, dq, qt=qt, dot=dot, doc=doc, lse=lse, delta=delta, q0=q0):
            off = pl.multiple_of(b * BK, BK)
            kt = k_ref[:, pl.ds(off, BK)]
            vt = v_ref[:, pl.ds(off, BK)]
            s = mm(kt, qt, 0, 0) * 0.125
            s = jnp.where(attn_mask(s, off, q0, doc), s, NEG)
            p = jnp.exp(s - lse)
            dp = mm(vt, dot, 0, 0)
            ds = (p * (dp - delta)).astype(BF)
            dk_ref[:, pl.ds(off, BK)] += mm(qt, ds, 1, 1)
            dv_ref[:, pl.ds(off, BK)] += mm(dot, p.astype(BF), 1, 1)
            return dq + mm(kt, ds, 1, 0)

        last = (q0 + BQ - 1) // BK
        dq = lax.fori_loop(lo_ref[qb], last + 1, step, jnp.zeros((HD, BQ), F32))
        dq_ref[:, cols] = dq * 0.125
    dk_ref[...] = dk_ref[...] * 0.125


def head_spec(width):
    return pl.BlockSpec((HD, width), lambda h, lo: (h, 0))


def attn_forward(lo, q_t, k_t, v_t, doc, shift):
    cols, rows = q_t.shape
    window = k_t.shape[1]
    heads = cols // HD
    return pl.pallas_call(
        functools.partial(attn_fwd_kernel, shift=shift),
        out_shape=(
            jax.ShapeDtypeStruct((cols, rows), BF),
            jax.ShapeDtypeStruct((heads, 1, rows), F32),
        ),
        grid_spec=pltpu.PrefetchScalarGridSpec(
            num_scalar_prefetch=1,
            grid=(heads,),
            in_specs=[
                head_spec(rows),
                head_spec(window),
                head_spec(window),
                pl.BlockSpec((1, rows), lambda h, lo: (0, 0)),
            ],
            out_specs=[
                head_spec(rows),
                pl.BlockSpec((1, 1, rows), lambda h, lo: (h, 0, 0)),
            ],
        ),
        name="attn_fwd",
    )(lo, q_t, k_t, v_t, doc)


def attn_backward(lo, q_t, k_t, v_t, o_t, do_t, lse, doc, shift):
    cols, rows = q_t.shape
    window = k_t.shape[1]
    heads = cols // HD
    return pl.pallas_call(
        functools.partial(attn_bwd_kernel, shift=shift),
        out_shape=(
            jax.ShapeDtypeStruct((cols, rows), F32),
            jax.ShapeDtypeStruct((cols, window), F32),
            jax.ShapeDtypeStruct((cols, window), F32),
        ),
        grid_spec=pltpu.PrefetchScalarGridSpec(
            num_scalar_prefetch=1,
            grid=(heads,),
            in_specs=[
                head_spec(rows),
                head_spec(window),
                head_spec(window),
                head_spec(rows),
                head_spec(rows),
                pl.BlockSpec((1, 1, rows), lambda h, lo: (h, 0, 0)),
                pl.BlockSpec((1, rows), lambda h, lo: (0, 0)),
            ],
            out_specs=[head_spec(rows), head_spec(window), head_spec(window)],
        ),
        name="attn_bwd",
    )(lo, q_t, k_t, v_t, o_t, do_t, lse, doc)


def ffn_kernel(*refs, gated):
    if gated:
        x_ref, g_ref, gate_ref, win_ref, wout_ref = refs[:5]
        y_ref, dx_ref, dgate_ref, gin_ref, gout_ref, acc_in, acc_out = refs[5:]
    else:
        x_ref, g_ref, win_ref, wout_ref = refs[:4]
        y_ref, dx_ref, gin_ref, gout_ref, acc_in, acc_out = refs[4:]
    src, _, rows, width = x_ref.shape
    step = pl.program_id(1)

    @pl.when(step == 0)
    def _():
        acc_in[...] = jnp.zeros_like(acc_in)
        acc_out[...] = jnp.zeros_like(acc_out)

    x = x_ref[...].reshape(src * rows, width)
    g = g_ref[...].reshape(src * rows, width)
    w_gate = win_ref[0, 0]
    w_up = win_ref[0, 1]
    w_out = wout_ref[0]
    gate_pre = mm(x, w_gate, 1, 0)
    up_pre = mm(x, w_up, 1, 0)
    sig = 1.0 / (1.0 + jnp.exp(-gate_pre))
    silu = gate_pre * sig
    hidden = (silu * up_pre).astype(BF)
    y = mm(hidden, w_out, 1, 1)
    if gated:
        gf = g.astype(F32)
        gate = gate_ref[...].reshape(src * rows, 1)
        dgate_ref[...] = jnp.sum(gf * y, axis=1, keepdims=True).reshape(src, 1, rows, 1)
        dy = (gate * gf).astype(BF)
    else:
        dy = g
    y_ref[...] = y.astype(BF).reshape(src, 1, rows, width)
    dh = mm(dy, w_out, 1, 0)
    dgp = (dh * up_pre * (sig * (1.0 + gate_pre * (1.0 - sig)))).astype(BF)
    dup = (dh * silu).astype(BF)
    dx = mm(dgp, w_gate, 1, 1) + mm(dup, w_up, 1, 1)
    dx_ref[...] = dx.astype(BF).reshape(src, 1, rows, width)
    acc_in[0] += mm(x, dgp, 0, 0)
    acc_in[1] += mm(x, dup, 0, 0)
    acc_out[...] += mm(dy, hidden, 0, 0)

    @pl.when(step == pl.num_programs(1) - 1)
    def _():
        gin_ref[0] = acc_in[...].astype(BF)
        gout_ref[0] = acc_out[...].astype(BF)


def ffn(x, g, gate, w_in, w_out, block):
    sources, experts, rows, width = x.shape
    units = w_out.shape[2]
    gated = gate is not None
    block = math.gcd(sources, block)
    big = pl.BlockSpec((block, 1, rows, width), lambda e, s: (s, e, 0, 0))
    thin = pl.BlockSpec((block, 1, rows, 1), lambda e, s: (s, e, 0, 0))
    w_in_spec = pl.BlockSpec((1, 2, width, units), lambda e, s: (e, 0, 0, 0))
    w_out_spec = pl.BlockSpec((1, width, units), lambda e, s: (e, 0, 0))
    wide = jax.ShapeDtypeStruct(x.shape, BF)
    outs = [wide, wide]
    out_specs = [big, big]
    if gated:
        outs.append(jax.ShapeDtypeStruct(gate.shape, F32))
        out_specs.append(thin)
    outs += [
        jax.ShapeDtypeStruct((experts, 2, width, units), BF),
        jax.ShapeDtypeStruct((experts, width, units), BF),
    ]
    out_specs += [w_in_spec, w_out_spec]
    return pl.pallas_call(
        functools.partial(ffn_kernel, gated=gated),
        out_shape=outs,
        grid=(experts, sources // block),
        in_specs=[big, big] + ([thin] if gated else []) + [w_in_spec, w_out_spec],
        out_specs=out_specs,
        scratch_shapes=[
            pltpu.VMEM((2, width, units), F32),
            pltpu.VMEM((width, units), F32),
        ],
        compiler_params=pltpu.CompilerParams(
            dimension_semantics=("arbitrary", "arbitrary"), vmem_limit_bytes=56 * 1024 * 1024
        ),
        name="ffn_experts" if gated else "ffn_shared",
    )(*([x, g] + ([gate] if gated else []) + [w_in, w_out]))


def after(value, *first):
    return lax.optimization_barrier((value,) + first)[0]


def pair_slots(pair_route, order, experts, capacity):
    count = order.shape[0]
    flat = pair_route.reshape(count)
    number = jnp.arange(count, dtype=jnp.int32)
    ids = jnp.arange(experts, dtype=jnp.int32)
    owner = (flat[:, None] == ids[None, :]).astype(BF)
    ranked = jnp.dot(
        (order[:, None] == number[None, :]).astype(BF), owner, preferred_element_type=F32
    ).astype(BF)
    earlier = jnp.dot(
        (number[None, :] < number[:, None]).astype(BF), ranked, preferred_element_type=F32
    )
    ranked_slot = (jnp.minimum(earlier, float(capacity)) * ranked).astype(BF)
    slot = jnp.sum(
        jnp.dot(
            (order[None, :] == number[:, None]).astype(BF),
            ranked_slot,
            preferred_element_type=F32,
        ),
        axis=1,
    ).astype(jnp.int32)
    place = jnp.where(slot < capacity, flat * capacity + slot, experts * capacity)
    return place.reshape(pair_route.shape)


def own_sum(parts, axis):
    devices = lax.axis_size(DC)
    shape = parts.shape
    cut = shape[:axis] + (devices, shape[axis] // devices) + shape[axis + 1 :]
    swapped = lax.all_to_all(
        parts.astype(BF).reshape(cut), DC, split_axis=axis, concat_axis=axis, tiled=True
    )
    return jnp.sum(swapped.astype(F32), axis=axis)


def half_turn(values_t, cos_t, sin_t):
    cols, rows = values_t.shape
    split = values_t.reshape(cols // HD, 2, HALF, rows)
    a, b = split[:, 0], split[:, 1]
    return jnp.stack([a * cos_t - b * sin_t, b * cos_t + a * sin_t], axis=1).reshape(cols, rows)


def shards(
    tokens,
    segment_ids,
    routes,
    pair_order,
    gain_attn,
    qkv_weight,
    out_weight,
    gain_ffn,
    router_weight,
    shared_in,
    shared_out,
    expert_in,
    expert_out,
    out_grad,
):
    rows, width = tokens.shape[1], tokens.shape[2]
    ctx_count = lax.axis_size("ctx")
    ctx_at = lax.axis_index("ctx")
    inputs = tokens[0].astype(F32)
    grad_low = out_grad[0]
    grad_layer = grad_low.astype(F32)
    seg_all = segment_ids[0]
    my_routes = routes[0]

    heads_cols = qkv_weight.shape[2]
    qkv_cols = 3 * heads_cols
    experts = router_weight.shape[1]
    thin = jnp.concatenate(
        [
            qkv_weight.transpose(1, 0, 2).reshape(-1, qkv_cols),
            out_weight,
            router_weight,
            gain_attn[:, None],
            gain_ffn[:, None],
        ],
        axis=1,
    )
    thin_full = lax.all_gather(thin, DC, axis=0, tiled=True)
    qkv_full = thin_full[:, :qkv_cols]
    out_full = thin_full[:, qkv_cols : qkv_cols + heads_cols]
    router_full = thin_full[:, qkv_cols + heads_cols : qkv_cols + heads_cols + experts]
    attn_gain = thin_full[:, -2].astype(F32)
    ffn_gain = thin_full[:, -1].astype(F32)

    local_experts = expert_in.shape[0]
    spread = local_experts % ctx_count == 0
    expert_axes = DC if spread else ("dp",)
    owners = lax.axis_size(expert_axes)
    own = experts // owners
    capacity = 10 * rows // (4 * experts)
    slots = experts * capacity

    def swap(values):
        return lax.all_to_all(values, expert_axes, split_axis=0, concat_axis=0, tiled=True)

    place = pair_slots(my_routes, pair_order[0, 0], experts, capacity)
    slot_ids = jnp.arange(slots, dtype=jnp.int32)
    hit0 = place[None, :, 0] == slot_ids[:, None]
    hit1 = place[None, :, 1] == slot_ids[:, None]
    to_slot = (hit0 | hit1).astype(BF)
    slot_g = jnp.dot(to_slot, grad_low, preferred_element_type=F32).astype(BF)

    inv1 = lax.rsqrt(jnp.mean(inputs * inputs, axis=-1, keepdims=True) + EPSILON)
    n1 = inputs * inv1
    normed = (n1 * attn_gain).astype(BF)
    row_start = ctx_at * rows
    query_pos = row_start + jnp.arange(rows, dtype=jnp.int32)
    inverse = 1.0 / 10000.0 ** (jnp.arange(HALF, dtype=F32) * (2.0 / HD))
    angles = inverse[:, None] * query_pos.astype(F32)[None, :]
    cos_t, sin_t = jnp.cos(angles), jnp.sin(angles)
    raw_t = jnp.einsum("dc,ld->cl", qkv_full, normed, preferred_element_type=F32)
    q_t = half_turn(raw_t[:heads_cols], cos_t, sin_t).astype(BF)
    k_t = half_turn(raw_t[heads_cols : 2 * heads_cols], cos_t, sin_t).astype(BF)
    v_t = raw_t[2 * heads_cols :].astype(BF)
    kv_t = jnp.concatenate([k_t, v_t], axis=0)
    before = min(ctx_count - 1, -(-(LONGEST - 1) // rows))
    shift = before * rows
    pieces = [kv_t]
    for hop in range(1, before + 1):
        links = [(i, i + hop) for i in range(ctx_count - hop)]
        pieces.insert(0, lax.ppermute(kv_t, "ctx", links))
    kv_win = jnp.concatenate(pieces, axis=1)
    k_win, v_win = kv_win[:heads_cols], kv_win[heads_cols:]

    expert_in, expert_out, slot_g, _ = lax.optimization_barrier(
        (expert_in, expert_out, slot_g, kv_win)
    )
    if spread:
        ein = lax.all_to_all(expert_in, "ctx", split_axis=0, concat_axis=2, tiled=True)
        eout = lax.all_to_all(expert_out, "ctx", split_axis=0, concat_axis=1, tiled=True)
    else:
        ein = lax.all_gather(expert_in, "ctx", axis=2, tiled=True)
        eout = lax.all_gather(expert_out, "ctx", axis=1, tiled=True)
    got_g = swap(slot_g.reshape(owners, own, capacity, width))

    starts = jnp.sum(
        seg_all[:, None] < jnp.arange(DOCS, dtype=jnp.int32)[None, :], axis=0, dtype=jnp.int32
    )
    query_seg = lax.dynamic_slice_in_dim(seg_all, row_start, rows)
    doc = jnp.sum(
        jnp.where(
            query_seg[:, None] == jnp.arange(DOCS, dtype=jnp.int32)[None, :], starts[None, :], 0
        ),
        axis=1,
    ) - (row_start - shift)
    lo = jnp.maximum(doc[::BQ], 0) // BK
    doc = doc[None, :]
    att_t, lse = attn_forward(lo, q_t, k_win, v_win, doc, shift)
    branch_part = jnp.einsum("cl,dc->ld", att_t, out_full, preferred_element_type=F32)
    branch = lax.psum(branch_part.astype(BF), "tensor")
    branch, ein, eout, got_g = lax.optimization_barrier((branch, ein, eout, got_g))
    branch = branch.astype(F32)
    resid = inputs + branch

    inv2 = lax.rsqrt(jnp.mean(resid * resid, axis=-1, keepdims=True) + EPSILON)
    n2 = resid * inv2
    normed2 = (n2 * ffn_gain).astype(BF)
    slot_x = jnp.dot(to_slot, normed2, preferred_element_type=F32).astype(BF)
    got_x = swap(slot_x.reshape(owners, own, capacity, width))
    logits = jnp.dot(normed2, router_full, preferred_element_type=F32)
    picked = my_routes[:, :, None] == jnp.arange(experts, dtype=jnp.int32)[None, None, :]
    chosen = jnp.sum(jnp.where(picked, logits[:, None, :], 0.0), axis=2)
    chosen_exp = jnp.exp(chosen - jnp.max(chosen, axis=1, keepdims=True))
    gates = chosen_exp / jnp.sum(chosen_exp, axis=1, keepdims=True)
    slot_gate = jnp.sum(
        jnp.where(hit0, gates[None, :, 0], 0.0) + jnp.where(hit1, gates[None, :, 1], 0.0), axis=1
    )
    got_gate = swap(slot_gate.reshape(owners, own * capacity))

    shared_w = after(jnp.concatenate([shared_in, shared_out[None]], axis=0), got_x)
    shared_full = lax.all_gather(shared_w, DC, axis=1, tiled=True)
    y, dx, dgate, g_ein, g_eout = ffn(
        got_x, got_g, got_gate.reshape(owners, own, capacity, 1), ein, eout, 4
    )
    back_dx = swap(dx).reshape(slots, width)
    back_dgate = swap(dgate.reshape(owners, own * capacity)).reshape(slots)

    parts = 4
    shared_shape = (parts, 1, rows // parts, width)
    sh_y, sh_dx, sh_gin, sh_gout = ffn(
        normed2.reshape(shared_shape),
        grad_low.reshape(shared_shape),
        None,
        shared_full[None, :2],
        shared_full[None, 2],
        2,
    )
    back_dx, sh_dx = lax.optimization_barrier((back_dx, sh_dx))

    at0 = place[:, 0, None] == slot_ids[None, :]
    at1 = place[:, 1, None] == slot_ids[None, :]
    dn2_part = jnp.dot((at0 | at1).astype(BF), back_dx, preferred_element_type=F32)
    dgates = jnp.stack(
        [
            jnp.sum(jnp.where(at0, back_dgate[None, :], 0.0), axis=1),
            jnp.sum(jnp.where(at1, back_dgate[None, :], 0.0), axis=1),
        ],
        axis=1,
    )
    dchosen = gates * (dgates - jnp.sum(gates * dgates, axis=1, keepdims=True))
    dlogits = jnp.sum(jnp.where(picked, dchosen[:, :, None], 0.0), axis=1).astype(BF)
    dn2_part = (
        dn2_part
        + sh_dx.reshape(rows, width).astype(F32)
        + jnp.einsum("le,de->ld", dlogits, router_full, preferred_element_type=F32)
    )
    dn2_low = dn2_part.astype(BF)
    back_y = swap(after(y, dn2_low)).reshape(slots, width)
    dn2 = lax.psum(dn2_low, "tensor")
    dn2, back_y = lax.optimization_barrier((dn2, back_y))
    g_eout, sh_grad, _ = lax.optimization_barrier(
        (g_eout, jnp.concatenate([sh_gin[0], sh_gout], axis=0), dn2)
    )
    if spread:
        grad_eout = lax.all_to_all(g_eout, "ctx", split_axis=1, concat_axis=0, tiled=True)
    else:
        grad_eout = lax.psum_scatter(g_eout, "ctx", scatter_dimension=1, tiled=True)
    total_shared = own_sum(sh_grad, 1)
    dn2 = dn2.astype(F32)
    router_part = jnp.einsum("ld,le->de", normed2, dlogits, preferred_element_type=F32)
    gain2_part = jnp.sum(dn2_part * n2, axis=0)

    scaled2 = ffn_gain * dn2
    dresid = grad_layer + inv2 * (scaled2 - n2 * jnp.mean(scaled2 * n2, axis=-1, keepdims=True))
    dbranch = dresid.astype(BF)
    datt_t = jnp.einsum("dc,ld->cl", out_full, dbranch, preferred_element_type=F32).astype(BF)

    weight0 = jnp.where(at0, gates[:, 0, None], 0.0)
    weight1 = jnp.where(at1, gates[:, 1, None], 0.0)
    ffn_part = jnp.dot(
        (weight0 + weight1).astype(BF), back_y, preferred_element_type=F32
    ) + sh_y.reshape(rows, width).astype(F32)
    ffn_low, datt_t = lax.optimization_barrier((ffn_part.astype(BF), datt_t))
    ffn_total = lax.psum(ffn_low, "tensor")

    dq_t, dk_win, dv_win = attn_backward(
        lo, q_t, k_win, v_win, att_t, datt_t, lse, doc, shift
    )
    dkv_win = jnp.concatenate([dk_win, dv_win], axis=0)
    dkv = dkv_win[:, shift:]
    for hop in range(1, before + 1):
        links = [(i + hop, i) for i in range(ctx_count - hop)]
        piece = dkv_win[:, shift - hop * rows : shift - (hop - 1) * rows]
        dkv = dkv + lax.ppermute(piece.astype(BF), "ctx", links).astype(F32)
    dq_raw = half_turn(dq_t, cos_t, -sin_t)
    dk_raw = half_turn(dkv[:heads_cols], cos_t, -sin_t)
    draw_t = jnp.concatenate([dq_raw, dk_raw, dkv[heads_cols:]], axis=0).astype(BF)
    dn1_part = jnp.einsum("cl,dc->ld", draw_t, qkv_full, preferred_element_type=F32)
    dn1_low, ffn_total, g_ein, grad_eout, total_shared = lax.optimization_barrier(
        (dn1_part.astype(BF), ffn_total, g_ein, grad_eout, total_shared)
    )
    layer_out = (resid + ffn_total.astype(F32)).astype(BF)
    dn1 = lax.psum(dn1_low, "tensor")
    gain1_part = jnp.sum(dn1_part * n1, axis=0)
    grad_qkv = jnp.einsum("ld,cl->dc", normed, draw_t, preferred_element_type=F32)
    grad_outw = jnp.einsum("ld,cl->dc", dbranch, att_t, preferred_element_type=F32)
    small = jnp.concatenate([router_part, gain1_part[:, None], gain2_part[:, None]], axis=1)
    tail = own_sum(
        jnp.concatenate([grad_qkv, grad_outw, small], axis=1), 0
    )
    total_qkv = tail[:, : 3 * heads_cols].reshape(-1, 3, heads_cols).transpose(1, 0, 2)
    total_outw = tail[:, 3 * heads_cols : 4 * heads_cols]
    small = lax.psum(tail[:, 4 * heads_cols :], "tensor")
    g_ein = after(g_ein, tail)
    if spread:
        grad_ein = lax.all_to_all(g_ein, "ctx", split_axis=2, concat_axis=0, tiled=True)
    else:
        grad_ein = lax.psum_scatter(g_ein, "ctx", scatter_dimension=2, tiled=True)
    dn1 = after(dn1, small, grad_ein).astype(F32)
    scaled1 = attn_gain * dn1
    grad_tokens = dresid + inv1 * (
        scaled1 - n1 * jnp.mean(scaled1 * n1, axis=-1, keepdims=True)
    )
    return (
        layer_out[None],
        grad_tokens[None],
        small[:, experts],
        total_qkv,
        total_outw,
        small[:, experts + 1],
        small[:, :experts],
        total_shared[:2],
        total_shared[2],
        grad_ein.astype(F32),
        grad_eout.astype(F32),
    )


def solution(mesh):
    return jax.shard_map(
        shards,
        mesh=mesh,
        in_specs=(
            P("dp", "ctx", None),
            P("dp", None),
            P("dp", "ctx", None),
            P("dp", "ctx", None),
            P(DC),
            P(None, DC, "tensor"),
            P(DC, "tensor"),
            P(DC),
            P(DC, None),
            P(None, DC, "tensor"),
            P(DC, "tensor"),
            P("dp", None, "ctx", "tensor"),
            P("dp", "ctx", "tensor"),
            P("dp", "ctx", None),
        ),
        out_specs=(
            P("dp", "ctx", None),
            P("dp", "ctx", None),
            P(DC),
            P(None, DC, "tensor"),
            P(DC, "tensor"),
            P(DC),
            P(DC, None),
            P(None, DC, "tensor"),
            P(DC, "tensor"),
            P("dp", None, "ctx", "tensor"),
            P("dp", "ctx", "tensor"),
        ),
        check_vma=False,
    )
```

```python
import functools
import math

import jax
import jax.numpy as jnp
from jax import lax
from jax.experimental import pallas as pl
from jax.experimental.pallas import tpu as pltpu
from jax.sharding import PartitionSpec as P

HD = 64
HALF = HD // 2
EPSILON = 1e-06
LONGEST = 2000
DOCS = 5
BQ = 256
BK = 256
BF = jnp.bfloat16
F32 = jnp.float32
NEG = -1e30
DC = ("dp", "ctx")


def mm(a, b, ca, cb):
    return lax.dot_general(a, b, (((ca,), (cb,)), ((), ())), preferred_element_type=F32)


def attn_mask(scores_t, key_start, query_start, doc_row):
    rows, cols = scores_t.shape
    kpos = key_start + lax.broadcasted_iota(jnp.int32, (rows, cols), 0)
    qpos = query_start + lax.broadcasted_iota(jnp.int32, (rows, cols), 1)
    return (kpos <= qpos) & (kpos >= doc_row)


def attn_fwd_kernel(lo_ref, q_ref, k_ref, v_ref, doc_ref, o_ref, lse_ref, *, shift):
    rows = q_ref.shape[1]
    for qb in range(rows // BQ):
        qt = q_ref[:, qb * BQ : (qb + 1) * BQ]
        doc = doc_ref[:, qb * BQ : (qb + 1) * BQ]
        q0 = shift + qb * BQ

        def step(b, carry, qt=qt, doc=doc, q0=q0):
            peak, total, acc = carry
            off = pl.multiple_of(b * BK, BK)
            kt = k_ref[:, pl.ds(off, BK)]
            vt = v_ref[:, pl.ds(off, BK)]
            s = mm(kt, qt, 0, 0) * 0.125
            s = jnp.where(attn_mask(s, off, q0, doc), s, NEG)
            new = jnp.maximum(peak, jnp.max(s, axis=0, keepdims=True))
            p = jnp.exp(s - new)
            fix = jnp.exp(peak - new)
            total = total * fix + jnp.sum(p, axis=0, keepdims=True)
            acc = acc * fix + mm(vt, p.astype(BF), 1, 0)
            return new, total, acc

        init = (
            jnp.full((1, BQ), NEG, F32),
            jnp.zeros((1, BQ), F32),
            jnp.zeros((HD, BQ), F32),
        )
        last = (q0 + BQ - 1) // BK
        carry = step(last, init)
        peak, total, acc = lax.fori_loop(lo_ref[qb], last, step, carry)
        o_ref[:, qb * BQ : (qb + 1) * BQ] = (acc / total).astype(BF)
        lse_ref[0, :, qb * BQ : (qb + 1) * BQ] = peak + jnp.log(total)


def attn_bwd_kernel(
    lo_ref, q_ref, k_ref, v_ref, o_ref, do_ref, lse_ref, doc_ref, dq_ref, dk_ref, dv_ref, *, shift
):
    rows = q_ref.shape[1]
    dk_ref[...] = jnp.zeros_like(dk_ref)
    dv_ref[...] = jnp.zeros_like(dv_ref)
    for qb in range(rows // BQ):
        cols = slice(qb * BQ, (qb + 1) * BQ)
        qt = q_ref[:, cols]
        dot = do_ref[:, cols]
        doc = doc_ref[:, cols]
        lse = lse_ref[0, :, cols]
        delta = jnp.sum(dot.astype(F32) * o_ref[:, cols].astype(F32), axis=0, keepdims=True)
        q0 = shift + qb * BQ

        def step(b, dq, qt=qt, dot=dot, doc=doc, lse=lse, delta=delta, q0=q0):
            off = pl.multiple_of(b * BK, BK)
            kt = k_ref[:, pl.ds(off, BK)]
            vt = v_ref[:, pl.ds(off, BK)]
            s = mm(kt, qt, 0, 0) * 0.125
            s = jnp.where(attn_mask(s, off, q0, doc), s, NEG)
            p = jnp.exp(s - lse)
            dp = mm(vt, dot, 0, 0)
            ds = (p * (dp - delta)).astype(BF)
            dk_ref[:, pl.ds(off, BK)] += mm(qt, ds, 1, 1)
            dv_ref[:, pl.ds(off, BK)] += mm(dot, p.astype(BF), 1, 1)
            return dq + mm(kt, ds, 1, 0)

        last = (q0 + BQ - 1) // BK
        dq = lax.fori_loop(lo_ref[qb], last + 1, step, jnp.zeros((HD, BQ), F32))
        dq_ref[:, cols] = dq * 0.125
    dk_ref[...] = dk_ref[...] * 0.125


def head_spec(width):
    return pl.BlockSpec((HD, width), lambda h, lo: (h, 0))


def attn_forward(lo, q_t, k_t, v_t, doc, shift):
    cols, rows = q_t.shape
    window = k_t.shape[1]
    heads = cols // HD
    return pl.pallas_call(
        functools.partial(attn_fwd_kernel, shift=shift),
        out_shape=(
            jax.ShapeDtypeStruct((cols, rows), BF),
            jax.ShapeDtypeStruct((heads, 1, rows), F32),
        ),
        grid_spec=pltpu.PrefetchScalarGridSpec(
            num_scalar_prefetch=1,
            grid=(heads,),
            in_specs=[
                head_spec(rows),
                head_spec(window),
                head_spec(window),
                pl.BlockSpec((1, rows), lambda h, lo: (0, 0)),
            ],
            out_specs=[
                head_spec(rows),
                pl.BlockSpec((1, 1, rows), lambda h, lo: (h, 0, 0)),
            ],
        ),
        name="attn_fwd",
    )(lo, q_t, k_t, v_t, doc)


def attn_backward(lo, q_t, k_t, v_t, o_t, do_t, lse, doc, shift):
    cols, rows = q_t.shape
    window = k_t.shape[1]
    heads = cols // HD
    return pl.pallas_call(
        functools.partial(attn_bwd_kernel, shift=shift),
        out_shape=(
            jax.ShapeDtypeStruct((cols, rows), F32),
            jax.ShapeDtypeStruct((cols, window), F32),
            jax.ShapeDtypeStruct((cols, window), F32),
        ),
        grid_spec=pltpu.PrefetchScalarGridSpec(
            num_scalar_prefetch=1,
            grid=(heads,),
            in_specs=[
                head_spec(rows),
                head_spec(window),
                head_spec(window),
                head_spec(rows),
                head_spec(rows),
                pl.BlockSpec((1, 1, rows), lambda h, lo: (h, 0, 0)),
                pl.BlockSpec((1, rows), lambda h, lo: (0, 0)),
            ],
            out_specs=[head_spec(rows), head_spec(window), head_spec(window)],
        ),
        name="attn_bwd",
    )(lo, q_t, k_t, v_t, o_t, do_t, lse, doc)


def ffn_kernel(*refs, gated):
    if gated:
        x_ref, g_ref, gate_ref, win_ref, wout_ref = refs[:5]
        y_ref, dx_ref, dgate_ref, gin_ref, gout_ref, acc_in, acc_out = refs[5:]
    else:
        x_ref, g_ref, win_ref, wout_ref = refs[:4]
        y_ref, dx_ref, gin_ref, gout_ref, acc_in, acc_out = refs[4:]
    src, _, rows, width = x_ref.shape
    step = pl.program_id(1)

    @pl.when(step == 0)
    def _():
        acc_in[...] = jnp.zeros_like(acc_in)
        acc_out[...] = jnp.zeros_like(acc_out)

    x = x_ref[...].reshape(src * rows, width)
    g = g_ref[...].reshape(src * rows, width)
    w_gate = win_ref[0, 0]
    w_up = win_ref[0, 1]
    w_out = wout_ref[0]
    gate_pre = mm(x, w_gate, 1, 0)
    up_pre = mm(x, w_up, 1, 0)
    sig = 1.0 / (1.0 + jnp.exp(-gate_pre))
    silu = gate_pre * sig
    hidden = (silu * up_pre).astype(BF)
    y = mm(hidden, w_out, 1, 1)
    if gated:
        gf = g.astype(F32)
        gate = gate_ref[...].reshape(src * rows, 1)
        dgate_ref[...] = jnp.sum(gf * y, axis=1, keepdims=True).reshape(src, 1, rows, 1)
        dy = (gate * gf).astype(BF)
    else:
        dy = g
    y_ref[...] = y.astype(BF).reshape(src, 1, rows, width)
    dh = mm(dy, w_out, 1, 0)
    dgp = (dh * up_pre * (sig * (1.0 + gate_pre * (1.0 - sig)))).astype(BF)
    dup = (dh * silu).astype(BF)
    dx = mm(dgp, w_gate, 1, 1) + mm(dup, w_up, 1, 1)
    dx_ref[...] = dx.astype(BF).reshape(src, 1, rows, width)
    acc_in[0] += mm(x, dgp, 0, 0)
    acc_in[1] += mm(x, dup, 0, 0)
    acc_out[...] += mm(dy, hidden, 0, 0)

    @pl.when(step == pl.num_programs(1) - 1)
    def _():
        gin_ref[0] = acc_in[...].astype(BF)
        gout_ref[0] = acc_out[...].astype(BF)


def ffn(x, g, gate, w_in, w_out, block):
    sources, experts, rows, width = x.shape
    units = w_out.shape[2]
    gated = gate is not None
    block = math.gcd(sources, block)
    big = pl.BlockSpec((block, 1, rows, width), lambda e, s: (s, e, 0, 0))
    thin = pl.BlockSpec((block, 1, rows, 1), lambda e, s: (s, e, 0, 0))
    w_in_spec = pl.BlockSpec((1, 2, width, units), lambda e, s: (e, 0, 0, 0))
    w_out_spec = pl.BlockSpec((1, width, units), lambda e, s: (e, 0, 0))
    wide = jax.ShapeDtypeStruct(x.shape, BF)
    outs = [wide, wide]
    out_specs = [big, big]
    if gated:
        outs.append(jax.ShapeDtypeStruct(gate.shape, F32))
        out_specs.append(thin)
    outs += [
        jax.ShapeDtypeStruct((experts, 2, width, units), BF),
        jax.ShapeDtypeStruct((experts, width, units), BF),
    ]
    out_specs += [w_in_spec, w_out_spec]
    return pl.pallas_call(
        functools.partial(ffn_kernel, gated=gated),
        out_shape=outs,
        grid=(experts, sources // block),
        in_specs=[big, big] + ([thin] if gated else []) + [w_in_spec, w_out_spec],
        out_specs=out_specs,
        scratch_shapes=[
            pltpu.VMEM((2, width, units), F32),
            pltpu.VMEM((width, units), F32),
        ],
        compiler_params=pltpu.CompilerParams(
            dimension_semantics=("arbitrary", "arbitrary"), vmem_limit_bytes=56 * 1024 * 1024
        ),
        name="ffn_experts" if gated else "ffn_shared",
    )(*([x, g] + ([gate] if gated else []) + [w_in, w_out]))


def after(value, *first):
    return lax.optimization_barrier((value,) + first)[0]


def pair_slots(pair_route, order, experts, capacity):
    count = order.shape[0]
    flat = pair_route.reshape(count)
    number = jnp.arange(count, dtype=jnp.int32)
    ids = jnp.arange(experts, dtype=jnp.int32)
    owner = (flat[:, None] == ids[None, :]).astype(BF)
    ranked = jnp.dot(
        (order[:, None] == number[None, :]).astype(BF), owner, preferred_element_type=F32
    ).astype(BF)
    earlier = jnp.dot(
        (number[None, :] < number[:, None]).astype(BF), ranked, preferred_element_type=F32
    )
    ranked_slot = (jnp.minimum(earlier, float(capacity)) * ranked).astype(BF)
    slot = jnp.sum(
        jnp.dot(
            (order[None, :] == number[:, None]).astype(BF),
            ranked_slot,
            preferred_element_type=F32,
        ),
        axis=1,
    ).astype(jnp.int32)
    place = jnp.where(slot < capacity, flat * capacity + slot, experts * capacity)
    return place.reshape(pair_route.shape)


def own_sum(parts, axis):
    devices = lax.axis_size(DC)
    shape = parts.shape
    cut = shape[:axis] + (devices, shape[axis] // devices) + shape[axis + 1 :]
    swapped = lax.all_to_all(
        parts.astype(BF).reshape(cut), DC, split_axis=axis, concat_axis=axis, tiled=True
    )
    return jnp.sum(swapped.astype(F32), axis=axis)


def half_turn(values_t, cos_t, sin_t):
    cols, rows = values_t.shape
    split = values_t.reshape(cols // HD, 2, HALF, rows)
    a, b = split[:, 0], split[:, 1]
    return jnp.stack([a * cos_t - b * sin_t, b * cos_t + a * sin_t], axis=1).reshape(cols, rows)


def shards(
    tokens,
    segment_ids,
    routes,
    pair_order,
    gain_attn,
    qkv_weight,
    out_weight,
    gain_ffn,
    router_weight,
    shared_in,
    shared_out,
    expert_in,
    expert_out,
    out_grad,
):
    rows, width = tokens.shape[1], tokens.shape[2]
    ctx_count = lax.axis_size("ctx")
    ctx_at = lax.axis_index("ctx")
    inputs = tokens[0].astype(F32)
    grad_low = out_grad[0]
    grad_layer = grad_low.astype(F32)
    seg_all = segment_ids[0]
    my_routes = routes[0]

    heads_cols = qkv_weight.shape[2]
    qkv_cols = 3 * heads_cols
    experts = router_weight.shape[1]
    thin = jnp.concatenate(
        [
            qkv_weight.transpose(1, 0, 2).reshape(-1, qkv_cols),
            out_weight,
            router_weight,
            gain_attn[:, None],
            gain_ffn[:, None],
        ],
        axis=1,
    )
    thin_full = lax.all_gather(thin, DC, axis=0, tiled=True)
    qkv_full = thin_full[:, :qkv_cols]
    out_full = thin_full[:, qkv_cols : qkv_cols + heads_cols]
    out_tensor = lax.all_gather(out_full, "tensor", axis=0)
    router_full = thin_full[:, qkv_cols + heads_cols : qkv_cols + heads_cols + experts]
    attn_gain = thin_full[:, -2].astype(F32)
    ffn_gain = thin_full[:, -1].astype(F32)

    local_experts = expert_in.shape[0]
    spread = local_experts % ctx_count == 0
    expert_axes = DC if spread else ("dp",)
    owners = lax.axis_size(expert_axes)
    own = experts // owners
    capacity = 10 * rows // (4 * experts)
    slots = experts * capacity

    def swap(values):
        return lax.all_to_all(values, expert_axes, split_axis=0, concat_axis=0, tiled=True)

    place = pair_slots(my_routes, pair_order[0, 0], experts, capacity)
    slot_ids = jnp.arange(slots, dtype=jnp.int32)
    owner_at = lax.axis_index(expert_axes)
    all_place = lax.all_gather(place.T, expert_axes, axis=0)
    hit0 = place[None, :, 0] == slot_ids[:, None]
    hit1 = place[None, :, 1] == slot_ids[:, None]
    to_slot = (hit0 | hit1).astype(BF)
    slot_g = jnp.dot(to_slot, grad_low, preferred_element_type=F32).astype(BF)

    inv1 = lax.rsqrt(jnp.mean(inputs * inputs, axis=-1, keepdims=True) + EPSILON)
    n1 = inputs * inv1
    normed = (n1 * attn_gain).astype(BF)
    row_start = ctx_at * rows
    query_pos = row_start + jnp.arange(rows, dtype=jnp.int32)
    inverse = 1.0 / 10000.0 ** (jnp.arange(HALF, dtype=F32) * (2.0 / HD))
    angles = inverse[:, None] * query_pos.astype(F32)[None, :]
    cos_t, sin_t = jnp.cos(angles), jnp.sin(angles)
    raw_t = jnp.einsum("dc,ld->cl", qkv_full, normed, preferred_element_type=F32)
    q_t = half_turn(raw_t[:heads_cols], cos_t, sin_t).astype(BF)
    k_t = half_turn(raw_t[heads_cols : 2 * heads_cols], cos_t, sin_t).astype(BF)
    v_t = raw_t[2 * heads_cols :].astype(BF)
    if spread:
        eout = lax.all_to_all(expert_out, "ctx", split_axis=0, concat_axis=1, tiled=True)
    else:
        eout = lax.all_gather(expert_out, "ctx", axis=1, tiled=True)
    kv_t = after(jnp.concatenate([k_t, v_t], axis=0), eout, all_place)
    before = min(ctx_count - 1, -(-(LONGEST - 1) // rows))
    shift = before * rows
    pieces = [kv_t]
    for hop in range(1, before + 1):
        links = [(i, i + hop) for i in range(ctx_count - hop)]
        pieces.insert(0, lax.ppermute(kv_t, "ctx", links))
    kv_win = jnp.concatenate(pieces, axis=1)
    k_win, v_win = kv_win[:heads_cols], kv_win[heads_cols:]

    expert_in = after(expert_in, kv_win)
    if spread:
        ein = lax.all_to_all(expert_in, "ctx", split_axis=0, concat_axis=2, tiled=True)
    else:
        ein = lax.all_gather(expert_in, "ctx", axis=2, tiled=True)

    starts = jnp.sum(
        seg_all[:, None] < jnp.arange(DOCS, dtype=jnp.int32)[None, :], axis=0, dtype=jnp.int32
    )
    query_seg = lax.dynamic_slice_in_dim(seg_all, row_start, rows)
    doc = jnp.sum(
        jnp.where(
            query_seg[:, None] == jnp.arange(DOCS, dtype=jnp.int32)[None, :], starts[None, :], 0
        ),
        axis=1,
    ) - (row_start - shift)
    lo = jnp.maximum(doc[::BQ], 0) // BK
    doc = doc[None, :]
    att_t, lse = attn_forward(lo, q_t, k_win, v_win, doc, shift)
    tensor_count = lax.axis_size("tensor")
    tensor_at = lax.axis_index("tensor")
    att_parts, out_parts = [att_t], [out_full]
    for hop in range(1, tensor_count):
        links = [(i, (i + hop) % tensor_count) for i in range(tensor_count)]
        att_parts.append(lax.ppermute(att_t, "tensor", links))
        out_parts.append(
            lax.dynamic_index_in_dim(
                out_tensor, (tensor_at - hop) % tensor_count, 0, keepdims=False
            )
        )
    got_g = swap(after(slot_g, ein, att_t).reshape(owners, own, capacity, width))
    branch = jnp.einsum(
        "cl,dc->ld",
        jnp.concatenate(att_parts, axis=0),
        jnp.concatenate(out_parts, axis=1),
        preferred_element_type=F32,
    )
    resid = inputs + branch

    inv2 = lax.rsqrt(jnp.mean(resid * resid, axis=-1, keepdims=True) + EPSILON)
    n2 = resid * inv2
    normed2 = (n2 * ffn_gain).astype(BF)
    normed2, ein, got_g = lax.optimization_barrier((normed2, ein, got_g))
    slot_x = jnp.dot(to_slot, normed2, preferred_element_type=F32).astype(BF)
    got_x = swap(slot_x.reshape(owners, own, capacity, width))
    logits = jnp.dot(normed2, router_full, preferred_element_type=F32)
    picked = my_routes[:, :, None] == jnp.arange(experts, dtype=jnp.int32)[None, None, :]
    chosen = jnp.sum(jnp.where(picked, logits[:, None, :], 0.0), axis=2)
    chosen_exp = jnp.exp(chosen - jnp.max(chosen, axis=1, keepdims=True))
    gates = chosen_exp / jnp.sum(chosen_exp, axis=1, keepdims=True)
    all_gates = lax.all_gather(gates.T, expert_axes, axis=0)
    my_slots = owner_at * own * capacity + jnp.arange(own * capacity, dtype=jnp.int32)
    got_gate = jnp.sum(
        jnp.where(
            all_place[:, :, None, :] == my_slots[None, None, :, None],
            all_gates[:, :, None, :],
            0.0,
        ),
        axis=(1, 3),
    )

    shared_w = after(jnp.concatenate([shared_in, shared_out[None]], axis=0), got_x)
    shared_full = lax.all_gather(shared_w, DC, axis=1, tiled=True)
    y, dx, dgate, g_ein, g_eout = ffn(
        got_x, got_g, got_gate.reshape(owners, own, capacity, 1), ein, eout, 4
    )
    back_dx = swap(dx).reshape(slots, width)
    all_dgate = lax.all_gather(dgate.reshape(owners, own * capacity), expert_axes, axis=0)
    back_dgate = lax.dynamic_index_in_dim(all_dgate, owner_at, 1, keepdims=False).reshape(slots)

    parts = 4
    shared_shape = (parts, 1, rows // parts, width)
    sh_y, sh_dx, sh_gin, sh_gout = ffn(
        normed2.reshape(shared_shape),
        grad_low.reshape(shared_shape),
        None,
        shared_full[None, :2],
        shared_full[None, 2],
        2,
    )
    back_dx, sh_dx = lax.optimization_barrier((back_dx, sh_dx))

    at0 = place[:, 0, None] == slot_ids[None, :]
    at1 = place[:, 1, None] == slot_ids[None, :]
    dn2_part = jnp.dot((at0 | at1).astype(BF), back_dx, preferred_element_type=F32)
    dgates = jnp.stack(
        [
            jnp.sum(jnp.where(at0, back_dgate[None, :], 0.0), axis=1),
            jnp.sum(jnp.where(at1, back_dgate[None, :], 0.0), axis=1),
        ],
        axis=1,
    )
    dchosen = gates * (dgates - jnp.sum(gates * dgates, axis=1, keepdims=True))
    dlogits = jnp.sum(jnp.where(picked, dchosen[:, :, None], 0.0), axis=1).astype(BF)
    dn2_part = (
        dn2_part
        + sh_dx.reshape(rows, width).astype(F32)
        + jnp.einsum("le,de->ld", dlogits, router_full, preferred_element_type=F32)
    )
    dn2_low = dn2_part.astype(BF)
    back_y = swap(after(y, dn2_low)).reshape(slots, width)
    dn2 = lax.psum(dn2_low, "tensor")
    dn2, back_y = lax.optimization_barrier((dn2, back_y))
    g_eout, sh_grad, _ = lax.optimization_barrier(
        (g_eout, jnp.concatenate([sh_gin[0], sh_gout], axis=0), dn2)
    )
    if spread:
        grad_eout = lax.all_to_all(g_eout, "ctx", split_axis=1, concat_axis=0, tiled=True)
    else:
        grad_eout = lax.psum_scatter(g_eout, "ctx", scatter_dimension=1, tiled=True)
    total_shared = own_sum(sh_grad, 1)
    dn2 = dn2.astype(F32)
    router_part = jnp.einsum("ld,le->de", normed2, dlogits, preferred_element_type=F32)
    gain2_part = jnp.sum(dn2_part * n2, axis=0)

    scaled2 = ffn_gain * dn2
    dresid = grad_layer + inv2 * (scaled2 - n2 * jnp.mean(scaled2 * n2, axis=-1, keepdims=True))
    dbranch = dresid.astype(BF)
    datt_t = jnp.einsum("dc,ld->cl", out_full, dbranch, preferred_element_type=F32).astype(BF)

    weight0 = jnp.where(at0, gates[:, 0, None], 0.0)
    weight1 = jnp.where(at1, gates[:, 1, None], 0.0)
    ffn_part = jnp.dot(
        (weight0 + weight1).astype(BF), back_y, preferred_element_type=F32
    ) + sh_y.reshape(rows, width).astype(F32)
    ffn_low, datt_t = lax.optimization_barrier((ffn_part.astype(BF), datt_t))
    ffn_total = lax.psum(ffn_low, "tensor")

    dq_t, dk_win, dv_win = attn_backward(
        lo, q_t, k_win, v_win, att_t, datt_t, lse, doc, shift
    )
    dkv_win = jnp.concatenate([dk_win, dv_win], axis=0)
    dkv = dkv_win[:, shift:]
    for hop in range(1, before + 1):
        links = [(i + hop, i) for i in range(ctx_count - hop)]
        piece = dkv_win[:, shift - hop * rows : shift - (hop - 1) * rows]
        dkv = dkv + lax.ppermute(piece.astype(BF), "ctx", links).astype(F32)
    dq_raw = half_turn(dq_t, cos_t, -sin_t)
    dk_raw = half_turn(dkv[:heads_cols], cos_t, -sin_t)
    draw_t = jnp.concatenate([dq_raw, dk_raw, dkv[heads_cols:]], axis=0).astype(BF)
    dn1_part = jnp.einsum("cl,dc->ld", draw_t, qkv_full, preferred_element_type=F32)
    dn1_low, ffn_total, g_ein, grad_eout, total_shared = lax.optimization_barrier(
        (dn1_part.astype(BF), ffn_total, g_ein, grad_eout, total_shared)
    )
    layer_out = (resid + ffn_total.astype(F32)).astype(BF)
    dn1 = lax.psum(dn1_low, "tensor")
    gain1_part = jnp.sum(dn1_part * n1, axis=0)
    grad_qkv = jnp.einsum("ld,cl->dc", normed, draw_t, preferred_element_type=F32)
    grad_outw = jnp.einsum("ld,cl->dc", dbranch, att_t, preferred_element_type=F32)
    small = jnp.concatenate([router_part, gain1_part[:, None], gain2_part[:, None]], axis=1)
    tail = own_sum(
        jnp.concatenate([grad_qkv, grad_outw, small], axis=1), 0
    )
    total_qkv = tail[:, : 3 * heads_cols].reshape(-1, 3, heads_cols).transpose(1, 0, 2)
    total_outw = tail[:, 3 * heads_cols : 4 * heads_cols]
    small = lax.psum(tail[:, 4 * heads_cols :], "tensor")
    g_ein = after(g_ein, tail)
    if spread:
        grad_ein = lax.all_to_all(g_ein, "ctx", split_axis=2, concat_axis=0, tiled=True)
    else:
        grad_ein = lax.psum_scatter(g_ein, "ctx", scatter_dimension=2, tiled=True)
    dn1 = after(dn1, small, grad_ein).astype(F32)
    scaled1 = attn_gain * dn1
    grad_tokens = dresid + inv1 * (
        scaled1 - n1 * jnp.mean(scaled1 * n1, axis=-1, keepdims=True)
    )
    return (
        layer_out[None],
        grad_tokens[None],
        small[:, experts],
        total_qkv,
        total_outw,
        small[:, experts + 1],
        small[:, :experts],
        total_shared[:2],
        total_shared[2],
        grad_ein.astype(F32),
        grad_eout.astype(F32),
    )


def solution(mesh):
    return jax.shard_map(
        shards,
        mesh=mesh,
        in_specs=(
            P("dp", "ctx", None),
            P("dp", None),
            P("dp", "ctx", None),
            P("dp", "ctx", None),
            P(DC),
            P(None, DC, "tensor"),
            P(DC, "tensor"),
            P(DC),
            P(DC, None),
            P(None, DC, "tensor"),
            P(DC, "tensor"),
            P("dp", None, "ctx", "tensor"),
            P("dp", "ctx", "tensor"),
            P("dp", "ctx", None),
        ),
        out_specs=(
            P("dp", "ctx", None),
            P("dp", "ctx", None),
            P(DC),
            P(None, DC, "tensor"),
            P(DC, "tensor"),
            P(DC),
            P(DC, None),
            P(None, DC, "tensor"),
            P(DC, "tensor"),
            P("dp", None, "ctx", "tensor"),
            P("dp", "ctx", "tensor"),
        ),
        check_vma=False,
    )
```

```python
import functools
import math

import jax
import jax.numpy as jnp
from jax import lax
from jax.experimental import pallas as pl
from jax.experimental.layout import Layout, with_layout_constraint
from jax.experimental.pallas import tpu as pltpu
from jax.sharding import PartitionSpec as P

HD = 64
HALF = HD // 2
EPSILON = 1e-06
LONGEST = 2000
DOCS = 5
BQ = 512
BK = 256
BF = jnp.bfloat16
F32 = jnp.float32
NEG = -1e30
DC = ("dp", "ctx")


def mm(a, b, ca, cb):
    return lax.dot_general(a, b, (((ca,), (cb,)), ((), ())), preferred_element_type=F32)


def attn_mask(key_start, query_start, doc_row):
    kpos = key_start + lax.broadcasted_iota(jnp.int32, (BK, BQ), 0)
    qpos = query_start + lax.broadcasted_iota(jnp.int32, (BK, BQ), 1)
    return (kpos <= qpos) & (kpos >= doc_row)


def attn_fwd_kernel(lo_ref, q_ref, k_ref, v_ref, doc_ref, o_ref, lse_ref, *, shift):
    cols, rows = q_ref.shape
    heads = [slice(at, at + HD) for at in range(0, cols, HD)]
    for qb in range(rows // BQ):
        here = slice(qb * BQ, (qb + 1) * BQ)
        qs = [q_ref[h, here] * 0.125 for h in heads]
        doc = doc_ref[:, here]
        q0 = shift + qb * BQ

        def step(b, carry, qs=qs, doc=doc, q0=q0):
            off = pl.multiple_of(b * BK, BK)
            mask = attn_mask(off, q0, doc)
            scores = [
                jnp.where(mask, mm(k_ref[h, pl.ds(off, BK)], q, 0, 0), NEG)
                for h, q in zip(heads, qs)
            ]
            out = []
            for h, s, (peak, total, acc) in zip(heads, scores, carry):
                new = jnp.maximum(peak, jnp.max(s, axis=0, keepdims=True))
                p = jnp.exp(s - new)
                fix = jnp.exp(peak - new)
                total = total * fix + jnp.sum(p, axis=0, keepdims=True)
                acc = acc * fix + mm(v_ref[h, pl.ds(off, BK)], p.astype(BF), 1, 0)
                out.append((new, total, acc))
            return tuple(out)

        init = tuple(
            (
                jnp.full((1, BQ), NEG, F32),
                jnp.zeros((1, BQ), F32),
                jnp.zeros((HD, BQ), F32),
            )
            for _ in heads
        )
        last = (q0 + BQ - 1) // BK
        carry = step(last, init)
        carry = lax.fori_loop(lo_ref[qb], last, step, carry)
        for n, (h, (peak, total, acc)) in enumerate(zip(heads, carry)):
            o_ref[h, here] = (acc / total).astype(BF)
            lse_ref[n : n + 1, here] = peak + jnp.log(total)


def attn_bwd_kernel(
    lo_ref, q_ref, k_ref, v_ref, o_ref, do_ref, lse_ref, doc_ref, dq_ref, dk_ref, dv_ref, *, shift
):
    cols, rows = q_ref.shape
    heads = [slice(at, at + HD) for at in range(0, cols, HD)]
    dk_ref[...] = jnp.zeros_like(dk_ref)
    dv_ref[...] = jnp.zeros_like(dv_ref)
    for qb in range(rows // BQ):
        here = slice(qb * BQ, (qb + 1) * BQ)
        qs = [q_ref[h, here] * 0.125 for h in heads]
        dos = [do_ref[h, here] for h in heads]
        doc = doc_ref[:, here]
        lses = [lse_ref[n : n + 1, here] for n in range(len(heads))]
        deltas = [
            jnp.sum(do.astype(F32) * o_ref[h, here].astype(F32), axis=0, keepdims=True)
            for h, do in zip(heads, dos)
        ]
        q0 = shift + qb * BQ

        def step(b, dqs, qs=qs, dos=dos, doc=doc, lses=lses, deltas=deltas, q0=q0):
            off = pl.multiple_of(b * BK, BK)
            keys = pl.ds(off, BK)
            mask = attn_mask(off, q0, doc)
            scores = [
                jnp.where(mask, mm(k_ref[h, keys], q, 0, 0), NEG) for h, q in zip(heads, qs)
            ]
            dps = [mm(v_ref[h, keys], do, 0, 0) for h, do in zip(heads, dos)]
            out = []
            for n, h in enumerate(heads):
                p = jnp.exp(scores[n] - lses[n])
                ds = (p * (dps[n] - deltas[n])).astype(BF)
                dk_ref[h, keys] += mm(qs[n], ds, 1, 1)
                dv_ref[h, keys] += mm(dos[n], p.astype(BF), 1, 1)
                out.append(dqs[n] + mm(k_ref[h, keys], ds, 1, 0))
            return tuple(out)

        last = (q0 + BQ - 1) // BK
        zero = tuple(jnp.zeros((HD, BQ), F32) for _ in heads)
        dqs = lax.fori_loop(lo_ref[qb], last + 1, step, zero)
        for h, dq in zip(heads, dqs):
            dq_ref[h, here] = dq * 0.125


def whole(shape):
    return pl.BlockSpec(shape, lambda n, lo: (0, 0))


def attn_forward(lo, q_t, k_t, v_t, doc, shift):
    heads, rows = q_t.shape[0] // HD, q_t.shape[1]
    ins = (q_t, k_t, v_t, doc)
    outs = (
        jax.ShapeDtypeStruct(q_t.shape, BF),
        jax.ShapeDtypeStruct((heads, rows), F32),
    )
    return pl.pallas_call(
        functools.partial(attn_fwd_kernel, shift=shift),
        out_shape=outs,
        grid_spec=pltpu.PrefetchScalarGridSpec(
            num_scalar_prefetch=1,
            grid=(1,),
            in_specs=[whole(v.shape) for v in ins],
            out_specs=[whole(v.shape) for v in outs],
        ),
        name="attn_fwd",
    )(lo, *ins)


def attn_backward(lo, q_t, k_t, v_t, o_t, do_t, lse, doc, shift):
    ins = (q_t, k_t, v_t, o_t, do_t, lse, doc)
    outs = (
        jax.ShapeDtypeStruct(q_t.shape, F32),
        jax.ShapeDtypeStruct(k_t.shape, F32),
        jax.ShapeDtypeStruct(k_t.shape, F32),
    )
    return pl.pallas_call(
        functools.partial(attn_bwd_kernel, shift=shift),
        out_shape=outs,
        grid_spec=pltpu.PrefetchScalarGridSpec(
            num_scalar_prefetch=1,
            grid=(1,),
            in_specs=[whole(v.shape) for v in ins],
            out_specs=[whole(v.shape) for v in outs],
        ),
        name="attn_bwd",
    )(lo, *ins)


def ffn_kernel(*refs, gated):
    if gated:
        first_ref, x_ref, g_ref, other_ref, router_ref, win_ref, wout_ref = refs[:7]
        y_ref, dx_ref, gin_ref, gout_ref, grouter_ref, acc_in, acc_out, acc_router = refs[7:]
    else:
        x_ref, g_ref, win_ref, wout_ref = refs[:4]
        y_ref, dx_ref, gin_ref, gout_ref, acc_in, acc_out = refs[4:]
    src, _, rows, width = x_ref.shape
    expert, step = pl.program_id(0), pl.program_id(1)

    @pl.when(step == 0)
    def _():
        acc_in[...] = jnp.zeros_like(acc_in)
        acc_out[...] = jnp.zeros_like(acc_out)

    if gated:

        @pl.when((step == 0) & (expert == 0))
        def _():
            acc_router[...] = jnp.zeros_like(acc_router)

    x = x_ref[...].reshape(src * rows, width)
    g = g_ref[...].reshape(src * rows, width)
    w_gate = win_ref[0, 0]
    w_up = win_ref[0, 1]
    w_out = wout_ref[0]
    gate_pre = mm(x, w_gate, 1, 0)
    up_pre = mm(x, w_up, 1, 0)
    sig = 1.0 / (1.0 + jnp.exp(-gate_pre))
    silu = gate_pre * sig
    hidden = (silu * up_pre).astype(BF)
    y = mm(hidden, w_out, 1, 1)
    if gated:
        router = router_ref[...]
        logits = mm(x, router, 1, 0)
        ids = lax.broadcasted_iota(jnp.int32, logits.shape, 1)
        here = ids == first_ref[0] + expert
        there = ids == other_ref[...].reshape(src * rows, 1)
        apart = jnp.sum(
            jnp.where(here, logits, 0.0) - jnp.where(there, logits, 0.0), axis=1, keepdims=True
        )
        gate = 1.0 / (1.0 + jnp.exp(-apart))
        gate_other = 1.0 / (1.0 + jnp.exp(apart))
        gf = g.astype(F32)
        dpair = gate * gate_other * jnp.sum(gf * y, axis=1, keepdims=True)
        dlogits = (jnp.where(here, dpair, 0.0) - jnp.where(there, dpair, 0.0)).astype(BF)
        acc_router[...] += mm(x, dlogits, 0, 0)
        dy = (gate * gf).astype(BF)
        y = gate * y
    else:
        dy = g
    y_ref[...] = y.astype(BF).reshape(src, 1, rows, width)
    dh = mm(dy, w_out, 1, 0)
    dgp = (dh * up_pre * (sig * (1.0 + gate_pre * (1.0 - sig)))).astype(BF)
    dup = (dh * silu).astype(BF)
    dx = mm(dgp, w_gate, 1, 1) + mm(dup, w_up, 1, 1)
    if gated:
        dx = dx + mm(dlogits, router, 1, 1)
    dx_ref[...] = dx.astype(BF).reshape(src, 1, rows, width)
    acc_in[0] += mm(x, dgp, 0, 0)
    acc_in[1] += mm(x, dup, 0, 0)
    acc_out[...] += mm(dy, hidden, 0, 0)

    @pl.when(step == pl.num_programs(1) - 1)
    def _():
        gin_ref[0] = acc_in[...].astype(BF)
        gout_ref[0] = acc_out[...].astype(BF)
        if gated:
            grouter_ref[...] = acc_router[...]


def ffn(x, g, w_in, w_out, block, routing=None):
    sources, experts, rows, width = x.shape
    units = w_out.shape[2]
    gated = routing is not None
    block = math.gcd(sources, block)
    big = pl.BlockSpec((block, 1, rows, width), lambda e, s, *_: (s, e, 0, 0))
    w_in_spec = pl.BlockSpec((1, 2, width, units), lambda e, s, *_: (e, 0, 0, 0))
    w_out_spec = pl.BlockSpec((1, width, units), lambda e, s, *_: (e, 0, 0))
    wide = jax.ShapeDtypeStruct(x.shape, BF)
    ins = [x, g]
    in_specs = [big, big]
    outs = [
        wide,
        wide,
        jax.ShapeDtypeStruct((experts, 2, width, units), BF),
        jax.ShapeDtypeStruct((experts, width, units), BF),
    ]
    out_specs = [big, big, w_in_spec, w_out_spec]
    scratch = [pltpu.VMEM((2, width, units), F32), pltpu.VMEM((width, units), F32)]
    if gated:
        first, other, router = routing
        router_spec = pl.BlockSpec(router.shape, lambda e, s, *_: (0, 0))
        ins = [first] + ins + [other, router]
        in_specs += [pl.BlockSpec((block, 1, rows, 1), lambda e, s, *_: (s, e, 0, 0)), router_spec]
        outs.append(jax.ShapeDtypeStruct(router.shape, F32))
        out_specs.append(router_spec)
        scratch.append(pltpu.VMEM(router.shape, F32))
    return pl.pallas_call(
        functools.partial(ffn_kernel, gated=gated),
        out_shape=outs,
        grid_spec=pltpu.PrefetchScalarGridSpec(
            num_scalar_prefetch=1 if gated else 0,
            grid=(experts, sources // block),
            in_specs=in_specs + [w_in_spec, w_out_spec],
            out_specs=out_specs,
            scratch_shapes=scratch,
        ),
        compiler_params=pltpu.CompilerParams(
            dimension_semantics=("arbitrary", "arbitrary"), vmem_limit_bytes=56 * 1024 * 1024
        ),
        name="ffn_experts" if gated else "ffn_shared",
    )(*ins, w_in, w_out)


def after(value, *first):
    return lax.optimization_barrier((value,) + first)[0]


def pair_slots(pair_route, order, experts, capacity):
    count = order.shape[0]
    flat = pair_route.reshape(count)
    number = jnp.arange(count, dtype=jnp.int32)
    ids = jnp.arange(experts, dtype=jnp.int32)
    owner = (flat[:, None] == ids[None, :]).astype(BF)
    ranked = jnp.dot(
        (order[:, None] == number[None, :]).astype(BF), owner, preferred_element_type=F32
    ).astype(BF)
    earlier = jnp.dot(
        (number[None, :] < number[:, None]).astype(BF), ranked, preferred_element_type=F32
    )
    ranked_slot = (jnp.minimum(earlier, float(capacity)) * ranked).astype(BF)
    slot = jnp.sum(
        jnp.dot(
            (order[None, :] == number[:, None]).astype(BF),
            ranked_slot,
            preferred_element_type=F32,
        ),
        axis=1,
    ).astype(jnp.int32)
    place = jnp.where(slot < capacity, flat * capacity + slot, experts * capacity)
    return place.reshape(pair_route.shape)


def own_sum(parts, axis):
    devices = lax.axis_size(DC)
    shape = parts.shape
    cut = shape[:axis] + (devices, shape[axis] // devices) + shape[axis + 1 :]
    swapped = lax.all_to_all(
        parts.astype(BF).reshape(cut), DC, split_axis=axis, concat_axis=axis, tiled=True
    )
    return jnp.sum(swapped.astype(F32), axis=axis)


def half_turn(values_t, cos_t, sin_t):
    cols, rows = values_t.shape
    split = values_t.reshape(cols // HD, 2, HALF, rows)
    a, b = split[:, 0], split[:, 1]
    return jnp.stack([a * cos_t - b * sin_t, b * cos_t + a * sin_t], axis=1).reshape(cols, rows)


def shards(
    tokens,
    segment_ids,
    routes,
    pair_order,
    gain_attn,
    qkv_weight,
    out_weight,
    gain_ffn,
    router_weight,
    shared_in,
    shared_out,
    expert_in,
    expert_out,
    out_grad,
):
    rows, width = tokens.shape[1], tokens.shape[2]
    ctx_count = lax.axis_size("ctx")
    ctx_at = lax.axis_index("ctx")
    inputs = tokens[0].astype(F32)
    grad_low = out_grad[0]
    grad_layer = grad_low.astype(F32)
    seg_all = segment_ids[0]
    my_routes = routes[0]

    heads_cols = qkv_weight.shape[2]
    qkv_cols = 3 * heads_cols
    experts = router_weight.shape[1]
    thin = jnp.concatenate(
        [
            qkv_weight.transpose(1, 0, 2).reshape(-1, qkv_cols),
            out_weight,
            router_weight,
            gain_attn[:, None],
            gain_ffn[:, None],
        ],
        axis=1,
    )
    thin_full = lax.all_gather(thin, DC, axis=0, tiled=True)
    qkv_full = thin_full[:, :qkv_cols]
    out_full = thin_full[:, qkv_cols : qkv_cols + heads_cols]
    out_tensor = lax.all_gather(out_full, "tensor", axis=0)
    router_full = thin_full[:, qkv_cols + heads_cols : qkv_cols + heads_cols + experts]
    attn_gain = thin_full[:, -2].astype(F32)
    ffn_gain = thin_full[:, -1].astype(F32)

    local_experts = expert_in.shape[0]
    spread = local_experts % ctx_count == 0
    expert_axes = DC if spread else ("dp",)
    owners = lax.axis_size(expert_axes)
    own = experts // owners
    capacity = 10 * rows // (4 * experts)
    slots = experts * capacity

    def swap(values):
        return lax.all_to_all(values, expert_axes, split_axis=0, concat_axis=0, tiled=True)

    place = pair_slots(my_routes, pair_order[0, 0], experts, capacity)
    slot_ids = jnp.arange(slots, dtype=jnp.int32)
    owner_at = lax.axis_index(expert_axes)
    first = owner_at * own
    my_slots = first * capacity + jnp.arange(own * capacity, dtype=jnp.int32)
    pairs = lax.all_gather(
        jnp.stack([place[:, 0], place[:, 1], my_routes[:, 1], my_routes[:, 0]]),
        expert_axes,
        axis=0,
    )
    slot_other = (
        jnp.sum(
            jnp.where(
                pairs[:, :2, None, :] == my_slots[None, None, :, None],
                pairs[:, 2:, None, :] + 1,
                0,
            ),
            axis=(1, 3),
        )
        - 1
    ).reshape(owners, own, capacity, 1)
    hit0 = place[None, :, 0] == slot_ids[:, None]
    hit1 = place[None, :, 1] == slot_ids[:, None]
    to_slot = (hit0 | hit1).astype(BF)
    slot_g = jnp.dot(to_slot, grad_low, preferred_element_type=F32).astype(BF)

    inv1 = lax.rsqrt(jnp.mean(inputs * inputs, axis=-1, keepdims=True) + EPSILON)
    n1 = inputs * inv1
    normed = (n1 * attn_gain).astype(BF)
    row_start = ctx_at * rows
    query_pos = row_start + jnp.arange(rows, dtype=jnp.int32)
    inverse = 1.0 / 10000.0 ** (jnp.arange(HALF, dtype=F32) * (2.0 / HD))
    angles = inverse[:, None] * query_pos.astype(F32)[None, :]
    cos_t, sin_t = jnp.cos(angles), jnp.sin(angles)
    raw_t = jnp.einsum("dc,ld->cl", qkv_full, normed, preferred_element_type=F32)
    q_t = half_turn(raw_t[:heads_cols], cos_t, sin_t).astype(BF)
    k_t = half_turn(raw_t[heads_cols : 2 * heads_cols], cos_t, sin_t).astype(BF)
    v_t = raw_t[2 * heads_cols :].astype(BF)
    expert_out = after(expert_out, thin_full)
    if spread:
        eout = lax.all_to_all(expert_out, "ctx", split_axis=0, concat_axis=1, tiled=True)
    else:
        eout = lax.all_gather(expert_out, "ctx", axis=1, tiled=True)
    kv_t = after(jnp.concatenate([k_t, v_t], axis=0), slot_other, slot_g)
    before = min(ctx_count - 1, -(-(LONGEST - 1) // rows))
    shift = before * rows
    pieces = [kv_t]
    for hop in range(1, before + 1):
        links = [(i, i + hop) for i in range(ctx_count - hop)]
        pieces.insert(0, lax.ppermute(kv_t, "ctx", links))
    kv_win = jnp.concatenate(pieces, axis=1)
    k_win, v_win = kv_win[:heads_cols], kv_win[heads_cols:]

    expert_in = after(expert_in, kv_win)
    if spread:
        ein = lax.all_to_all(expert_in, "ctx", split_axis=0, concat_axis=2, tiled=True)
    else:
        ein = lax.all_gather(expert_in, "ctx", axis=2, tiled=True)

    starts = jnp.sum(
        seg_all[:, None] < jnp.arange(DOCS, dtype=jnp.int32)[None, :], axis=0, dtype=jnp.int32
    )
    query_seg = lax.dynamic_slice_in_dim(seg_all, row_start, rows)
    doc = jnp.sum(
        jnp.where(
            query_seg[:, None] == jnp.arange(DOCS, dtype=jnp.int32)[None, :], starts[None, :], 0
        ),
        axis=1,
    ) - (row_start - shift)
    lo = jnp.maximum(doc[::BQ], 0) // BK
    doc = doc[None, :]
    att_t, lse = attn_forward(lo, q_t, k_win, v_win, doc, shift)
    tensor_count = lax.axis_size("tensor")
    tensor_at = lax.axis_index("tensor")
    att_parts, out_parts = [att_t], [out_full]
    for hop in range(1, tensor_count):
        links = [(i, (i + hop) % tensor_count) for i in range(tensor_count)]
        att_parts.append(lax.ppermute(att_t, "tensor", links))
        out_parts.append(
            lax.dynamic_index_in_dim(
                out_tensor, (tensor_at - hop) % tensor_count, 0, keepdims=False
            )
        )
    ein = after(ein, eout)
    got_g = swap(after(slot_g, ein, att_t).reshape(owners, own, capacity, width))
    branch = jnp.einsum(
        "cl,dc->ld",
        jnp.concatenate(att_parts, axis=0),
        jnp.concatenate(out_parts, axis=1),
        preferred_element_type=F32,
    )
    branch = with_layout_constraint(branch, Layout((0, 1)))
    resid = inputs + branch

    inv2 = lax.rsqrt(jnp.mean(resid * resid, axis=-1, keepdims=True) + EPSILON)
    n2 = resid * inv2
    normed2 = (n2 * ffn_gain).astype(BF)
    normed2, ein, got_g = lax.optimization_barrier((normed2, ein, got_g))
    slot_x = jnp.dot(to_slot, normed2, preferred_element_type=F32).astype(BF)
    got_x = swap(slot_x.reshape(owners, own, capacity, width))
    shared_w = after(jnp.concatenate([shared_in, shared_out[None]], axis=0), got_x)
    shared_full = lax.all_gather(shared_w, DC, axis=1, tiled=True)
    lanes = -experts % 128
    y, dx, g_ein, g_eout, router_part = ffn(
        got_x,
        got_g,
        ein,
        eout,
        4,
        (
            jnp.reshape(first, (1,)).astype(jnp.int32),
            slot_other,
            jnp.pad(router_full, ((0, 0), (0, lanes))),
        ),
    )
    router_part = router_part[:, :experts]
    back_dx = swap(dx).reshape(slots, width)

    parts = 4
    shared_shape = (parts, 1, rows // parts, width)
    sh_y, sh_dx, sh_gin, sh_gout = ffn(
        normed2.reshape(shared_shape),
        grad_low.reshape(shared_shape),
        shared_full[None, :2],
        shared_full[None, 2],
        2,
    )
    back_dx, sh_dx = lax.optimization_barrier((back_dx, sh_dx))

    from_slot = (
        (place[:, 0, None] == slot_ids[None, :]) | (place[:, 1, None] == slot_ids[None, :])
    ).astype(BF)
    dn2_part = jnp.dot(from_slot, back_dx, preferred_element_type=F32) + sh_dx.reshape(
        rows, width
    ).astype(F32)
    dn2_low = dn2_part.astype(BF)
    back_y = swap(after(y, dn2_low)).reshape(slots, width)
    dn2 = lax.psum(dn2_low, "tensor")
    g_eout = after(g_eout, back_y)
    if spread:
        grad_eout = lax.all_to_all(g_eout, "ctx", split_axis=1, concat_axis=0, tiled=True)
    else:
        grad_eout = lax.psum_scatter(g_eout, "ctx", scatter_dimension=1, tiled=True)
    dn2, back_y, grad_eout = lax.optimization_barrier((dn2, back_y, grad_eout))
    sh_grad = after(jnp.concatenate([sh_gin[0], sh_gout], axis=0), dn2)
    total_shared = own_sum(sh_grad, 1)
    dn2 = dn2.astype(F32)
    gain2_part = jnp.sum(dn2_part * n2, axis=0)

    scaled2 = ffn_gain * dn2
    dresid = grad_layer + inv2 * (scaled2 - n2 * jnp.mean(scaled2 * n2, axis=-1, keepdims=True))
    dbranch = dresid.astype(BF)
    datt_t = jnp.einsum("dc,ld->cl", out_full, dbranch, preferred_element_type=F32).astype(BF)

    ffn_part = jnp.dot(from_slot, back_y, preferred_element_type=F32) + sh_y.reshape(
        rows, width
    ).astype(F32)
    ffn_low, datt_t = lax.optimization_barrier((ffn_part.astype(BF), datt_t))
    ffn_total = lax.psum(ffn_low, "tensor")

    dq_t, dk_win, dv_win = attn_backward(
        lo, q_t, k_win, v_win, att_t, datt_t, lse, doc, shift
    )
    dkv_win = jnp.concatenate([dk_win, dv_win], axis=0)
    dkv = dkv_win[:, shift:]
    for hop in range(1, before + 1):
        links = [(i + hop, i) for i in range(ctx_count - hop)]
        piece = dkv_win[:, shift - hop * rows : shift - (hop - 1) * rows]
        dkv = dkv + lax.ppermute(piece.astype(BF), "ctx", links).astype(F32)
    dq_raw = half_turn(dq_t, cos_t, -sin_t)
    dk_raw = half_turn(dkv[:heads_cols], cos_t, -sin_t)
    draw_t = jnp.concatenate([dq_raw, dk_raw, dkv[heads_cols:]], axis=0).astype(BF)
    dn1_part = jnp.einsum("cl,dc->ld", draw_t, qkv_full, preferred_element_type=F32)
    dn1_low, ffn_total = lax.optimization_barrier((dn1_part.astype(BF), ffn_total))
    layer_out = (resid + ffn_total.astype(F32)).astype(BF)
    dn1 = lax.psum(dn1_low, "tensor")
    gain1_part = jnp.sum(dn1_part * n1, axis=0)
    grad_qkv = jnp.einsum("ld,cl->dc", normed, draw_t, preferred_element_type=F32)
    grad_outw = jnp.einsum("ld,cl->dc", dbranch, att_t, preferred_element_type=F32)
    small = jnp.concatenate([router_part, gain1_part[:, None], gain2_part[:, None]], axis=1)
    tail = own_sum(
        jnp.concatenate([grad_qkv, grad_outw, small], axis=1), 0
    )
    total_qkv = tail[:, : 3 * heads_cols].reshape(-1, 3, heads_cols).transpose(1, 0, 2)
    total_outw = tail[:, 3 * heads_cols : 4 * heads_cols]
    small = lax.psum(tail[:, 4 * heads_cols :], "tensor")
    g_ein = after(g_ein, tail, total_shared)
    if spread:
        grad_ein = lax.all_to_all(g_ein, "ctx", split_axis=2, concat_axis=0, tiled=True)
    else:
        grad_ein = lax.psum_scatter(g_ein, "ctx", scatter_dimension=2, tiled=True)
    dn1 = after(dn1, small, grad_ein).astype(F32)
    scaled1 = attn_gain * dn1
    grad_tokens = dresid + inv1 * (
        scaled1 - n1 * jnp.mean(scaled1 * n1, axis=-1, keepdims=True)
    )
    return (
        layer_out[None],
        grad_tokens[None],
        small[:, experts],
        total_qkv,
        total_outw,
        small[:, experts + 1],
        small[:, :experts],
        total_shared[:2],
        total_shared[2],
        grad_ein.astype(F32),
        grad_eout.astype(F32),
    )


def solution(mesh):
    return jax.shard_map(
        shards,
        mesh=mesh,
        in_specs=(
            P("dp", "ctx", None),
            P("dp", None),
            P("dp", "ctx", None),
            P("dp", "ctx", None),
            P(DC),
            P(None, DC, "tensor"),
            P(DC, "tensor"),
            P(DC),
            P(DC, None),
            P(None, DC, "tensor"),
            P(DC, "tensor"),
            P("dp", None, "ctx", "tensor"),
            P("dp", "ctx", "tensor"),
            P("dp", "ctx", None),
        ),
        out_specs=(
            P("dp", "ctx", None),
            P("dp", "ctx", None),
            P(DC),
            P(None, DC, "tensor"),
            P(DC, "tensor"),
            P(DC),
            P(DC, None),
            P(None, DC, "tensor"),
            P(DC, "tensor"),
            P("dp", None, "ctx", "tensor"),
            P("dp", "ctx", "tensor"),
        ),
        check_vma=False,
    )
```

```python
import functools
import math

import jax
import jax.numpy as jnp
from jax import lax
from jax.experimental import pallas as pl
from jax.experimental.layout import Layout, with_layout_constraint
from jax.experimental.pallas import tpu as pltpu
from jax.sharding import PartitionSpec as P


HD = 64
HALF = HD // 2
EPSILON = 1e-06
LONGEST = 2000
DOCS = 5
BQ = 512
BK = 256
BF = jnp.bfloat16
F32 = jnp.float32
NEG = -1e30
DC = ("dp", "ctx")


def mm(a, b, ca, cb):
    return lax.dot_general(a, b, (((ca,), (cb,)), ((), ())), preferred_element_type=F32)


def attn_mask(key_start, query_start, doc_row):
    kpos = key_start + lax.broadcasted_iota(jnp.int32, (BK, BQ), 0)
    qpos = query_start + lax.broadcasted_iota(jnp.int32, (BK, BQ), 1)
    return (kpos <= qpos) & (kpos >= doc_row)


def attn_fwd_kernel(lo_ref, q_ref, k_ref, v_ref, doc_ref, o_ref, lse_ref, *, shift):
    cols, rows = q_ref.shape
    heads = [slice(at, at + HD) for at in range(0, cols, HD)]
    for qb in range(rows // BQ):
        here = slice(qb * BQ, (qb + 1) * BQ)
        qs = [q_ref[h, here] * 0.125 for h in heads]
        doc = doc_ref[:, here]
        q0 = shift + qb * BQ

        def step(b, carry, qs=qs, doc=doc, q0=q0):
            off = pl.multiple_of(b * BK, BK)
            mask = attn_mask(off, q0, doc)
            scores = [
                jnp.where(mask, mm(k_ref[h, pl.ds(off, BK)], q, 0, 0), NEG)
                for h, q in zip(heads, qs)
            ]
            out = []
            for h, s, (peak, total, acc) in zip(heads, scores, carry):
                new = jnp.maximum(peak, jnp.max(s, axis=0, keepdims=True))
                p = jnp.exp(s - new)
                fix = jnp.exp(peak - new)
                total = total * fix + jnp.sum(p, axis=0, keepdims=True)
                acc = acc * fix + mm(v_ref[h, pl.ds(off, BK)], p.astype(BF), 1, 0)
                out.append((new, total, acc))
            return tuple(out)

        init = tuple(
            (
                jnp.full((1, BQ), NEG, F32),
                jnp.zeros((1, BQ), F32),
                jnp.zeros((HD, BQ), F32),
            )
            for _ in heads
        )
        last = (q0 + BQ - 1) // BK
        carry = step(last, init)
        carry = lax.fori_loop(lo_ref[qb], last, step, carry)
        for n, (h, (peak, total, acc)) in enumerate(zip(heads, carry)):
            o_ref[h, here] = (acc / total).astype(BF)
            lse_ref[n : n + 1, here] = peak + jnp.log(total)


def attn_bwd_kernel(
    lo_ref, q_ref, k_ref, v_ref, o_ref, do_ref, lse_ref, doc_ref, dq_ref, dk_ref, dv_ref, *, shift
):
    cols, rows = q_ref.shape
    heads = [slice(at, at + HD) for at in range(0, cols, HD)]
    dk_ref[...] = jnp.zeros_like(dk_ref)
    dv_ref[...] = jnp.zeros_like(dv_ref)
    for qb in range(rows // BQ):
        here = slice(qb * BQ, (qb + 1) * BQ)
        qs = [q_ref[h, here] * 0.125 for h in heads]
        dos = [do_ref[h, here] for h in heads]
        doc = doc_ref[:, here]
        lses = [lse_ref[n : n + 1, here] for n in range(len(heads))]
        deltas = [
            jnp.sum(do.astype(F32) * o_ref[h, here].astype(F32), axis=0, keepdims=True)
            for h, do in zip(heads, dos)
        ]
        q0 = shift + qb * BQ

        def step(b, dqs, qs=qs, dos=dos, doc=doc, lses=lses, deltas=deltas, q0=q0):
            off = pl.multiple_of(b * BK, BK)
            keys = pl.ds(off, BK)
            mask = attn_mask(off, q0, doc)
            scores = [
                jnp.where(mask, mm(k_ref[h, keys], q, 0, 0), NEG) for h, q in zip(heads, qs)
            ]
            dps = [mm(v_ref[h, keys], do, 0, 0) for h, do in zip(heads, dos)]
            out = []
            for n, h in enumerate(heads):
                p = jnp.exp(scores[n] - lses[n])
                ds = (p * (dps[n] - deltas[n])).astype(BF)
                dk_ref[h, keys] += mm(qs[n], ds, 1, 1)
                dv_ref[h, keys] += mm(dos[n], p.astype(BF), 1, 1)
                out.append(dqs[n] + mm(k_ref[h, keys], ds, 1, 0))
            return tuple(out)

        last = (q0 + BQ - 1) // BK
        zero = tuple(jnp.zeros((HD, BQ), F32) for _ in heads)
        dqs = lax.fori_loop(lo_ref[qb], last + 1, step, zero)
        for h, dq in zip(heads, dqs):
            dq_ref[h, here] = dq * 0.125


def whole(shape):
    return pl.BlockSpec(shape, lambda n, lo: (0, 0))


def attn_forward(lo, q_t, k_t, v_t, doc, shift):
    heads, rows = q_t.shape[0] // HD, q_t.shape[1]
    ins = (q_t, k_t, v_t, doc)
    outs = (
        jax.ShapeDtypeStruct(q_t.shape, BF),
        jax.ShapeDtypeStruct((heads, rows), F32),
    )
    return pl.pallas_call(
        functools.partial(attn_fwd_kernel, shift=shift),
        out_shape=outs,
        grid_spec=pltpu.PrefetchScalarGridSpec(
            num_scalar_prefetch=1,
            grid=(1,),
            in_specs=[whole(v.shape) for v in ins],
            out_specs=[whole(v.shape) for v in outs],
        ),
        name="attn_fwd",
    )(lo, *ins)


def attn_backward(lo, q_t, k_t, v_t, o_t, do_t, lse, doc, shift):
    ins = (q_t, k_t, v_t, o_t, do_t, lse, doc)
    outs = (
        jax.ShapeDtypeStruct(q_t.shape, F32),
        jax.ShapeDtypeStruct(k_t.shape, F32),
        jax.ShapeDtypeStruct(k_t.shape, F32),
    )
    return pl.pallas_call(
        functools.partial(attn_bwd_kernel, shift=shift),
        out_shape=outs,
        grid_spec=pltpu.PrefetchScalarGridSpec(
            num_scalar_prefetch=1,
            grid=(1,),
            in_specs=[whole(v.shape) for v in ins],
            out_specs=[whole(v.shape) for v in outs],
        ),
        name="attn_bwd",
    )(lo, *ins)


def ffn_kernel(*refs, gated):
    if gated:
        first_ref, x_ref, g_ref, other_ref, router_ref, win_ref, wout_ref = refs[:7]
        y_ref, dx_ref, gin_ref, gout_ref, grouter_ref, acc_in, acc_out, acc_router = refs[7:]
    else:
        x_ref, g_ref, win_ref, wout_ref = refs[:4]
        y_ref, dx_ref, gin_ref, gout_ref, acc_in, acc_out = refs[4:]
    src, _, rows, width = x_ref.shape
    expert, step = pl.program_id(0), pl.program_id(1)

    @pl.when(step == 0)
    def _():
        acc_in[...] = jnp.zeros_like(acc_in)
        acc_out[...] = jnp.zeros_like(acc_out)

    if gated:

        @pl.when((step == 0) & (expert == 0))
        def _():
            acc_router[...] = jnp.zeros_like(acc_router)

    x = x_ref[...].reshape(src * rows, width)
    g = g_ref[...].reshape(src * rows, width)
    w_gate = win_ref[0, 0]
    w_up = win_ref[0, 1]
    w_out = wout_ref[0]
    gate_pre = mm(x, w_gate, 1, 0)
    up_pre = mm(x, w_up, 1, 0)
    sig = 1.0 / (1.0 + jnp.exp(-gate_pre))
    silu = gate_pre * sig
    hidden = (silu * up_pre).astype(BF)
    y = mm(hidden, w_out, 1, 1)
    if gated:
        router = router_ref[...]
        logits = mm(x, router, 1, 0)
        ids = lax.broadcasted_iota(jnp.int32, logits.shape, 1)
        here = ids == first_ref[0] + expert
        there = ids == other_ref[...].reshape(src * rows, 1)
        apart = jnp.sum(
            jnp.where(here, logits, 0.0) - jnp.where(there, logits, 0.0), axis=1, keepdims=True
        )
        gate = 1.0 / (1.0 + jnp.exp(-apart))
        gate_other = 1.0 / (1.0 + jnp.exp(apart))
        gf = g.astype(F32)
        dpair = gate * gate_other * jnp.sum(gf * y, axis=1, keepdims=True)
        dlogits = (jnp.where(here, dpair, 0.0) - jnp.where(there, dpair, 0.0)).astype(BF)
        acc_router[...] += mm(x, dlogits, 0, 0)
        dy = (gate * gf).astype(BF)
        y = gate * y
    else:
        dy = g
    y_ref[...] = y.astype(BF).reshape(src, 1, rows, width)
    dh = mm(dy, w_out, 1, 0)
    dgp = (dh * up_pre * (sig * (1.0 + gate_pre * (1.0 - sig)))).astype(BF)
    dup = (dh * silu).astype(BF)
    dx = mm(dgp, w_gate, 1, 1) + mm(dup, w_up, 1, 1)
    if gated:
        dx = dx + mm(dlogits, router, 1, 1)
    dx_ref[...] = dx.astype(BF).reshape(src, 1, rows, width)
    acc_in[0] += mm(x, dgp, 0, 0)
    acc_in[1] += mm(x, dup, 0, 0)
    acc_out[...] += mm(dy, hidden, 0, 0)

    @pl.when(step == pl.num_programs(1) - 1)
    def _():
        gin_ref[0] = acc_in[...].astype(BF)
        gout_ref[0] = acc_out[...].astype(BF)
        if gated:
            grouter_ref[...] = acc_router[...]


def ffn(x, g, w_in, w_out, block, routing=None):
    sources, experts, rows, width = x.shape
    units = w_out.shape[2]
    gated = routing is not None
    block = math.gcd(sources, block)
    big = pl.BlockSpec((block, 1, rows, width), lambda e, s, *_: (s, e, 0, 0))
    w_in_spec = pl.BlockSpec((1, 2, width, units), lambda e, s, *_: (e, 0, 0, 0))
    w_out_spec = pl.BlockSpec((1, width, units), lambda e, s, *_: (e, 0, 0))
    wide = jax.ShapeDtypeStruct(x.shape, BF)
    ins = [x, g]
    in_specs = [big, big]
    outs = [
        wide,
        wide,
        jax.ShapeDtypeStruct((experts, 2, width, units), BF),
        jax.ShapeDtypeStruct((experts, width, units), BF),
    ]
    out_specs = [big, big, w_in_spec, w_out_spec]
    scratch = [pltpu.VMEM((2, width, units), F32), pltpu.VMEM((width, units), F32)]
    if gated:
        first, other, router = routing
        router_spec = pl.BlockSpec(router.shape, lambda e, s, *_: (0, 0))
        ins = [first] + ins + [other, router]
        in_specs += [pl.BlockSpec((block, 1, rows, 1), lambda e, s, *_: (s, e, 0, 0)), router_spec]
        outs.append(jax.ShapeDtypeStruct(router.shape, F32))
        out_specs.append(router_spec)
        scratch.append(pltpu.VMEM(router.shape, F32))
    return pl.pallas_call(
        functools.partial(ffn_kernel, gated=gated),
        out_shape=outs,
        grid_spec=pltpu.PrefetchScalarGridSpec(
            num_scalar_prefetch=1 if gated else 0,
            grid=(experts, sources // block),
            in_specs=in_specs + [w_in_spec, w_out_spec],
            out_specs=out_specs,
            scratch_shapes=scratch,
        ),
        compiler_params=pltpu.CompilerParams(
            dimension_semantics=("arbitrary", "arbitrary"), vmem_limit_bytes=56 * 1024 * 1024
        ),
        name="ffn_experts" if gated else "ffn_shared",
    )(*ins, w_in, w_out)


def tie(*values):
    return lax.optimization_barrier(values)


def pair_slots(pair_route, order, experts, capacity):
    count = order.shape[0]
    flat = pair_route.reshape(count)
    number = jnp.arange(count, dtype=jnp.int32)
    ids = jnp.arange(experts, dtype=jnp.int32)
    owner = (flat[:, None] == ids[None, :]).astype(BF)
    ranked = jnp.dot(
        (order[:, None] == number[None, :]).astype(BF), owner, preferred_element_type=F32
    ).astype(BF)
    earlier = jnp.dot(
        (number[None, :] < number[:, None]).astype(BF), ranked, preferred_element_type=F32
    )
    ranked_slot = (jnp.minimum(earlier, float(capacity)) * ranked).astype(BF)
    slot = jnp.sum(
        jnp.dot(
            (order[None, :] == number[:, None]).astype(BF),
            ranked_slot,
            preferred_element_type=F32,
        ),
        axis=1,
    ).astype(jnp.int32)
    place = jnp.where(slot < capacity, flat * capacity + slot, experts * capacity)
    return place.reshape(pair_route.shape)


def own_sum(parts, axis):
    devices = lax.axis_size(DC)
    shape = parts.shape
    cut = shape[:axis] + (devices, shape[axis] // devices) + shape[axis + 1 :]
    swapped = lax.all_to_all(
        parts.astype(BF).reshape(cut), DC, split_axis=axis, concat_axis=axis, tiled=True
    )
    return jnp.sum(swapped.astype(F32), axis=axis)


def half_turn(values_t, cos_t, sin_t):
    cols, rows = values_t.shape
    split = values_t.reshape(cols // HD, 2, HALF, rows)
    a, b = split[:, 0], split[:, 1]
    return jnp.stack([a * cos_t - b * sin_t, b * cos_t + a * sin_t], axis=1).reshape(cols, rows)


def shards(
    tokens,
    segment_ids,
    routes,
    pair_order,
    gain_attn,
    qkv_weight,
    out_weight,
    gain_ffn,
    router_weight,
    shared_in,
    shared_out,
    expert_in,
    expert_out,
    out_grad,
):
    rows, width = tokens.shape[1], tokens.shape[2]
    ctx_count = lax.axis_size("ctx")
    ctx_at = lax.axis_index("ctx")
    inputs = tokens[0].astype(F32)
    grad_low = out_grad[0]
    grad_layer = grad_low.astype(F32)
    seg_all = segment_ids[0]
    my_routes = routes[0]

    heads_cols = qkv_weight.shape[2]
    qkv_cols = 3 * heads_cols
    experts = router_weight.shape[1]
    thin = jnp.concatenate(
        [
            qkv_weight.transpose(1, 0, 2).reshape(-1, qkv_cols),
            out_weight,
            router_weight,
            gain_attn[:, None],
            gain_ffn[:, None],
        ],
        axis=1,
    )
    thin_full = lax.all_gather(thin, DC, axis=0, tiled=True)
    qkv_full = thin_full[:, :qkv_cols]
    out_full = thin_full[:, qkv_cols : qkv_cols + heads_cols]
    out_tensor = lax.all_gather(out_full, "tensor", axis=0)
    router_full = thin_full[:, qkv_cols + heads_cols : qkv_cols + heads_cols + experts]
    attn_gain = thin_full[:, -2].astype(F32)
    ffn_gain = thin_full[:, -1].astype(F32)

    local_experts = expert_in.shape[0]
    spread = local_experts % ctx_count == 0
    expert_axes = DC if spread else ("dp",)
    owners = lax.axis_size(expert_axes)
    own = experts // owners
    capacity = 10 * rows // (4 * experts)

    def swap(values):
        return lax.all_to_all(values, expert_axes, split_axis=0, concat_axis=0, tiled=True)

    place = pair_slots(my_routes, pair_order[0, 0], experts, capacity)
    block_ids = [
        (
            jnp.arange(owners, dtype=jnp.int32)[:, None] * (own * capacity)
            + (n * capacity + jnp.arange(capacity, dtype=jnp.int32))[None, :]
        ).reshape(-1)
        for n in range(own)
    ]
    owner_at = lax.axis_index(expert_axes)
    first = owner_at * own
    my_slots = first * capacity + jnp.arange(own * capacity, dtype=jnp.int32)
    pairs = lax.all_gather(
        jnp.stack([place[:, 0], place[:, 1], my_routes[:, 1], my_routes[:, 0]]),
        expert_axes,
        axis=0,
    )
    slot_other = (
        jnp.sum(
            jnp.where(
                pairs[:, :2, None, :] == my_slots[None, None, :, None],
                pairs[:, 2:, None, :] + 1,
                0,
            ),
            axis=(1, 3),
        )
        - 1
    ).reshape(owners, own, capacity, 1)
    to_slot = [
        ((place[None, :, 0] == ids[:, None]) | (place[None, :, 1] == ids[:, None])).astype(BF)
        for ids in block_ids
    ]
    slot_g = jnp.stack(
        [
            jnp.dot(hits, grad_low, preferred_element_type=F32)
            .astype(BF)
            .reshape(owners, capacity, width)
            for hits in to_slot
        ],
        axis=1,
    )

    inv1 = lax.rsqrt(jnp.mean(inputs * inputs, axis=-1, keepdims=True) + EPSILON)
    n1 = inputs * inv1
    normed = (n1 * attn_gain).astype(BF)
    row_start = ctx_at * rows
    query_pos = row_start + jnp.arange(rows, dtype=jnp.int32)
    inverse = 1.0 / 10000.0 ** (jnp.arange(HALF, dtype=F32) * (2.0 / HD))
    angles = inverse[:, None] * query_pos.astype(F32)[None, :]
    cos_t, sin_t = jnp.cos(angles), jnp.sin(angles)
    raw_t = jnp.einsum("dc,ld->cl", qkv_full, normed, preferred_element_type=F32)
    q_t = half_turn(raw_t[:heads_cols], cos_t, sin_t).astype(BF)
    k_t = half_turn(raw_t[heads_cols : 2 * heads_cols], cos_t, sin_t).astype(BF)
    v_t = raw_t[2 * heads_cols :].astype(BF)
    if spread:
        eout = lax.all_to_all(expert_out, "ctx", split_axis=0, concat_axis=1, tiled=True)
    else:
        eout = lax.all_gather(expert_out, "ctx", axis=1, tiled=True)
    kv_t, slot_other, slot_g, eout = tie(
        jnp.concatenate([k_t, v_t], axis=0), slot_other, slot_g, eout
    )
    before = min(ctx_count - 1, -(-(LONGEST - 1) // rows))
    shift = before * rows
    pieces = [kv_t]
    for hop in range(1, before + 1):
        links = [(i, i + hop) for i in range(ctx_count - hop)]
        pieces.insert(0, lax.ppermute(kv_t, "ctx", links))
    kv_win = jnp.concatenate(pieces, axis=1)
    k_win, v_win = kv_win[:heads_cols], kv_win[heads_cols:]

    got_g = swap(slot_g)

    starts = jnp.sum(
        seg_all[:, None] < jnp.arange(DOCS, dtype=jnp.int32)[None, :], axis=0, dtype=jnp.int32
    )
    query_seg = lax.dynamic_slice_in_dim(seg_all, row_start, rows)
    doc = jnp.sum(
        jnp.where(
            query_seg[:, None] == jnp.arange(DOCS, dtype=jnp.int32)[None, :], starts[None, :], 0
        ),
        axis=1,
    ) - (row_start - shift)
    lo = jnp.maximum(doc[::BQ], 0) // BK
    doc = doc[None, :]
    att_t, lse = attn_forward(lo, q_t, k_win, v_win, doc, shift)
    expert_in, lse, got_g = tie(expert_in, lse, got_g)
    if spread:
        ein = lax.all_to_all(expert_in, "ctx", split_axis=0, concat_axis=2, tiled=True)
    else:
        ein = lax.all_gather(expert_in, "ctx", axis=2, tiled=True)
    tensor_count = lax.axis_size("tensor")
    tensor_at = lax.axis_index("tensor")
    att_parts, out_parts = [att_t], [out_full]
    for hop in range(1, tensor_count):
        links = [(i, (i + hop) % tensor_count) for i in range(tensor_count)]
        att_parts.append(lax.ppermute(att_t, "tensor", links))
        out_parts.append(
            lax.dynamic_index_in_dim(
                out_tensor, (tensor_at - hop) % tensor_count, 0, keepdims=False
            )
        )
    branch = jnp.einsum(
        "cl,dc->ld",
        jnp.concatenate(att_parts, axis=0),
        jnp.concatenate(out_parts, axis=1),
        preferred_element_type=F32,
    )
    branch = with_layout_constraint(branch, Layout((0, 1)))
    resid = inputs + branch

    inv2 = lax.rsqrt(jnp.mean(resid * resid, axis=-1, keepdims=True) + EPSILON)
    n2 = resid * inv2
    normed2 = (n2 * ffn_gain).astype(BF)
    normed2, ein = lax.optimization_barrier((normed2, ein))

    got_x = []
    for hits in to_slot:
        sent = jnp.dot(hits, normed2, preferred_element_type=F32).astype(BF)
        if got_x:
            sent, got_x[-1] = tie(sent, got_x[-1])
        got_x.append(swap(sent.reshape(owners, 1, capacity, width)))
    shared_w = jnp.concatenate([shared_in, shared_out[None]], axis=0)
    shared_w, got_x[0] = tie(shared_w, got_x[0])
    shared_full = lax.all_gather(shared_w, DC, axis=1, tiled=True)
    router_wide = jnp.pad(router_full, ((0, 0), (0, -experts % 128)))
    ys, back_dx, g_eins, g_eouts, routers = [], [], [], [], []
    for n in range(own):
        y, dx, g_ein, g_eout, g_router = ffn(
            got_x[n],
            got_g[:, n : n + 1],
            ein[n : n + 1],
            eout[n : n + 1],
            4,
            (
                jnp.reshape(first + n, (1,)).astype(jnp.int32),
                slot_other[:, n : n + 1],
                router_wide,
            ),
        )
        ys.append(y)
        g_eins.append(g_ein)
        g_eouts.append(g_eout)
        routers.append(g_router)
        if n + 1 < own:
            dx, got_x[n + 1] = tie(dx, got_x[n + 1])
        if back_dx:
            dx, back_dx[-1] = tie(dx, back_dx[-1])
        back_dx.append(swap(dx).reshape(-1, width))
    router_part = sum(routers)[:, :experts]
    g_ein = jnp.concatenate(g_eins, axis=0)
    g_eout = jnp.concatenate(g_eouts, axis=0)

    parts = 4
    shared_shape = (parts, 1, rows // parts, width)
    sh_y, sh_dx, sh_gin, sh_gout = ffn(
        normed2.reshape(shared_shape),
        grad_low.reshape(shared_shape),
        shared_full[None, :2],
        shared_full[None, 2],
        2,
    )
    back_dx[-1], sh_dx = lax.optimization_barrier((back_dx[-1], sh_dx))

    from_slot = [
        ((place[:, 0, None] == ids[None, :]) | (place[:, 1, None] == ids[None, :])).astype(BF)
        for ids in block_ids
    ]

    def at_tokens(parts, local):
        total = local.reshape(rows, width).astype(F32)
        for hits, part in zip(from_slot, parts):
            total = total + jnp.dot(hits, part, preferred_element_type=F32)
        return total

    dn2_part = at_tokens(back_dx, sh_dx)
    dn2_low = dn2_part.astype(BF)
    ys[0], dn2_low = tie(ys[0], dn2_low)
    back_y = []
    for y in ys:
        if back_y:
            y, back_y[-1] = tie(y, back_y[-1])
        back_y.append(swap(y).reshape(-1, width))
    dn2 = lax.psum(dn2_low, "tensor")
    sh_grad, back_y[-1] = tie(jnp.concatenate([sh_gin[0], sh_gout], axis=0), back_y[-1])
    total_shared = own_sum(sh_grad, 1)
    g_eout, total_shared = tie(g_eout, total_shared)
    if spread:
        grad_eout = lax.all_to_all(g_eout, "ctx", split_axis=1, concat_axis=0, tiled=True)
    else:
        grad_eout = lax.psum_scatter(g_eout, "ctx", scatter_dimension=1, tiled=True)
    dn2, back_y[-1] = tie(dn2, back_y[-1])
    dn2 = dn2.astype(F32)
    gain2_part = jnp.sum(dn2_part * n2, axis=0)

    scaled2 = ffn_gain * dn2
    dresid = grad_layer + inv2 * (scaled2 - n2 * jnp.mean(scaled2 * n2, axis=-1, keepdims=True))
    dbranch = dresid.astype(BF)
    datt_t = jnp.einsum("dc,ld->cl", out_full, dbranch, preferred_element_type=F32).astype(BF)

    ffn_part = at_tokens(back_y, sh_y)
    ffn_low, datt_t = lax.optimization_barrier((ffn_part.astype(BF), datt_t))
    ffn_total = lax.psum(ffn_low, "tensor")

    dq_t, dk_win, dv_win = attn_backward(
        lo, q_t, k_win, v_win, att_t, datt_t, lse, doc, shift
    )
    dkv_win = jnp.concatenate([dk_win, dv_win], axis=0)
    dkv = dkv_win[:, shift:]
    for hop in range(1, before + 1):
        links = [(i + hop, i) for i in range(ctx_count - hop)]
        piece = dkv_win[:, shift - hop * rows : shift - (hop - 1) * rows]
        dkv = dkv + lax.ppermute(piece.astype(BF), "ctx", links).astype(F32)
    dq_raw = half_turn(dq_t, cos_t, -sin_t)
    dk_raw = half_turn(dkv[:heads_cols], cos_t, -sin_t)
    draw_t = jnp.concatenate([dq_raw, dk_raw, dkv[heads_cols:]], axis=0).astype(BF)
    dn1_part = jnp.einsum("cl,dc->ld", draw_t, qkv_full, preferred_element_type=F32)
    dn1_low, ffn_total = lax.optimization_barrier((dn1_part.astype(BF), ffn_total))
    layer_out = (resid + ffn_total.astype(F32)).astype(BF)
    dn1 = lax.psum(dn1_low, "tensor")
    gain1_part = jnp.sum(dn1_part * n1, axis=0)
    grad_qkv = jnp.einsum("ld,cl->dc", normed, draw_t, preferred_element_type=F32)
    grad_outw = jnp.einsum("ld,cl->dc", dbranch, att_t, preferred_element_type=F32)
    small = jnp.concatenate([router_part, gain1_part[:, None], gain2_part[:, None]], axis=1)
    mixed, grad_eout = tie(jnp.concatenate([grad_qkv, grad_outw, small], axis=1), grad_eout)
    tail = own_sum(mixed, 0)
    g_ein, tail = tie(g_ein, tail)
    small = lax.psum(tail[:, 4 * heads_cols :], "tensor")
    total_qkv = tail[:, : 3 * heads_cols].reshape(-1, 3, heads_cols).transpose(1, 0, 2)
    total_outw = tail[:, 3 * heads_cols : 4 * heads_cols]
    if spread:
        grad_ein = lax.all_to_all(g_ein, "ctx", split_axis=2, concat_axis=0, tiled=True)
    else:
        grad_ein = lax.psum_scatter(g_ein, "ctx", scatter_dimension=2, tiled=True)
    dn1, small, grad_ein = tie(dn1, small, grad_ein)
    dn1 = dn1.astype(F32)
    scaled1 = attn_gain * dn1
    grad_tokens = dresid + inv1 * (
        scaled1 - n1 * jnp.mean(scaled1 * n1, axis=-1, keepdims=True)
    )
    return (
        layer_out[None],
        grad_tokens[None],
        small[:, experts],
        total_qkv,
        total_outw,
        small[:, experts + 1],
        small[:, :experts],
        total_shared[:2],
        total_shared[2],
        grad_ein.astype(F32),
        grad_eout.astype(F32),
    )


def solution(mesh):
    return layer(mesh)


def layer(mesh):
    return jax.shard_map(
        shards,
        mesh=mesh,
        in_specs=(
            P("dp", "ctx", None),
            P("dp", None),
            P("dp", "ctx", None),
            P("dp", "ctx", None),
            P(DC),
            P(None, DC, "tensor"),
            P(DC, "tensor"),
            P(DC),
            P(DC, None),
            P(None, DC, "tensor"),
            P(DC, "tensor"),
            P("dp", None, "ctx", "tensor"),
            P("dp", "ctx", "tensor"),
            P("dp", "ctx", None),
        ),
        out_specs=(
            P("dp", "ctx", None),
            P("dp", "ctx", None),
            P(DC),
            P(None, DC, "tensor"),
            P(DC, "tensor"),
            P(DC),
            P(DC, None),
            P(None, DC, "tensor"),
            P(DC, "tensor"),
            P("dp", None, "ctx", "tensor"),
            P("dp", "ctx", "tensor"),
        ),
        check_vma=False,
    )
```

```python
import functools
import math

import jax
import jax.numpy as jnp
from jax import lax
from jax.experimental import pallas as pl
from jax.experimental.layout import Layout, with_layout_constraint
from jax.experimental.pallas import tpu as pltpu
from jax.sharding import PartitionSpec as P


HD = 64
HALF = HD // 2
EPSILON = 1e-06
LONGEST = 2000
DOCS = 5
BQ = 512
BK = 256
BF = jnp.bfloat16
F32 = jnp.float32
NEG = -1e30
DC = ("dp", "ctx")


def mm(a, b, ca, cb):
    return lax.dot_general(a, b, (((ca,), (cb,)), ((), ())), preferred_element_type=F32)


def attn_mask(key_start, query_start, doc_row):
    kpos = key_start + lax.broadcasted_iota(jnp.int32, (BK, BQ), 0)
    qpos = query_start + lax.broadcasted_iota(jnp.int32, (BK, BQ), 1)
    return (kpos <= qpos) & (kpos >= doc_row)


def attn_fwd_kernel(lo_ref, q_ref, k_ref, v_ref, doc_ref, o_ref, lse_ref, *, shift):
    cols, rows = q_ref.shape
    heads = [slice(at, at + HD) for at in range(0, cols, HD)]
    for qb in range(rows // BQ):
        here = slice(qb * BQ, (qb + 1) * BQ)
        qs = [q_ref[h, here] * 0.125 for h in heads]
        doc = doc_ref[:, here]
        q0 = shift + qb * BQ

        def step(b, carry, qs=qs, doc=doc, q0=q0):
            off = pl.multiple_of(b * BK, BK)
            mask = attn_mask(off, q0, doc)
            scores = [
                jnp.where(mask, mm(k_ref[h, pl.ds(off, BK)], q, 0, 0), NEG)
                for h, q in zip(heads, qs)
            ]
            out = []
            for h, s, (peak, total, acc) in zip(heads, scores, carry):
                new = jnp.maximum(peak, jnp.max(s, axis=0, keepdims=True))
                p = jnp.exp(s - new)
                fix = jnp.exp(peak - new)
                total = total * fix + jnp.sum(p, axis=0, keepdims=True)
                acc = acc * fix + mm(v_ref[h, pl.ds(off, BK)], p.astype(BF), 1, 0)
                out.append((new, total, acc))
            return tuple(out)

        init = tuple(
            (
                jnp.full((1, BQ), NEG, F32),
                jnp.zeros((1, BQ), F32),
                jnp.zeros((HD, BQ), F32),
            )
            for _ in heads
        )
        last = (q0 + BQ - 1) // BK
        carry = step(last, init)
        carry = lax.fori_loop(lo_ref[qb], last, step, carry)
        for n, (h, (peak, total, acc)) in enumerate(zip(heads, carry)):
            o_ref[h, here] = (acc / total).astype(BF)
            lse_ref[n : n + 1, here] = peak + jnp.log(total)


def attn_bwd_kernel(
    lo_ref, q_ref, k_ref, v_ref, o_ref, do_ref, lse_ref, doc_ref, dq_ref, dk_ref, dv_ref, *, shift
):
    cols, rows = q_ref.shape
    heads = [slice(at, at + HD) for at in range(0, cols, HD)]
    dk_ref[...] = jnp.zeros_like(dk_ref)
    dv_ref[...] = jnp.zeros_like(dv_ref)
    for qb in range(rows // BQ):
        here = slice(qb * BQ, (qb + 1) * BQ)
        qs = [q_ref[h, here] * 0.125 for h in heads]
        dos = [do_ref[h, here] for h in heads]
        doc = doc_ref[:, here]
        lses = [lse_ref[n : n + 1, here] for n in range(len(heads))]
        deltas = [
            jnp.sum(do.astype(F32) * o_ref[h, here].astype(F32), axis=0, keepdims=True)
            for h, do in zip(heads, dos)
        ]
        q0 = shift + qb * BQ

        def step(b, dqs, qs=qs, dos=dos, doc=doc, lses=lses, deltas=deltas, q0=q0):
            off = pl.multiple_of(b * BK, BK)
            keys = pl.ds(off, BK)
            mask = attn_mask(off, q0, doc)
            scores = [
                jnp.where(mask, mm(k_ref[h, keys], q, 0, 0), NEG) for h, q in zip(heads, qs)
            ]
            dps = [mm(v_ref[h, keys], do, 0, 0) for h, do in zip(heads, dos)]
            out = []
            for n, h in enumerate(heads):
                p = jnp.exp(scores[n] - lses[n])
                ds = (p * (dps[n] - deltas[n])).astype(BF)
                dk_ref[h, keys] += mm(qs[n], ds, 1, 1)
                dv_ref[h, keys] += mm(dos[n], p.astype(BF), 1, 1)
                out.append(dqs[n] + mm(k_ref[h, keys], ds, 1, 0))
            return tuple(out)

        last = (q0 + BQ - 1) // BK
        zero = tuple(jnp.zeros((HD, BQ), F32) for _ in heads)
        dqs = lax.fori_loop(lo_ref[qb], last + 1, step, zero)
        for h, dq in zip(heads, dqs):
            dq_ref[h, here] = dq * 0.125


def whole(shape):
    return pl.BlockSpec(shape, lambda n, lo: (0, 0))


def attn_forward(lo, q_t, k_t, v_t, doc, shift):
    heads, rows = q_t.shape[0] // HD, q_t.shape[1]
    ins = (q_t, k_t, v_t, doc)
    outs = (
        jax.ShapeDtypeStruct(q_t.shape, BF),
        jax.ShapeDtypeStruct((heads, rows), F32),
    )
    return pl.pallas_call(
        functools.partial(attn_fwd_kernel, shift=shift),
        out_shape=outs,
        grid_spec=pltpu.PrefetchScalarGridSpec(
            num_scalar_prefetch=1,
            grid=(1,),
            in_specs=[whole(v.shape) for v in ins],
            out_specs=[whole(v.shape) for v in outs],
        ),
        name="attn_fwd",
    )(lo, *ins)


def attn_backward(lo, q_t, k_t, v_t, o_t, do_t, lse, doc, shift):
    ins = (q_t, k_t, v_t, o_t, do_t, lse, doc)
    outs = (
        jax.ShapeDtypeStruct(q_t.shape, F32),
        jax.ShapeDtypeStruct(k_t.shape, F32),
        jax.ShapeDtypeStruct(k_t.shape, F32),
    )
    return pl.pallas_call(
        functools.partial(attn_bwd_kernel, shift=shift),
        out_shape=outs,
        grid_spec=pltpu.PrefetchScalarGridSpec(
            num_scalar_prefetch=1,
            grid=(1,),
            in_specs=[whole(v.shape) for v in ins],
            out_specs=[whole(v.shape) for v in outs],
        ),
        name="attn_bwd",
    )(lo, *ins)


def ffn_kernel(*refs, gated):
    if gated:
        first_ref, x_ref, g_ref, other_ref, router_ref, win_ref, wout_ref = refs[:7]
        y_ref, dx_ref, gin_ref, gout_ref, grouter_ref, acc_in, acc_out, acc_router = refs[7:]
    else:
        x_ref, g_ref, win_ref, wout_ref = refs[:4]
        y_ref, dx_ref, gin_ref, gout_ref, acc_in, acc_out = refs[4:]
    src, _, rows, width = x_ref.shape
    expert, step = pl.program_id(0), pl.program_id(1)

    @pl.when(step == 0)
    def _():
        acc_in[...] = jnp.zeros_like(acc_in)
        acc_out[...] = jnp.zeros_like(acc_out)

    if gated:

        @pl.when((step == 0) & (expert == 0))
        def _():
            acc_router[...] = jnp.zeros_like(acc_router)

    x = x_ref[...].reshape(src * rows, width)
    g = g_ref[...].reshape(src * rows, width)
    w_gate = win_ref[0, 0]
    w_up = win_ref[0, 1]
    w_out = wout_ref[0]
    gate_pre = mm(x, w_gate, 1, 0)
    up_pre = mm(x, w_up, 1, 0)
    sig = 1.0 / (1.0 + jnp.exp(-gate_pre))
    silu = gate_pre * sig
    hidden = (silu * up_pre).astype(BF)
    y = mm(hidden, w_out, 1, 1)
    if gated:
        router = router_ref[...]
        logits = mm(x, router, 1, 0)
        ids = lax.broadcasted_iota(jnp.int32, logits.shape, 1)
        here = ids == first_ref[0] + expert
        there = ids == other_ref[...].reshape(src * rows, 1)
        apart = jnp.sum(
            jnp.where(here, logits, 0.0) - jnp.where(there, logits, 0.0), axis=1, keepdims=True
        )
        gate = 1.0 / (1.0 + jnp.exp(-apart))
        gate_other = 1.0 / (1.0 + jnp.exp(apart))
        gf = g.astype(F32)
        dpair = gate * gate_other * jnp.sum(gf * y, axis=1, keepdims=True)
        dlogits = (jnp.where(here, dpair, 0.0) - jnp.where(there, dpair, 0.0)).astype(BF)
        acc_router[...] += mm(x, dlogits, 0, 0)
        dy = (gate * gf).astype(BF)
        y = gate * y
    else:
        dy = g
    y_ref[...] = y.astype(BF).reshape(src, 1, rows, width)
    dh = mm(dy, w_out, 1, 0)
    dgp = (dh * up_pre * (sig * (1.0 + gate_pre * (1.0 - sig)))).astype(BF)
    dup = (dh * silu).astype(BF)
    dx = mm(dgp, w_gate, 1, 1) + mm(dup, w_up, 1, 1)
    if gated:
        dx = dx + mm(dlogits, router, 1, 1)
    dx_ref[...] = dx.astype(BF).reshape(src, 1, rows, width)
    acc_in[0] += mm(x, dgp, 0, 0)
    acc_in[1] += mm(x, dup, 0, 0)
    acc_out[...] += mm(dy, hidden, 0, 0)

    @pl.when(step == pl.num_programs(1) - 1)
    def _():
        gin_ref[0] = acc_in[...].astype(BF)
        gout_ref[0] = acc_out[...].astype(BF)
        if gated:
            grouter_ref[...] = acc_router[...]


def ffn(x, g, w_in, w_out, block, routing=None, at=0):
    sources, experts, rows, width = x.shape
    units = w_out.shape[2]
    gated = routing is not None
    block = math.gcd(sources, block)
    big = pl.BlockSpec((block, 1, rows, width), lambda e, s, *_: (s, e, 0, 0))
    big_at = pl.BlockSpec((block, 1, rows, width), lambda e, s, *_: (s, at + e, 0, 0))
    w_in_at = pl.BlockSpec((1, 2, width, units), lambda e, s, *_: (at + e, 0, 0, 0))
    w_out_at = pl.BlockSpec((1, width, units), lambda e, s, *_: (at + e, 0, 0))
    w_in_spec = pl.BlockSpec((1, 2, width, units), lambda e, s, *_: (e, 0, 0, 0))
    w_out_spec = pl.BlockSpec((1, width, units), lambda e, s, *_: (e, 0, 0))
    wide = jax.ShapeDtypeStruct(x.shape, BF)
    ins = [x, g]
    in_specs = [big, big_at]
    outs = [
        wide,
        wide,
        jax.ShapeDtypeStruct((experts, 2, width, units), BF),
        jax.ShapeDtypeStruct((experts, width, units), BF),
    ]
    out_specs = [big, big, w_in_spec, w_out_spec]
    scratch = [pltpu.VMEM((2, width, units), F32), pltpu.VMEM((width, units), F32)]
    if gated:
        first, other, router = routing
        router_spec = pl.BlockSpec(router.shape, lambda e, s, *_: (0, 0))
        ins = [first] + ins + [other, router]
        thin = pl.BlockSpec((block, 1, rows, 1), lambda e, s, *_: (s, at + e, 0, 0))
        in_specs += [thin, router_spec]
        outs.append(jax.ShapeDtypeStruct(router.shape, F32))
        out_specs.append(router_spec)
        scratch.append(pltpu.VMEM(router.shape, F32))
    return pl.pallas_call(
        functools.partial(ffn_kernel, gated=gated),
        out_shape=outs,
        grid_spec=pltpu.PrefetchScalarGridSpec(
            num_scalar_prefetch=1 if gated else 0,
            grid=(experts, sources // block),
            in_specs=in_specs + [w_in_at, w_out_at],
            out_specs=out_specs,
            scratch_shapes=scratch,
        ),
        compiler_params=pltpu.CompilerParams(
            dimension_semantics=("arbitrary", "arbitrary"), vmem_limit_bytes=56 * 1024 * 1024
        ),
        name="ffn_experts" if gated else "ffn_shared",
    )(*ins, w_in, w_out)


def tie(*values):
    return lax.optimization_barrier(values)


def pair_slots(pair_route, order, experts, capacity):
    count = order.shape[0]
    flat = pair_route.reshape(count)
    number = jnp.arange(count, dtype=jnp.int32)
    ids = jnp.arange(experts, dtype=jnp.int32)
    owner = (flat[:, None] == ids[None, :]).astype(BF)
    ranked = jnp.dot(
        (order[:, None] == number[None, :]).astype(BF), owner, preferred_element_type=F32
    ).astype(BF)
    earlier = jnp.dot(
        (number[None, :] < number[:, None]).astype(BF), ranked, preferred_element_type=F32
    )
    ranked_slot = (jnp.minimum(earlier, float(capacity)) * ranked).astype(BF)
    slot = jnp.sum(
        jnp.dot(
            (order[None, :] == number[:, None]).astype(BF),
            ranked_slot,
            preferred_element_type=F32,
        ),
        axis=1,
    ).astype(jnp.int32)
    place = jnp.where(slot < capacity, flat * capacity + slot, experts * capacity)
    return place.reshape(pair_route.shape)


def own_sum(parts, axis):
    devices = lax.axis_size(DC)
    shape = parts.shape
    cut = shape[:axis] + (devices, shape[axis] // devices) + shape[axis + 1 :]
    swapped = lax.all_to_all(
        parts.astype(BF).reshape(cut), DC, split_axis=axis, concat_axis=axis, tiled=True
    )
    return jnp.sum(swapped.astype(F32), axis=axis)


def half_turn(values_t, cos_t, sin_t):
    cols, rows = values_t.shape
    split = values_t.reshape(cols // HD, 2, HALF, rows)
    a, b = split[:, 0], split[:, 1]
    return jnp.stack([a * cos_t - b * sin_t, b * cos_t + a * sin_t], axis=1).reshape(cols, rows)


def shards(
    tokens,
    segment_ids,
    routes,
    pair_order,
    gain_attn,
    qkv_weight,
    out_weight,
    gain_ffn,
    router_weight,
    shared_in,
    shared_out,
    expert_in,
    expert_out,
    out_grad,
):
    rows, width = tokens.shape[1], tokens.shape[2]
    ctx_count = lax.axis_size("ctx")
    ctx_at = lax.axis_index("ctx")
    inputs = tokens[0].astype(F32)
    grad_low = out_grad[0]
    grad_layer = grad_low.astype(F32)
    seg_all = segment_ids[0]
    my_routes = routes[0]

    heads_cols = qkv_weight.shape[2]
    qkv_cols = 3 * heads_cols
    experts = router_weight.shape[1]
    thin = jnp.concatenate(
        [
            qkv_weight.transpose(1, 0, 2).reshape(-1, qkv_cols),
            out_weight,
            router_weight,
            gain_attn[:, None],
            gain_ffn[:, None],
        ],
        axis=1,
    )
    thin_full = lax.all_gather(thin, DC, axis=0, tiled=True)
    qkv_full = thin_full[:, :qkv_cols]
    out_full = thin_full[:, qkv_cols : qkv_cols + heads_cols]
    out_tensor = lax.all_gather(out_full, "tensor", axis=0)
    router_full = thin_full[:, qkv_cols + heads_cols : qkv_cols + heads_cols + experts]
    attn_gain = thin_full[:, -2].astype(F32)
    ffn_gain = thin_full[:, -1].astype(F32)

    local_experts = expert_in.shape[0]
    spread = local_experts % ctx_count == 0
    expert_axes = DC if spread else ("dp",)
    owners = lax.axis_size(expert_axes)
    own = experts // owners
    capacity = 10 * rows // (4 * experts)

    def swap(values):
        return lax.all_to_all(values, expert_axes, split_axis=0, concat_axis=0, tiled=True)

    place = pair_slots(my_routes, pair_order[0, 0], experts, capacity)
    block_ids = [
        (
            jnp.arange(owners, dtype=jnp.int32)[:, None] * (own * capacity)
            + (n * capacity + jnp.arange(capacity, dtype=jnp.int32))[None, :]
        ).reshape(-1)
        for n in range(own)
    ]
    owner_at = lax.axis_index(expert_axes)
    first = owner_at * own
    my_slots = first * capacity + jnp.arange(own * capacity, dtype=jnp.int32)
    pairs = lax.all_gather(
        jnp.stack([place[:, 0], place[:, 1], my_routes[:, 1], my_routes[:, 0]]),
        expert_axes,
        axis=0,
    )
    slot_other = (
        jnp.sum(
            jnp.where(
                pairs[:, :2, None, :] == my_slots[None, None, :, None],
                pairs[:, 2:, None, :] + 1,
                0,
            ),
            axis=(1, 3),
        )
        - 1
    ).reshape(owners, own, capacity, 1)
    to_slot = [
        ((place[None, :, 0] == ids[:, None]) | (place[None, :, 1] == ids[:, None])).astype(BF)
        for ids in block_ids
    ]
    slot_g = jnp.stack(
        [
            jnp.dot(hits, grad_low, preferred_element_type=F32)
            .astype(BF)
            .reshape(owners, capacity, width)
            for hits in to_slot
        ],
        axis=1,
    )

    inv1 = lax.rsqrt(jnp.mean(inputs * inputs, axis=-1, keepdims=True) + EPSILON)
    n1 = inputs * inv1
    normed = (n1 * attn_gain).astype(BF)
    row_start = ctx_at * rows
    query_pos = row_start + jnp.arange(rows, dtype=jnp.int32)
    inverse = 1.0 / 10000.0 ** (jnp.arange(HALF, dtype=F32) * (2.0 / HD))
    angles = inverse[:, None] * query_pos.astype(F32)[None, :]
    cos_t, sin_t = jnp.cos(angles), jnp.sin(angles)
    raw_t = jnp.einsum("dc,ld->cl", qkv_full, normed, preferred_element_type=F32)
    q_t = half_turn(raw_t[:heads_cols], cos_t, sin_t).astype(BF)
    k_t = half_turn(raw_t[heads_cols : 2 * heads_cols], cos_t, sin_t).astype(BF)
    v_t = raw_t[2 * heads_cols :].astype(BF)
    if spread:
        eout = lax.all_to_all(expert_out, "ctx", split_axis=0, concat_axis=1, tiled=True)
    else:
        eout = lax.all_gather(expert_out, "ctx", axis=1, tiled=True)
    kv_t, slot_other, eout = tie(jnp.concatenate([k_t, v_t], axis=0), slot_other, eout)
    before = min(ctx_count - 1, -(-(LONGEST - 1) // rows))
    shift = before * rows
    pieces = [kv_t]
    for hop in range(1, before + 1):
        links = [(i, i + hop) for i in range(ctx_count - hop)]
        pieces.insert(0, lax.ppermute(kv_t, "ctx", links))
    kv_win = jnp.concatenate(pieces, axis=1)
    kv_win, slot_g = tie(kv_win, slot_g)
    k_win, v_win = kv_win[:heads_cols], kv_win[heads_cols:]

    got_g = swap(slot_g)

    starts = jnp.sum(
        seg_all[:, None] < jnp.arange(DOCS, dtype=jnp.int32)[None, :], axis=0, dtype=jnp.int32
    )
    query_seg = lax.dynamic_slice_in_dim(seg_all, row_start, rows)
    doc = jnp.sum(
        jnp.where(
            query_seg[:, None] == jnp.arange(DOCS, dtype=jnp.int32)[None, :], starts[None, :], 0
        ),
        axis=1,
    ) - (row_start - shift)
    lo = jnp.maximum(doc[::BQ], 0) // BK
    doc = doc[None, :]
    att_t, lse = attn_forward(lo, q_t, k_win, v_win, doc, shift)
    expert_in, lse, got_g = tie(expert_in, lse, got_g)
    if spread:
        ein = lax.all_to_all(expert_in, "ctx", split_axis=0, concat_axis=2, tiled=True)
    else:
        ein = lax.all_gather(expert_in, "ctx", axis=2, tiled=True)
    tensor_count = lax.axis_size("tensor")
    tensor_at = lax.axis_index("tensor")
    att_parts, out_parts = [att_t], [out_full]
    for hop in range(1, tensor_count):
        links = [(i, (i + hop) % tensor_count) for i in range(tensor_count)]
        att_parts.append(lax.ppermute(att_t, "tensor", links))
        out_parts.append(
            lax.dynamic_index_in_dim(
                out_tensor, (tensor_at - hop) % tensor_count, 0, keepdims=False
            )
        )
    branch = jnp.einsum(
        "cl,dc->ld",
        jnp.concatenate(att_parts, axis=0),
        jnp.concatenate(out_parts, axis=1),
        preferred_element_type=F32,
    )
    branch = with_layout_constraint(branch, Layout((0, 1)))
    resid = inputs + branch

    inv2 = lax.rsqrt(jnp.mean(resid * resid, axis=-1, keepdims=True) + EPSILON)
    n2 = resid * inv2
    normed2 = (n2 * ffn_gain).astype(BF)
    normed2, ein = lax.optimization_barrier((normed2, ein))

    got_x = []
    for hits in to_slot:
        sent = jnp.dot(hits, normed2, preferred_element_type=F32).astype(BF)
        if got_x:
            sent, got_x[-1] = tie(sent, got_x[-1])
        got_x.append(swap(sent.reshape(owners, 1, capacity, width)))
    shared_w = jnp.concatenate([shared_in, shared_out[None]], axis=0)
    shared_w, got_x[0] = tie(shared_w, got_x[0])
    shared_full = lax.all_gather(shared_w, DC, axis=1, tiled=True)
    router_wide = jnp.pad(router_full, ((0, 0), (0, -experts % 128)))
    ys, back_dx, g_eins, g_eouts, routers = [], [], [], [], []
    for n in range(own):
        y, dx, g_ein, g_eout, g_router = ffn(
            got_x[n],
            got_g,
            ein,
            eout,
            4,
            (jnp.reshape(first + n, (1,)).astype(jnp.int32), slot_other, router_wide),
            n,
        )
        ys.append(y)
        g_eins.append(g_ein)
        g_eouts.append(g_eout)
        routers.append(g_router)
        if n + 1 < own:
            dx, got_x[n + 1] = tie(dx, got_x[n + 1])
        if back_dx:
            dx, back_dx[-1] = tie(dx, back_dx[-1])
        back_dx.append(swap(dx).reshape(-1, width))
    router_part = sum(routers)[:, :experts]
    g_ein = jnp.concatenate(g_eins, axis=0)
    g_eout = jnp.concatenate(g_eouts, axis=0)

    parts = 4
    shared_shape = (parts, 1, rows // parts, width)
    sh_y, sh_dx, sh_gin, sh_gout = ffn(
        normed2.reshape(shared_shape),
        grad_low.reshape(shared_shape),
        shared_full[None, :2],
        shared_full[None, 2],
        2,
    )
    back_dx[-1], sh_dx = lax.optimization_barrier((back_dx[-1], sh_dx))

    from_slot = [
        ((place[:, 0, None] == ids[None, :]) | (place[:, 1, None] == ids[None, :])).astype(BF)
        for ids in block_ids
    ]

    def at_tokens(parts, local):
        total = local.reshape(rows, width).astype(F32)
        for hits, part in zip(from_slot, parts):
            total = total + jnp.dot(hits, part, preferred_element_type=F32)
        return total

    dn2_part = at_tokens(back_dx, sh_dx)
    dn2_low = dn2_part.astype(BF)
    ys[0], dn2_low = tie(ys[0], dn2_low)
    back_y = []
    for y in ys:
        if back_y:
            y, back_y[-1] = tie(y, back_y[-1])
        back_y.append(swap(y).reshape(-1, width))
    dn2 = lax.psum(dn2_low, "tensor")
    sh_grad, back_y[-1] = tie(jnp.concatenate([sh_gin[0], sh_gout], axis=0), back_y[-1])
    total_shared = own_sum(sh_grad, 1)
    dn2, back_y[-1] = tie(dn2, back_y[-1])
    dn2 = dn2.astype(F32)
    gain2_part = jnp.sum(dn2_part * n2, axis=0)

    scaled2 = ffn_gain * dn2
    dresid = grad_layer + inv2 * (scaled2 - n2 * jnp.mean(scaled2 * n2, axis=-1, keepdims=True))
    dbranch = dresid.astype(BF)
    datt_t = jnp.einsum("dc,ld->cl", out_full, dbranch, preferred_element_type=F32).astype(BF)

    ffn_part = at_tokens(back_y, sh_y)
    ffn_low, datt_t = lax.optimization_barrier((ffn_part.astype(BF), datt_t))
    ffn_total = lax.psum(ffn_low, "tensor")

    dq_t, dk_win, dv_win = attn_backward(
        lo, q_t, k_win, v_win, att_t, datt_t, lse, doc, shift
    )
    dkv_win = jnp.concatenate([dk_win, dv_win], axis=0)
    dkv = dkv_win[:, shift:]
    for hop in range(1, before + 1):
        links = [(i + hop, i) for i in range(ctx_count - hop)]
        piece = dkv_win[:, shift - hop * rows : shift - (hop - 1) * rows]
        dkv = dkv + lax.ppermute(piece.astype(BF), "ctx", links).astype(F32)
    dq_raw = half_turn(dq_t, cos_t, -sin_t)
    dk_raw = half_turn(dkv[:heads_cols], cos_t, -sin_t)
    draw_t = jnp.concatenate([dq_raw, dk_raw, dkv[heads_cols:]], axis=0).astype(BF)
    g_eout, draw_t, total_shared = tie(g_eout, draw_t, total_shared)
    if spread:
        grad_eout = lax.all_to_all(g_eout, "ctx", split_axis=1, concat_axis=0, tiled=True)
    else:
        grad_eout = lax.psum_scatter(g_eout, "ctx", scatter_dimension=1, tiled=True)
    dn1_part = jnp.einsum("cl,dc->ld", draw_t, qkv_full, preferred_element_type=F32)
    dn1_low, ffn_total = lax.optimization_barrier((dn1_part.astype(BF), ffn_total))
    layer_out = (resid + ffn_total.astype(F32)).astype(BF)
    dn1 = lax.psum(dn1_low, "tensor")
    gain1_part = jnp.sum(dn1_part * n1, axis=0)
    grad_qkv = jnp.einsum("ld,cl->dc", normed, draw_t, preferred_element_type=F32)
    grad_outw = jnp.einsum("ld,cl->dc", dbranch, att_t, preferred_element_type=F32)
    small = jnp.concatenate([router_part, gain1_part[:, None], gain2_part[:, None]], axis=1)
    mixed, grad_eout = tie(jnp.concatenate([grad_qkv, grad_outw, small], axis=1), grad_eout)
    tail = own_sum(mixed, 0)
    g_ein, tail = tie(g_ein, tail)
    small = lax.psum(tail[:, 4 * heads_cols :], "tensor")
    total_qkv = tail[:, : 3 * heads_cols].reshape(-1, 3, heads_cols).transpose(1, 0, 2)
    total_outw = tail[:, 3 * heads_cols : 4 * heads_cols]
    if spread:
        grad_ein = lax.all_to_all(g_ein, "ctx", split_axis=2, concat_axis=0, tiled=True)
    else:
        grad_ein = lax.psum_scatter(g_ein, "ctx", scatter_dimension=2, tiled=True)
    dn1, small, grad_ein = tie(dn1, small, grad_ein)
    dn1 = dn1.astype(F32)
    scaled1 = attn_gain * dn1
    grad_tokens = dresid + inv1 * (
        scaled1 - n1 * jnp.mean(scaled1 * n1, axis=-1, keepdims=True)
    )
    return (
        layer_out[None],
        grad_tokens[None],
        small[:, experts],
        total_qkv,
        total_outw,
        small[:, experts + 1],
        small[:, :experts],
        total_shared[:2],
        total_shared[2],
        grad_ein.astype(F32),
        grad_eout.astype(F32),
    )


def solution(mesh):
    return layer(mesh)


def layer(mesh):
    return jax.shard_map(
        shards,
        mesh=mesh,
        in_specs=(
            P("dp", "ctx", None),
            P("dp", None),
            P("dp", "ctx", None),
            P("dp", "ctx", None),
            P(DC),
            P(None, DC, "tensor"),
            P(DC, "tensor"),
            P(DC),
            P(DC, None),
            P(None, DC, "tensor"),
            P(DC, "tensor"),
            P("dp", None, "ctx", "tensor"),
            P("dp", "ctx", "tensor"),
            P("dp", "ctx", None),
        ),
        out_specs=(
            P("dp", "ctx", None),
            P("dp", "ctx", None),
            P(DC),
            P(None, DC, "tensor"),
            P(DC, "tensor"),
            P(DC),
            P(DC, None),
            P(None, DC, "tensor"),
            P(DC, "tensor"),
            P("dp", None, "ctx", "tensor"),
            P("dp", "ctx", "tensor"),
        ),
        check_vma=False,
    )
```

```python
import functools
import math

import jax
import jax.numpy as jnp
from jax import lax
from jax.experimental import pallas as pl
from jax.experimental.layout import Layout, with_layout_constraint
from jax.experimental.pallas import tpu as pltpu
from jax.sharding import PartitionSpec as P


HD = 64
HALF = HD // 2
EPSILON = 1e-06
LONGEST = 2000
DOCS = 5
BQ = 512
BK = 256
BF = jnp.bfloat16
F32 = jnp.float32
NEG = -1e30
DC = ("dp", "ctx")


def mm(a, b, ca, cb):
    return lax.dot_general(a, b, (((ca,), (cb,)), ((), ())), preferred_element_type=F32)


def attn_mask(key_start, query_start, doc_row):
    kpos = key_start + lax.broadcasted_iota(jnp.int32, (BK, BQ), 0)
    qpos = query_start + lax.broadcasted_iota(jnp.int32, (BK, BQ), 1)
    return (kpos <= qpos) & (kpos >= doc_row)


def attn_fwd_kernel(lo_ref, q_ref, k_ref, v_ref, doc_ref, o_ref, lse_ref, *, shift):
    cols, rows = q_ref.shape
    heads = [slice(at, at + HD) for at in range(0, cols, HD)]
    for qb in range(rows // BQ):
        here = slice(qb * BQ, (qb + 1) * BQ)
        qs = [q_ref[h, here] * 0.125 for h in heads]
        doc = doc_ref[:, here]
        q0 = shift + qb * BQ

        def step(b, carry, qs=qs, doc=doc, q0=q0):
            off = pl.multiple_of(b * BK, BK)
            mask = attn_mask(off, q0, doc)
            scores = [
                jnp.where(mask, mm(k_ref[h, pl.ds(off, BK)], q, 0, 0), NEG)
                for h, q in zip(heads, qs)
            ]
            out = []
            for h, s, (peak, total, acc) in zip(heads, scores, carry):
                new = jnp.maximum(peak, jnp.max(s, axis=0, keepdims=True))
                p = jnp.exp(s - new)
                fix = jnp.exp(peak - new)
                total = total * fix + jnp.sum(p, axis=0, keepdims=True)
                acc = acc * fix + mm(v_ref[h, pl.ds(off, BK)], p.astype(BF), 1, 0)
                out.append((new, total, acc))
            return tuple(out)

        init = tuple(
            (
                jnp.full((1, BQ), NEG, F32),
                jnp.zeros((1, BQ), F32),
                jnp.zeros((HD, BQ), F32),
            )
            for _ in heads
        )
        last = (q0 + BQ - 1) // BK
        carry = step(last, init)
        carry = lax.fori_loop(lo_ref[qb], last, step, carry)
        for n, (h, (peak, total, acc)) in enumerate(zip(heads, carry)):
            o_ref[h, here] = (acc / total).astype(BF)
            lse_ref[n : n + 1, here] = peak + jnp.log(total)


def attn_bwd_kernel(
    lo_ref, q_ref, k_ref, v_ref, o_ref, do_ref, lse_ref, doc_ref, dq_ref, dk_ref, dv_ref, *, shift
):
    cols, rows = q_ref.shape
    heads = [slice(at, at + HD) for at in range(0, cols, HD)]
    dk_ref[...] = jnp.zeros_like(dk_ref)
    dv_ref[...] = jnp.zeros_like(dv_ref)
    for qb in range(rows // BQ):
        here = slice(qb * BQ, (qb + 1) * BQ)
        qs = [q_ref[h, here] * 0.125 for h in heads]
        dos = [do_ref[h, here] for h in heads]
        doc = doc_ref[:, here]
        lses = [lse_ref[n : n + 1, here] for n in range(len(heads))]
        deltas = [
            jnp.sum(do.astype(F32) * o_ref[h, here].astype(F32), axis=0, keepdims=True)
            for h, do in zip(heads, dos)
        ]
        q0 = shift + qb * BQ

        def step(b, dqs, qs=qs, dos=dos, doc=doc, lses=lses, deltas=deltas, q0=q0):
            off = pl.multiple_of(b * BK, BK)
            keys = pl.ds(off, BK)
            mask = attn_mask(off, q0, doc)
            scores = [
                jnp.where(mask, mm(k_ref[h, keys], q, 0, 0), NEG) for h, q in zip(heads, qs)
            ]
            dps = [mm(v_ref[h, keys], do, 0, 0) for h, do in zip(heads, dos)]
            out = []
            for n, h in enumerate(heads):
                p = jnp.exp(scores[n] - lses[n])
                ds = (p * (dps[n] - deltas[n])).astype(BF)
                dk_ref[h, keys] += mm(qs[n], ds, 1, 1)
                dv_ref[h, keys] += mm(dos[n], p.astype(BF), 1, 1)
                out.append(dqs[n] + mm(k_ref[h, keys], ds, 1, 0))
            return tuple(out)

        last = (q0 + BQ - 1) // BK
        zero = tuple(jnp.zeros((HD, BQ), F32) for _ in heads)
        dqs = lax.fori_loop(lo_ref[qb], last + 1, step, zero)
        for h, dq in zip(heads, dqs):
            dq_ref[h, here] = dq * 0.125


def whole(shape):
    return pl.BlockSpec(shape, lambda n, lo: (0, 0))


def attn_forward(lo, q_t, k_t, v_t, doc, shift):
    heads, rows = q_t.shape[0] // HD, q_t.shape[1]
    ins = (q_t, k_t, v_t, doc)
    outs = (
        jax.ShapeDtypeStruct(q_t.shape, BF),
        jax.ShapeDtypeStruct((heads, rows), F32),
    )
    return pl.pallas_call(
        functools.partial(attn_fwd_kernel, shift=shift),
        out_shape=outs,
        grid_spec=pltpu.PrefetchScalarGridSpec(
            num_scalar_prefetch=1,
            grid=(1,),
            in_specs=[whole(v.shape) for v in ins],
            out_specs=[whole(v.shape) for v in outs],
        ),
        name="attn_fwd",
    )(lo, *ins)


def attn_backward(lo, q_t, k_t, v_t, o_t, do_t, lse, doc, shift):
    ins = (q_t, k_t, v_t, o_t, do_t, lse, doc)
    outs = (
        jax.ShapeDtypeStruct(q_t.shape, F32),
        jax.ShapeDtypeStruct(k_t.shape, F32),
        jax.ShapeDtypeStruct(k_t.shape, F32),
    )
    return pl.pallas_call(
        functools.partial(attn_bwd_kernel, shift=shift),
        out_shape=outs,
        grid_spec=pltpu.PrefetchScalarGridSpec(
            num_scalar_prefetch=1,
            grid=(1,),
            in_specs=[whole(v.shape) for v in ins],
            out_specs=[whole(v.shape) for v in outs],
        ),
        name="attn_bwd",
    )(lo, *ins)


def ffn_kernel(*refs, gated):
    if gated:
        first_ref, x_ref, g_ref, other_ref, router_ref, win_ref, wout_ref = refs[:7]
        y_ref, dx_ref, gin_ref, gout_ref, grouter_ref, acc_in, acc_out, acc_router = refs[7:]
    else:
        x_ref, g_ref, win_ref, wout_ref = refs[:4]
        y_ref, dx_ref, gin_ref, gout_ref, acc_in, acc_out = refs[4:]
    src, _, rows, width = x_ref.shape
    expert, step = pl.program_id(0), pl.program_id(1)

    @pl.when(step == 0)
    def _():
        acc_in[...] = jnp.zeros_like(acc_in)
        acc_out[...] = jnp.zeros_like(acc_out)

    if gated:

        @pl.when((step == 0) & (expert == 0))
        def _():
            acc_router[...] = jnp.zeros_like(acc_router)

    x = x_ref[...].reshape(src * rows, width)
    g = g_ref[...].reshape(src * rows, width)
    w_gate = win_ref[0, 0]
    w_up = win_ref[0, 1]
    w_out = wout_ref[0]
    gate_pre = mm(x, w_gate, 1, 0)
    up_pre = mm(x, w_up, 1, 0)
    sig = 1.0 / (1.0 + jnp.exp(-gate_pre))
    silu = gate_pre * sig
    hidden = (silu * up_pre).astype(BF)
    y = mm(hidden, w_out, 1, 1)
    if gated:
        router = router_ref[...]
        logits = mm(x, router, 1, 0)
        ids = lax.broadcasted_iota(jnp.int32, logits.shape, 1)
        here = ids == first_ref[0] + expert
        there = ids == other_ref[...].reshape(src * rows, 1)
        apart = jnp.sum(
            jnp.where(here, logits, 0.0) - jnp.where(there, logits, 0.0), axis=1, keepdims=True
        )
        gate = 1.0 / (1.0 + jnp.exp(-apart))
        gate_other = 1.0 / (1.0 + jnp.exp(apart))
        gf = g.astype(F32)
        dpair = gate * gate_other * jnp.sum(gf * y, axis=1, keepdims=True)
        dlogits = (jnp.where(here, dpair, 0.0) - jnp.where(there, dpair, 0.0)).astype(BF)
        acc_router[...] += mm(x, dlogits, 0, 0)
        dy = (gate * gf).astype(BF)
        y = gate * y
    else:
        dy = g
    y_ref[...] = y.astype(BF).reshape(src, 1, rows, width)
    dh = mm(dy, w_out, 1, 0)
    dgp = (dh * up_pre * (sig * (1.0 + gate_pre * (1.0 - sig)))).astype(BF)
    dup = (dh * silu).astype(BF)
    dx = mm(dgp, w_gate, 1, 1) + mm(dup, w_up, 1, 1)
    if gated:
        dx = dx + mm(dlogits, router, 1, 1)
    dx_ref[...] = dx.astype(BF).reshape(src, 1, rows, width)
    acc_in[0] += mm(x, dgp, 0, 0)
    acc_in[1] += mm(x, dup, 0, 0)
    acc_out[...] += mm(dy, hidden, 0, 0)

    @pl.when(step == pl.num_programs(1) - 1)
    def _():
        cut = gin_ref.shape[3]
        for n in range(gin_ref.shape[0]):
            gin_ref[n, 0] = acc_in[:, n * cut : (n + 1) * cut].astype(BF)
            gout_ref[n, 0] = acc_out[n * cut : (n + 1) * cut].astype(BF)
        if gated:
            grouter_ref[...] = acc_router[...]


def ffn(x, g, w_in, w_out, block, parts, routing=None, at=0):
    sources, experts, rows, width = x.shape
    units = w_out.shape[2]
    gated = routing is not None
    block = math.gcd(sources, block)
    big = pl.BlockSpec((block, 1, rows, width), lambda e, s, *_: (s, e, 0, 0))
    big_at = pl.BlockSpec((block, 1, rows, width), lambda e, s, *_: (s, at + e, 0, 0))
    w_in_at = pl.BlockSpec((1, 2, width, units), lambda e, s, *_: (at + e, 0, 0, 0))
    w_out_at = pl.BlockSpec((1, width, units), lambda e, s, *_: (at + e, 0, 0))
    cut = width // parts
    g_in_spec = pl.BlockSpec((parts, 1, 2, cut, units), lambda e, s, *_: (0, e, 0, 0, 0))
    g_out_spec = pl.BlockSpec((parts, 1, cut, units), lambda e, s, *_: (0, e, 0, 0))
    wide = jax.ShapeDtypeStruct(x.shape, BF)
    ins = [x, g]
    in_specs = [big, big_at]
    outs = [
        wide,
        wide,
        jax.ShapeDtypeStruct((parts, experts, 2, cut, units), BF),
        jax.ShapeDtypeStruct((parts, experts, cut, units), BF),
    ]
    out_specs = [big, big, g_in_spec, g_out_spec]
    scratch = [pltpu.VMEM((2, width, units), F32), pltpu.VMEM((width, units), F32)]
    if gated:
        first, other, router = routing
        router_spec = pl.BlockSpec(router.shape, lambda e, s, *_: (0, 0))
        ins = [first] + ins + [other, router]
        thin = pl.BlockSpec((block, 1, rows, 1), lambda e, s, *_: (s, at + e, 0, 0))
        in_specs += [thin, router_spec]
        outs.append(jax.ShapeDtypeStruct(router.shape, F32))
        out_specs.append(router_spec)
        scratch.append(pltpu.VMEM(router.shape, F32))
    return pl.pallas_call(
        functools.partial(ffn_kernel, gated=gated),
        out_shape=outs,
        grid_spec=pltpu.PrefetchScalarGridSpec(
            num_scalar_prefetch=1 if gated else 0,
            grid=(experts, sources // block),
            in_specs=in_specs + [w_in_at, w_out_at],
            out_specs=out_specs,
            scratch_shapes=scratch,
        ),
        compiler_params=pltpu.CompilerParams(
            dimension_semantics=("arbitrary", "arbitrary"), vmem_limit_bytes=56 * 1024 * 1024
        ),
        name="ffn_experts" if gated else "ffn_shared",
    )(*ins, w_in, w_out)


def tie(*values):
    return lax.optimization_barrier(values)


def pair_slots(pair_route, order, experts, capacity):
    count = order.shape[0]
    flat = pair_route.reshape(count)
    number = jnp.arange(count, dtype=jnp.int32)
    ids = jnp.arange(experts, dtype=jnp.int32)
    owner = (flat[:, None] == ids[None, :]).astype(BF)
    ranked = jnp.dot(
        (order[:, None] == number[None, :]).astype(BF), owner, preferred_element_type=F32
    ).astype(BF)
    earlier = jnp.dot(
        (number[None, :] < number[:, None]).astype(BF), ranked, preferred_element_type=F32
    )
    ranked_slot = (jnp.minimum(earlier, float(capacity)) * ranked).astype(BF)
    slot = jnp.sum(
        jnp.dot(
            (order[None, :] == number[:, None]).astype(BF),
            ranked_slot,
            preferred_element_type=F32,
        ),
        axis=1,
    ).astype(jnp.int32)
    place = jnp.where(slot < capacity, flat * capacity + slot, experts * capacity)
    return place.reshape(pair_route.shape)


def own_sum(parts, axis):
    devices = lax.axis_size(DC)
    shape = parts.shape
    cut = shape[:axis] + (devices, shape[axis] // devices) + shape[axis + 1 :]
    swapped = lax.all_to_all(
        parts.astype(BF).reshape(cut), DC, split_axis=axis, concat_axis=axis, tiled=True
    )
    return jnp.sum(swapped.astype(F32), axis=axis)


def half_turn(values_t, cos_t, sin_t):
    cols, rows = values_t.shape
    split = values_t.reshape(cols // HD, 2, HALF, rows)
    a, b = split[:, 0], split[:, 1]
    return jnp.stack([a * cos_t - b * sin_t, b * cos_t + a * sin_t], axis=1).reshape(cols, rows)


def shards(
    tokens,
    segment_ids,
    routes,
    pair_order,
    gain_attn,
    qkv_weight,
    out_weight,
    gain_ffn,
    router_weight,
    shared_in,
    shared_out,
    expert_in,
    expert_out,
    out_grad,
):
    rows, width = tokens.shape[1], tokens.shape[2]
    ctx_count = lax.axis_size("ctx")
    ctx_at = lax.axis_index("ctx")
    inputs = tokens[0].astype(F32)
    grad_low = out_grad[0]
    grad_layer = grad_low.astype(F32)
    seg_all = segment_ids[0]
    my_routes = routes[0]

    heads_cols = qkv_weight.shape[2]
    qkv_cols = 3 * heads_cols
    experts = router_weight.shape[1]
    tensor_count = lax.axis_size("tensor")
    first_w = jnp.concatenate(
        [qkv_weight.transpose(1, 0, 2).reshape(-1, qkv_cols), gain_attn[:, None]], axis=1
    )
    first_full = lax.all_gather(first_w, DC, axis=0, tiled=True)
    qkv_full = first_full[:, :qkv_cols]
    attn_gain = first_full[:, qkv_cols].astype(F32)
    rings = [
        [(i, (i + hop) % tensor_count) for i in range(tensor_count)]
        for hop in range(1, tensor_count)
    ]
    second_w = jnp.concatenate(
        [out_weight]
        + [lax.ppermute(out_weight, "tensor", links) for links in rings]
        + [router_weight, gain_ffn[:, None]],
        axis=1,
    )

    local_experts = expert_in.shape[0]
    spread = local_experts % ctx_count == 0
    expert_axes = DC if spread else ("dp",)
    owners = lax.axis_size(expert_axes)
    own = experts // owners
    capacity = 10 * rows // (4 * experts)

    def swap(values):
        return lax.all_to_all(values, expert_axes, split_axis=0, concat_axis=0, tiled=True)

    place = pair_slots(my_routes, pair_order[0, 0], experts, capacity)
    block_ids = [
        (
            jnp.arange(owners, dtype=jnp.int32)[:, None] * (own * capacity)
            + (n * capacity + jnp.arange(capacity, dtype=jnp.int32))[None, :]
        ).reshape(-1)
        for n in range(own)
    ]
    first = lax.axis_index(expert_axes) * own
    my_slots = first * capacity + jnp.arange(own * capacity, dtype=jnp.int32)
    to_slot = [
        ((place[None, :, 0] == ids[:, None]) | (place[None, :, 1] == ids[:, None])).astype(BF)
        for ids in block_ids
    ]
    slot_g = jnp.stack(
        [
            jnp.dot(hits, grad_low, preferred_element_type=F32)
            .astype(BF)
            .reshape(owners, capacity, width)
            for hits in to_slot
        ],
        axis=1,
    )

    inv1 = lax.rsqrt(jnp.mean(inputs * inputs, axis=-1, keepdims=True) + EPSILON)
    n1 = inputs * inv1
    normed = (n1 * attn_gain).astype(BF)
    row_start = ctx_at * rows
    query_pos = row_start + jnp.arange(rows, dtype=jnp.int32)
    inverse = 1.0 / 10000.0 ** (jnp.arange(HALF, dtype=F32) * (2.0 / HD))
    angles = inverse[:, None] * query_pos.astype(F32)[None, :]
    cos_t, sin_t = jnp.cos(angles), jnp.sin(angles)
    expert_out, qkv_full = tie(expert_out, qkv_full)
    if spread:
        eout = lax.all_to_all(expert_out, "ctx", split_axis=0, concat_axis=1, tiled=True)
    else:
        eout = lax.all_gather(expert_out, "ctx", axis=1, tiled=True)
    raw_t = jnp.einsum("dc,ld->cl", qkv_full, normed, preferred_element_type=F32)
    q_t = half_turn(raw_t[:heads_cols], cos_t, sin_t).astype(BF)
    k_t = half_turn(raw_t[heads_cols : 2 * heads_cols], cos_t, sin_t).astype(BF)
    v_t = raw_t[2 * heads_cols :].astype(BF)
    kv_t = jnp.concatenate([k_t, v_t], axis=0)
    before = min(ctx_count - 1, -(-(LONGEST - 1) // rows))
    shift = before * rows
    pieces = [kv_t]
    for hop in range(1, before + 1):
        links = [(i, i + hop) for i in range(ctx_count - hop)]
        pieces.insert(0, lax.ppermute(kv_t, "ctx", links))
    kv_win = jnp.concatenate(pieces, axis=1)
    kv_win, slot_g, second_w, eout = tie(kv_win, slot_g, second_w, eout)
    k_win, v_win = kv_win[:heads_cols], kv_win[heads_cols:]

    got_g = swap(slot_g)
    second_full = lax.all_gather(second_w, DC, axis=0, tiled=True)
    out_all = second_full[:, : tensor_count * heads_cols]
    out_full = out_all[:, :heads_cols]
    router_full = second_full[:, tensor_count * heads_cols : -1]
    ffn_gain = second_full[:, -1].astype(F32)

    starts = jnp.sum(
        seg_all[:, None] < jnp.arange(DOCS, dtype=jnp.int32)[None, :], axis=0, dtype=jnp.int32
    )
    query_seg = lax.dynamic_slice_in_dim(seg_all, row_start, rows)
    doc = jnp.sum(
        jnp.where(
            query_seg[:, None] == jnp.arange(DOCS, dtype=jnp.int32)[None, :], starts[None, :], 0
        ),
        axis=1,
    ) - (row_start - shift)
    lo = jnp.maximum(doc[::BQ], 0) // BK
    doc = doc[None, :]
    att_t, lse = attn_forward(lo, q_t, k_win, v_win, doc, shift)
    place, expert_in, lse, got_g = tie(place, expert_in, lse, got_g)
    if spread:
        ein = lax.all_to_all(expert_in, "ctx", split_axis=0, concat_axis=2, tiled=True)
    else:
        ein = lax.all_gather(expert_in, "ctx", axis=2, tiled=True)
    pairs = lax.all_gather(
        jnp.stack([place[:, 0], place[:, 1], my_routes[:, 1], my_routes[:, 0]]),
        expert_axes,
        axis=0,
    )
    slot_other = (
        jnp.sum(
            jnp.where(
                pairs[:, :2, None, :] == my_slots[None, None, :, None],
                pairs[:, 2:, None, :] + 1,
                0,
            ),
            axis=(1, 3),
        )
        - 1
    ).reshape(owners, own, capacity, 1)
    att_parts = [att_t] + [lax.ppermute(att_t, "tensor", links) for links in rings]
    att_parts[-1], slot_other = tie(att_parts[-1], slot_other)
    branch = jnp.einsum(
        "cl,dc->ld", jnp.concatenate(att_parts, axis=0), out_all, preferred_element_type=F32
    )
    branch = with_layout_constraint(branch, Layout((0, 1)))
    resid = inputs + branch

    inv2 = lax.rsqrt(jnp.mean(resid * resid, axis=-1, keepdims=True) + EPSILON)
    n2 = resid * inv2
    normed2 = (n2 * ffn_gain).astype(BF)
    normed2, ein = lax.optimization_barrier((normed2, ein))

    got_x = []
    for hits in to_slot:
        sent = jnp.dot(hits, normed2, preferred_element_type=F32).astype(BF)
        if got_x:
            sent, got_x[-1] = tie(sent, got_x[-1])
        got_x.append(swap(sent.reshape(owners, 1, capacity, width)))
    shared_w = jnp.concatenate([shared_in, shared_out[None]], axis=0)
    shared_w, got_x[0] = tie(shared_w, got_x[0])
    shared_full = lax.all_gather(shared_w, DC, axis=1, tiled=True)
    router_wide = jnp.pad(router_full, ((0, 0), (0, -experts % 128)))
    ys, back_dx, g_eins, g_eouts, routers = [], [], [], [], []
    for n in range(own):
        y, dx, g_ein, g_eout, g_router = ffn(
            got_x[n],
            got_g,
            ein,
            eout,
            4,
            ctx_count,
            (jnp.reshape(first + n, (1,)).astype(jnp.int32), slot_other, router_wide),
            n,
        )
        ys.append(y)
        g_eins.append(g_ein)
        g_eouts.append(g_eout)
        routers.append(g_router)
        if n + 1 < own:
            dx, got_x[n + 1] = tie(dx, got_x[n + 1])
        if back_dx:
            dx, back_dx[-1] = tie(dx, back_dx[-1])
        back_dx.append(swap(dx).reshape(-1, width))
    router_part = sum(routers)[:, :experts]
    g_ein = jnp.concatenate(g_eins, axis=1)
    g_eout = jnp.concatenate(g_eouts, axis=1)

    def to_owner(values):
        if spread:
            swapped = lax.all_to_all(values, "ctx", split_axis=0, concat_axis=0, tiled=True)
            return swapped.reshape((-1,) + values.shape[2:])
        return lax.psum_scatter(values, "ctx", scatter_dimension=0, tiled=True)[0]

    parts = 4
    shared_shape = (parts, 1, rows // parts, width)
    sh_y, sh_dx, sh_gin, sh_gout = ffn(
        normed2.reshape(shared_shape),
        grad_low.reshape(shared_shape),
        shared_full[None, :2],
        shared_full[None, 2],
        2,
        lax.axis_size(DC),
    )
    back_dx[-1], sh_dx = lax.optimization_barrier((back_dx[-1], sh_dx))

    from_slot = [
        ((place[:, 0, None] == ids[None, :]) | (place[:, 1, None] == ids[None, :])).astype(BF)
        for ids in block_ids
    ]

    def at_tokens(parts, local):
        total = local.reshape(rows, width).astype(F32)
        for hits, part in zip(from_slot, parts):
            total = total + jnp.dot(hits, part, preferred_element_type=F32)
        return total

    dn2_part = at_tokens(back_dx, sh_dx)
    dn2_low = dn2_part.astype(BF)
    dn2 = lax.psum(dn2_low, "tensor")
    sh_grad, dn2_low = tie(jnp.concatenate([sh_gin[:, 0], sh_gout], axis=1), dn2_low)
    shared_parts = lax.all_to_all(sh_grad, DC, split_axis=0, concat_axis=0, tiled=True)
    ys[0], shared_parts = tie(ys[0], shared_parts)
    total_shared = jnp.sum(shared_parts.astype(F32), axis=0)
    back_y = []
    for y in ys:
        if back_y:
            y, back_y[-1] = tie(y, back_y[-1])
        back_y.append(swap(y).reshape(-1, width))
    g_eout, back_y[-1] = tie(g_eout, back_y[-1])
    grad_eout = to_owner(g_eout)
    dn2 = dn2.astype(F32)
    gain2_part = jnp.sum(dn2_part * n2, axis=0)

    scaled2 = ffn_gain * dn2
    dresid = grad_layer + inv2 * (scaled2 - n2 * jnp.mean(scaled2 * n2, axis=-1, keepdims=True))
    dbranch = dresid.astype(BF)
    datt_t = jnp.einsum("dc,ld->cl", out_full, dbranch, preferred_element_type=F32).astype(BF)

    ffn_part = at_tokens(back_y, sh_y)
    ffn_low, datt_t = lax.optimization_barrier((ffn_part.astype(BF), datt_t))
    ffn_total = lax.psum(ffn_low, "tensor")

    dq_t, dk_win, dv_win = attn_backward(
        lo, q_t, k_win, v_win, att_t, datt_t, lse, doc, shift
    )
    dkv_win = jnp.concatenate([dk_win, dv_win], axis=0)
    dkv = dkv_win[:, shift:]
    for hop in range(1, before + 1):
        links = [(i + hop, i) for i in range(ctx_count - hop)]
        piece = dkv_win[:, shift - hop * rows : shift - (hop - 1) * rows]
        dkv = dkv + lax.ppermute(piece.astype(BF), "ctx", links).astype(F32)
    dq_raw = half_turn(dq_t, cos_t, -sin_t)
    dk_raw = half_turn(dkv[:heads_cols], cos_t, -sin_t)
    draw_t = jnp.concatenate([dq_raw, dk_raw, dkv[heads_cols:]], axis=0).astype(BF)
    g_ein, draw_t, grad_eout = tie(g_ein, draw_t, grad_eout)
    grad_ein = to_owner(g_ein)
    dn1_part = jnp.einsum("cl,dc->ld", draw_t, qkv_full, preferred_element_type=F32)
    dn1_low, ffn_total = lax.optimization_barrier((dn1_part.astype(BF), ffn_total))
    layer_out = (resid + ffn_total.astype(F32)).astype(BF)
    dn1 = lax.psum(dn1_low, "tensor")
    gain1_part = jnp.sum(dn1_part * n1, axis=0)
    grad_qkv = with_layout_constraint(
        jnp.einsum("ld,cl->dc", normed, draw_t, preferred_element_type=F32).astype(BF),
        Layout((0, 1)),
    )
    grad_outw = with_layout_constraint(
        jnp.einsum("ld,cl->dc", dbranch, att_t, preferred_element_type=F32).astype(BF),
        Layout((0, 1)),
    )
    small = jnp.concatenate([router_part, gain1_part[:, None], gain2_part[:, None]], axis=1).astype(BF)
    mixed, grad_ein = tie(jnp.concatenate([grad_qkv, grad_outw, small], axis=1), grad_ein)
    tail = own_sum(mixed, 0)
    small = lax.psum(tail[:, 4 * heads_cols :], "tensor")
    total_qkv = tail[:, : 3 * heads_cols].reshape(-1, 3, heads_cols).transpose(1, 0, 2)
    total_outw = tail[:, 3 * heads_cols : 4 * heads_cols]
    dn1, small = tie(dn1, small)
    dn1 = dn1.astype(F32)
    scaled1 = attn_gain * dn1
    grad_tokens = dresid + inv1 * (
        scaled1 - n1 * jnp.mean(scaled1 * n1, axis=-1, keepdims=True)
    )
    return (
        layer_out[None],
        grad_tokens[None],
        small[:, experts],
        total_qkv,
        total_outw,
        small[:, experts + 1],
        small[:, :experts],
        total_shared[:2],
        total_shared[2],
        grad_ein.astype(F32),
        grad_eout.astype(F32),
    )


def solution(mesh):
    return layer(mesh)


def layer(mesh):
    return jax.shard_map(
        shards,
        mesh=mesh,
        in_specs=(
            P("dp", "ctx", None),
            P("dp", None),
            P("dp", "ctx", None),
            P("dp", "ctx", None),
            P(DC),
            P(None, DC, "tensor"),
            P(DC, "tensor"),
            P(DC),
            P(DC, None),
            P(None, DC, "tensor"),
            P(DC, "tensor"),
            P("dp", None, "ctx", "tensor"),
            P("dp", "ctx", "tensor"),
            P("dp", "ctx", None),
        ),
        out_specs=(
            P("dp", "ctx", None),
            P("dp", "ctx", None),
            P(DC),
            P(None, DC, "tensor"),
            P(DC, "tensor"),
            P(DC),
            P(DC, None),
            P(None, DC, "tensor"),
            P(DC, "tensor"),
            P("dp", None, "ctx", "tensor"),
            P("dp", "ctx", "tensor"),
        ),
        check_vma=False,
    )
```

```python
import functools
import math

import jax
import jax.numpy as jnp
from jax import lax
from jax.experimental import pallas as pl
from jax.experimental.layout import Layout, with_layout_constraint
from jax.experimental.pallas import tpu as pltpu
from jax.sharding import PartitionSpec as P


HD = 64
HALF = HD // 2
EPSILON = 1e-06
LONGEST = 2000
DOCS = 5
BQ = 512
BK = 256
BF = jnp.bfloat16
F32 = jnp.float32
NEG = -1e30
DC = ("dp", "ctx")


def mm(a, b, ca, cb):
    return lax.dot_general(a, b, (((ca,), (cb,)), ((), ())), preferred_element_type=F32)


def attn_mask(key_start, query_start, doc_row):
    kpos = key_start + lax.broadcasted_iota(jnp.int32, (BK, BQ), 0)
    qpos = query_start + lax.broadcasted_iota(jnp.int32, (BK, BQ), 1)
    return (kpos <= qpos) & (kpos >= doc_row)


def attn_fwd_kernel(lo_ref, q_ref, k_ref, v_ref, doc_ref, o_ref, lse_ref, *, shift):
    cols, rows = q_ref.shape
    heads = [slice(at, at + HD) for at in range(0, cols, HD)]
    for qb in range(rows // BQ):
        here = slice(qb * BQ, (qb + 1) * BQ)
        qs = [q_ref[h, here] * 0.125 for h in heads]
        doc = doc_ref[:, here]
        q0 = shift + qb * BQ

        def step(b, carry, qs=qs, doc=doc, q0=q0):
            off = pl.multiple_of(b * BK, BK)
            mask = attn_mask(off, q0, doc)
            scores = [
                jnp.where(mask, mm(k_ref[h, pl.ds(off, BK)], q, 0, 0), NEG)
                for h, q in zip(heads, qs)
            ]
            out = []
            for h, s, (peak, total, acc) in zip(heads, scores, carry):
                new = jnp.maximum(peak, jnp.max(s, axis=0, keepdims=True))
                p = jnp.exp(s - new)
                fix = jnp.exp(peak - new)
                total = total * fix + jnp.sum(p, axis=0, keepdims=True)
                acc = acc * fix + mm(v_ref[h, pl.ds(off, BK)], p.astype(BF), 1, 0)
                out.append((new, total, acc))
            return tuple(out)

        init = tuple(
            (
                jnp.full((1, BQ), NEG, F32),
                jnp.zeros((1, BQ), F32),
                jnp.zeros((HD, BQ), F32),
            )
            for _ in heads
        )
        last = (q0 + BQ - 1) // BK
        carry = step(last, init)
        carry = lax.fori_loop(lo_ref[qb], last, step, carry)
        for n, (h, (peak, total, acc)) in enumerate(zip(heads, carry)):
            o_ref[h, here] = (acc / total).astype(BF)
            lse_ref[n : n + 1, here] = peak + jnp.log(total)


def attn_bwd_kernel(
    lo_ref, q_ref, k_ref, v_ref, o_ref, do_ref, lse_ref, doc_ref, dq_ref, dk_ref, dv_ref, *, shift
):
    cols, rows = q_ref.shape
    heads = [slice(at, at + HD) for at in range(0, cols, HD)]
    dk_ref[...] = jnp.zeros_like(dk_ref)
    dv_ref[...] = jnp.zeros_like(dv_ref)
    for qb in range(rows // BQ):
        here = slice(qb * BQ, (qb + 1) * BQ)
        qs = [q_ref[h, here] * 0.125 for h in heads]
        dos = [do_ref[h, here] for h in heads]
        doc = doc_ref[:, here]
        lses = [lse_ref[n : n + 1, here] for n in range(len(heads))]
        deltas = [
            jnp.sum(do.astype(F32) * o_ref[h, here].astype(F32), axis=0, keepdims=True)
            for h, do in zip(heads, dos)
        ]
        q0 = shift + qb * BQ

        def step(b, dqs, qs=qs, dos=dos, doc=doc, lses=lses, deltas=deltas, q0=q0):
            off = pl.multiple_of(b * BK, BK)
            keys = pl.ds(off, BK)
            mask = attn_mask(off, q0, doc)
            scores = [
                jnp.where(mask, mm(k_ref[h, keys], q, 0, 0), NEG) for h, q in zip(heads, qs)
            ]
            dps = [mm(v_ref[h, keys], do, 0, 0) for h, do in zip(heads, dos)]
            out = []
            for n, h in enumerate(heads):
                p = jnp.exp(scores[n] - lses[n])
                ds = (p * (dps[n] - deltas[n])).astype(BF)
                dk_ref[h, keys] += mm(qs[n], ds, 1, 1)
                dv_ref[h, keys] += mm(dos[n], p.astype(BF), 1, 1)
                out.append(dqs[n] + mm(k_ref[h, keys], ds, 1, 0))
            return tuple(out)

        last = (q0 + BQ - 1) // BK
        zero = tuple(jnp.zeros((HD, BQ), F32) for _ in heads)
        dqs = lax.fori_loop(lo_ref[qb], last + 1, step, zero)
        for h, dq in zip(heads, dqs):
            dq_ref[h, here] = dq * 0.125


def whole(shape, at=0):
    return pl.BlockSpec(shape, lambda n, lo: (at, 0))


def attn_forward(lo, q_t, kv_t, doc, shift):
    heads, rows = q_t.shape[0] // HD, q_t.shape[1]
    half = (q_t.shape[0], kv_t.shape[1])
    ins = (q_t, kv_t, kv_t, doc)
    outs = (
        jax.ShapeDtypeStruct(q_t.shape, BF),
        jax.ShapeDtypeStruct((heads, rows), F32),
    )
    return pl.pallas_call(
        functools.partial(attn_fwd_kernel, shift=shift),
        out_shape=outs,
        grid_spec=pltpu.PrefetchScalarGridSpec(
            num_scalar_prefetch=1,
            grid=(1,),
            in_specs=[whole(q_t.shape), whole(half), whole(half, 1)]
            + [whole(v.shape) for v in ins[3:]],
            out_specs=[whole(v.shape) for v in outs],
        ),
        name="attn_fwd",
    )(lo, *ins)


def attn_backward(lo, q_t, kv_t, o_t, do_t, lse, doc, shift):
    half = (q_t.shape[0], kv_t.shape[1])
    ins = (q_t, kv_t, kv_t, o_t, do_t, lse, doc)
    outs = (
        jax.ShapeDtypeStruct(q_t.shape, F32),
        jax.ShapeDtypeStruct(half, F32),
        jax.ShapeDtypeStruct(half, F32),
    )
    return pl.pallas_call(
        functools.partial(attn_bwd_kernel, shift=shift),
        out_shape=outs,
        grid_spec=pltpu.PrefetchScalarGridSpec(
            num_scalar_prefetch=1,
            grid=(1,),
            in_specs=[whole(q_t.shape), whole(half), whole(half, 1)]
            + [whole(v.shape) for v in ins[3:]],
            out_specs=[whole(v.shape) for v in outs],
        ),
        name="attn_bwd",
    )(lo, *ins)


def ffn_kernel(*refs, gated):
    if gated:
        first_ref, x_ref, g_ref, router_ref, win_ref, wout_ref = refs[:6]
        y_ref, dx_ref, gin_ref, gout_ref, grouter_ref, acc_in, acc_out, acc_router = refs[6:]
    else:
        x_ref, g_ref, win_ref, wout_ref = refs[:4]
        y_ref, dx_ref, gin_ref, gout_ref, acc_in, acc_out = refs[4:]
    src, _, rows, width = x_ref.shape
    expert, step = pl.program_id(0), pl.program_id(1)

    @pl.when(step == 0)
    def _():
        acc_in[...] = jnp.zeros_like(acc_in)
        acc_out[...] = jnp.zeros_like(acc_out)

    if gated:

        @pl.when((step == 0) & (expert == 0))
        def _():
            acc_router[...] = jnp.zeros_like(acc_router)

    x = x_ref[...].reshape(src * rows, width)
    g = g_ref[..., :width].reshape(src * rows, width)
    w_gate = win_ref[0, 0]
    w_up = win_ref[0, 1]
    w_out = wout_ref[0]
    gate_pre = mm(x, w_gate, 1, 0)
    up_pre = mm(x, w_up, 1, 0)
    sig = 1.0 / (1.0 + jnp.exp(-gate_pre))
    silu = gate_pre * sig
    hidden = (silu * up_pre).astype(BF)
    y = mm(hidden, w_out, 1, 1)
    if gated:
        router = router_ref[...]
        logits = mm(x, router, 1, 0)
        ids = lax.broadcasted_iota(jnp.int32, logits.shape, 1)
        here = ids == first_ref[0] + expert
        marks = g_ref[..., width : width + 128].reshape(src * rows, 128)
        other = marks[:, :1].astype(F32).astype(jnp.int32) - 1 - (first_ref[0] + expert)
        there = ids == other
        apart = jnp.sum(
            jnp.where(here, logits, 0.0) - jnp.where(there, logits, 0.0), axis=1, keepdims=True
        )
        gate = 1.0 / (1.0 + jnp.exp(-apart))
        gate_other = 1.0 / (1.0 + jnp.exp(apart))
        gf = g.astype(F32)
        dpair = gate * gate_other * jnp.sum(gf * y, axis=1, keepdims=True)
        dlogits = (jnp.where(here, dpair, 0.0) - jnp.where(there, dpair, 0.0)).astype(BF)
        acc_router[...] += mm(x, dlogits, 0, 0)
        dy = (gate * gf).astype(BF)
        y = gate * y
    else:
        dy = g
    y_ref[...] = y.astype(BF).reshape(src, 1, rows, width)
    dh = mm(dy, w_out, 1, 0)
    dgp = (dh * up_pre * (sig * (1.0 + gate_pre * (1.0 - sig)))).astype(BF)
    dup = (dh * silu).astype(BF)
    dx = mm(dgp, w_gate, 1, 1) + mm(dup, w_up, 1, 1)
    if gated:
        dx = dx + mm(dlogits, router, 1, 1)
    dx_ref[...] = dx.astype(BF).reshape(src, 1, rows, width)
    acc_in[0] += mm(x, dgp, 0, 0)
    acc_in[1] += mm(x, dup, 0, 0)
    acc_out[...] += mm(dy, hidden, 0, 0)

    @pl.when(step == pl.num_programs(1) - 1)
    def _():
        cut = gin_ref.shape[3]
        for n in range(gin_ref.shape[0]):
            gin_ref[n, 0] = acc_in[:, n * cut : (n + 1) * cut].astype(BF)
            gout_ref[n, 0] = acc_out[n * cut : (n + 1) * cut].astype(BF)
        if gated:
            grouter_ref[...] = acc_router[...]


def ffn(x, g, w_in, w_out, block, parts, routing=None, at=0):
    sources, experts, rows, width = x.shape
    units = w_out.shape[2]
    gated = routing is not None
    block = math.gcd(sources, block)
    big = pl.BlockSpec((block, 1, rows, width), lambda e, s, *_: (s, e, 0, 0))
    big_at = pl.BlockSpec((block, 1, rows, g.shape[3]), lambda e, s, *_: (s, at + e, 0, 0))
    w_in_at = pl.BlockSpec((1, 2, width, units), lambda e, s, *_: (at + e, 0, 0, 0))
    w_out_at = pl.BlockSpec((1, width, units), lambda e, s, *_: (at + e, 0, 0))
    cut = width // parts
    g_in_spec = pl.BlockSpec((parts, 1, 2, cut, units), lambda e, s, *_: (0, e, 0, 0, 0))
    g_out_spec = pl.BlockSpec((parts, 1, cut, units), lambda e, s, *_: (0, e, 0, 0))
    wide = jax.ShapeDtypeStruct(x.shape, BF)
    ins = [x, g]
    in_specs = [big, big_at]
    outs = [
        wide,
        wide,
        jax.ShapeDtypeStruct((parts, experts, 2, cut, units), BF),
        jax.ShapeDtypeStruct((parts, experts, cut, units), BF),
    ]
    out_specs = [big, big, g_in_spec, g_out_spec]
    scratch = [pltpu.VMEM((2, width, units), F32), pltpu.VMEM((width, units), F32)]
    if gated:
        first, router = routing
        router_spec = pl.BlockSpec(router.shape, lambda e, s, *_: (0, 0))
        ins = [first] + ins + [router]
        in_specs.append(router_spec)
        outs.append(jax.ShapeDtypeStruct(router.shape, F32))
        out_specs.append(router_spec)
        scratch.append(pltpu.VMEM(router.shape, F32))
    return pl.pallas_call(
        functools.partial(ffn_kernel, gated=gated),
        out_shape=outs,
        grid_spec=pltpu.PrefetchScalarGridSpec(
            num_scalar_prefetch=1 if gated else 0,
            grid=(experts, sources // block),
            in_specs=in_specs + [w_in_at, w_out_at],
            out_specs=out_specs,
            scratch_shapes=scratch,
        ),
        compiler_params=pltpu.CompilerParams(
            dimension_semantics=("arbitrary", "arbitrary"), vmem_limit_bytes=56 * 1024 * 1024
        ),
        name="ffn_experts" if gated else "ffn_shared",
    )(*ins, w_in, w_out)


def tie(*values):
    return lax.optimization_barrier(values)


def pair_slots(pair_route, order, experts, capacity):
    count = order.shape[0]
    flat = pair_route.reshape(count)
    number = jnp.arange(count, dtype=jnp.int32)
    ids = jnp.arange(experts, dtype=jnp.int32)
    owner = (flat[:, None] == ids[None, :]).astype(BF)
    ranked = jnp.dot(
        (order[:, None] == number[None, :]).astype(BF), owner, preferred_element_type=F32
    ).astype(BF)
    earlier = jnp.dot(
        (number[None, :] < number[:, None]).astype(BF), ranked, preferred_element_type=F32
    )
    ranked_slot = (jnp.minimum(earlier, float(capacity)) * ranked).astype(BF)
    slot = jnp.sum(
        jnp.dot(
            (order[None, :] == number[:, None]).astype(BF),
            ranked_slot,
            preferred_element_type=F32,
        ),
        axis=1,
    ).astype(jnp.int32)
    place = jnp.where(slot < capacity, flat * capacity + slot, experts * capacity)
    return place.reshape(pair_route.shape)


def own_sum(parts, axis):
    devices = lax.axis_size(DC)
    shape = parts.shape
    cut = shape[:axis] + (devices, shape[axis] // devices) + shape[axis + 1 :]
    swapped = lax.all_to_all(
        parts.astype(BF).reshape(cut), DC, split_axis=axis, concat_axis=axis, tiled=True
    )
    return jnp.sum(swapped.astype(F32), axis=axis)


def half_turn(values_t, cos_t, sin_t):
    cols, rows = values_t.shape
    split = values_t.reshape(cols // HD, 2, HALF, rows)
    a, b = split[:, 0], split[:, 1]
    return jnp.stack([a * cos_t - b * sin_t, b * cos_t + a * sin_t], axis=1).reshape(cols, rows)


def shards(
    tokens,
    segment_ids,
    routes,
    pair_order,
    gain_attn,
    qkv_weight,
    out_weight,
    gain_ffn,
    router_weight,
    shared_in,
    shared_out,
    expert_in,
    expert_out,
    out_grad,
):
    rows, width = tokens.shape[1], tokens.shape[2]
    ctx_count = lax.axis_size("ctx")
    ctx_at = lax.axis_index("ctx")
    inputs = tokens[0].astype(F32)
    grad_low = out_grad[0]
    grad_layer = grad_low.astype(F32)
    seg_all = segment_ids[0]
    my_routes = routes[0]

    heads_cols = qkv_weight.shape[2]
    qkv_cols = 3 * heads_cols
    experts = router_weight.shape[1]
    tensor_count = lax.axis_size("tensor")
    first_w = jnp.concatenate(
        [qkv_weight.transpose(1, 0, 2).reshape(-1, qkv_cols), gain_attn[:, None]], axis=1
    )
    first_full = lax.all_gather(first_w, DC, axis=0, tiled=True)
    qkv_full = first_full[:, :qkv_cols]
    attn_gain = first_full[:, qkv_cols].astype(F32)
    rings = [
        [(i, (i + hop) % tensor_count) for i in range(tensor_count)]
        for hop in range(1, tensor_count)
    ]
    second_w = jnp.concatenate(
        [out_weight]
        + [lax.ppermute(out_weight, "tensor", links) for links in rings]
        + [router_weight, gain_ffn[:, None]],
        axis=1,
    )

    local_experts = expert_in.shape[0]
    spread = local_experts % ctx_count == 0
    expert_axes = DC if spread else ("dp",)
    owners = lax.axis_size(expert_axes)
    own = experts // owners
    capacity = 10 * rows // (4 * experts)

    def swap(values):
        return lax.all_to_all(values, expert_axes, split_axis=0, concat_axis=0, tiled=True)

    place = pair_slots(my_routes, pair_order[0, 0], experts, capacity)
    block_ids = [
        (
            jnp.arange(owners, dtype=jnp.int32)[:, None] * (own * capacity)
            + (n * capacity + jnp.arange(capacity, dtype=jnp.int32))[None, :]
        ).reshape(-1)
        for n in range(own)
    ]
    first = lax.axis_index(expert_axes) * own
    sums = (jnp.sum(my_routes, axis=1, keepdims=True) + 1).astype(BF)
    marked = jnp.concatenate([grad_low, jnp.pad(sums, ((0, 0), (0, 127)))], axis=1)
    to_slot = [
        ((place[None, :, 0] == ids[:, None]) | (place[None, :, 1] == ids[:, None])).astype(BF)
        for ids in block_ids
    ]
    slot_g = jnp.stack(
        [
            jnp.dot(hits, marked, preferred_element_type=F32)
            .astype(BF)
            .reshape(owners, capacity, width + 128)
            for hits in to_slot
        ],
        axis=1,
    )

    inv1 = lax.rsqrt(jnp.mean(inputs * inputs, axis=-1, keepdims=True) + EPSILON)
    n1 = inputs * inv1
    normed = (n1 * attn_gain).astype(BF)
    row_start = ctx_at * rows
    query_pos = row_start + jnp.arange(rows, dtype=jnp.int32)
    inverse = 1.0 / 10000.0 ** (jnp.arange(HALF, dtype=F32) * (2.0 / HD))
    angles = inverse[:, None] * query_pos.astype(F32)[None, :]
    cos_t, sin_t = jnp.cos(angles), jnp.sin(angles)
    expert_out, qkv_full = tie(expert_out, qkv_full)
    if spread:
        eout = lax.all_to_all(expert_out, "ctx", split_axis=0, concat_axis=1, tiled=True)
    else:
        eout = lax.all_gather(expert_out, "ctx", axis=1, tiled=True)
    raw_t = jnp.einsum("dc,ld->cl", qkv_full, normed, preferred_element_type=F32)
    q_t = half_turn(raw_t[:heads_cols], cos_t, sin_t).astype(BF)
    k_t = half_turn(raw_t[heads_cols : 2 * heads_cols], cos_t, sin_t).astype(BF)
    v_t = raw_t[2 * heads_cols :].astype(BF)
    kv_t = jnp.concatenate([k_t, v_t], axis=0)
    before = min(ctx_count - 1, -(-(LONGEST - 1) // rows))
    shift = before * rows
    pieces = [kv_t]
    for hop in range(1, before + 1):
        links = [(i, i + hop) for i in range(ctx_count - hop)]
        pieces.insert(0, lax.ppermute(kv_t, "ctx", links))
    kv_win = jnp.concatenate(pieces, axis=1)
    kv_win, slot_g, second_w, eout = tie(kv_win, slot_g, second_w, eout)

    got_g = swap(slot_g)
    second_full = lax.all_gather(second_w, DC, axis=0, tiled=True)
    out_all = second_full[:, : tensor_count * heads_cols]
    out_full = out_all[:, :heads_cols]
    router_full = second_full[:, tensor_count * heads_cols : -1]
    ffn_gain = second_full[:, -1].astype(F32)

    starts = jnp.sum(
        seg_all[:, None] < jnp.arange(DOCS, dtype=jnp.int32)[None, :], axis=0, dtype=jnp.int32
    )
    query_seg = lax.dynamic_slice_in_dim(seg_all, row_start, rows)
    doc = jnp.sum(
        jnp.where(
            query_seg[:, None] == jnp.arange(DOCS, dtype=jnp.int32)[None, :], starts[None, :], 0
        ),
        axis=1,
    ) - (row_start - shift)
    lo = jnp.maximum(doc[::BQ], 0) // BK
    doc = doc[None, :]
    att_t, lse = attn_forward(lo, q_t, kv_win, doc, shift)
    expert_in, lse, got_g = tie(expert_in, lse, got_g)
    if spread:
        ein = lax.all_to_all(expert_in, "ctx", split_axis=0, concat_axis=2, tiled=True)
    else:
        ein = lax.all_gather(expert_in, "ctx", axis=2, tiled=True)
    att_parts = [att_t] + [lax.ppermute(att_t, "tensor", links) for links in rings]
    branch = jnp.einsum(
        "cl,dc->ld", jnp.concatenate(att_parts, axis=0), out_all, preferred_element_type=F32
    )
    branch = with_layout_constraint(branch, Layout((0, 1)))
    resid = inputs + branch

    inv2 = lax.rsqrt(jnp.mean(resid * resid, axis=-1, keepdims=True) + EPSILON)
    n2 = resid * inv2
    normed2 = (n2 * ffn_gain).astype(BF)
    normed2, ein = lax.optimization_barrier((normed2, ein))

    got_x = []
    for hits in to_slot:
        sent = jnp.dot(hits, normed2, preferred_element_type=F32).astype(BF)
        if got_x:
            sent, got_x[-1] = tie(sent, got_x[-1])
        got_x.append(swap(sent.reshape(owners, 1, capacity, width)))
    shared_w = jnp.concatenate([shared_in, shared_out[None]], axis=0)
    shared_w, got_x[0] = tie(shared_w, got_x[0])
    shared_full = lax.all_gather(shared_w, DC, axis=1, tiled=True)
    router_wide = jnp.pad(router_full, ((0, 0), (0, -experts % 128)))
    ys, back_dx, g_eins, g_eouts, routers = [], [], [], [], []
    for n in range(own):
        y, dx, g_ein, g_eout, g_router = ffn(
            got_x[n],
            got_g,
            ein,
            eout,
            4,
            ctx_count,
            (jnp.reshape(first + n, (1,)).astype(jnp.int32), router_wide),
            n,
        )
        ys.append(y)
        g_eins.append(g_ein)
        g_eouts.append(g_eout)
        routers.append(g_router)
        if n + 1 < own:
            dx, got_x[n + 1] = tie(dx, got_x[n + 1])
        if back_dx:
            dx, back_dx[-1] = tie(dx, back_dx[-1])
        back_dx.append(swap(dx).reshape(-1, width))
    router_part = sum(routers)[:, :experts]
    g_ein = jnp.concatenate(g_eins, axis=1)
    g_eout = jnp.concatenate(g_eouts, axis=1)

    def to_owner(values):
        if spread:
            swapped = lax.all_to_all(values, "ctx", split_axis=0, concat_axis=0, tiled=True)
            return swapped.reshape((-1,) + values.shape[2:])
        return lax.psum_scatter(values, "ctx", scatter_dimension=0, tiled=True)[0]

    parts = 4
    shared_shape = (parts, 1, rows // parts, width)
    sh_y, sh_dx, sh_gin, sh_gout = ffn(
        normed2.reshape(shared_shape),
        grad_low.reshape(shared_shape),
        shared_full[None, :2],
        shared_full[None, 2],
        2,
        lax.axis_size(DC),
    )
    back_dx[-1], sh_dx = lax.optimization_barrier((back_dx[-1], sh_dx))

    from_slot = [
        ((place[:, 0, None] == ids[None, :]) | (place[:, 1, None] == ids[None, :])).astype(BF)
        for ids in block_ids
    ]

    def at_tokens(parts, local):
        total = local.reshape(rows, width).astype(F32)
        for hits, part in zip(from_slot, parts):
            total = total + jnp.dot(hits, part, preferred_element_type=F32)
        return total

    dn2_part = at_tokens(back_dx, sh_dx)
    dn2_low = dn2_part.astype(BF)
    dn2 = lax.psum(dn2_low, "tensor")
    ys[0], dn2_low = tie(ys[0], dn2_low)
    back_y = []
    for y in ys:
        if back_y:
            y, back_y[-1] = tie(y, back_y[-1])
        back_y.append(swap(y).reshape(-1, width))
    sh_grad, back_y[-1] = tie(jnp.concatenate([sh_gin[:, 0], sh_gout], axis=1), back_y[-1])
    shared_parts = lax.all_to_all(sh_grad, DC, split_axis=0, concat_axis=0, tiled=True)
    dn2, back_y[-1] = tie(dn2, back_y[-1])
    dn2 = dn2.astype(F32)
    gain2_part = jnp.sum(dn2_part * n2, axis=0)

    scaled2 = ffn_gain * dn2
    dresid = grad_layer + inv2 * (scaled2 - n2 * jnp.mean(scaled2 * n2, axis=-1, keepdims=True))
    dbranch = dresid.astype(BF)
    datt_t = jnp.einsum("dc,ld->cl", out_full, dbranch, preferred_element_type=F32).astype(BF)

    ffn_part = at_tokens(back_y, sh_y)
    ffn_low, datt_t = lax.optimization_barrier((ffn_part.astype(BF), datt_t))
    ffn_total = lax.psum(ffn_low, "tensor")

    dq_t, dk_win, dv_win = attn_backward(
        lo, q_t, kv_win, att_t, datt_t, lse, doc, shift
    )
    dkv_win = jnp.concatenate([dk_win, dv_win], axis=0)
    dkv = dkv_win[:, shift:]
    for hop in range(1, before + 1):
        links = [(i + hop, i) for i in range(ctx_count - hop)]
        piece = dkv_win[:, shift - hop * rows : shift - (hop - 1) * rows]
        dkv = dkv + lax.ppermute(piece.astype(BF), "ctx", links).astype(F32)
    dq_raw = half_turn(dq_t, cos_t, -sin_t)
    dk_raw = half_turn(dkv[:heads_cols], cos_t, -sin_t)
    draw_t = jnp.concatenate([dq_raw, dk_raw, dkv[heads_cols:]], axis=0).astype(BF)
    g_eout, draw_t, shared_parts = tie(g_eout, draw_t, shared_parts)
    total_shared = jnp.sum(shared_parts.astype(F32), axis=0)
    grad_eout = to_owner(g_eout)
    dn1_part = jnp.einsum("cl,dc->ld", draw_t, qkv_full, preferred_element_type=F32)
    dn1_low, ffn_total = lax.optimization_barrier((dn1_part.astype(BF), ffn_total))
    layer_out = (resid + ffn_total.astype(F32)).astype(BF)
    dn1 = lax.psum(dn1_low, "tensor")
    gain1_part = jnp.sum(dn1_part * n1, axis=0)
    grad_qkv = with_layout_constraint(
        jnp.einsum("ld,cl->dc", normed, draw_t, preferred_element_type=F32).astype(BF),
        Layout((0, 1)),
    )
    grad_outw = with_layout_constraint(
        jnp.einsum("ld,cl->dc", dbranch, att_t, preferred_element_type=F32).astype(BF),
        Layout((0, 1)),
    )
    small = jnp.concatenate([router_part, gain1_part[:, None], gain2_part[:, None]], axis=1).astype(BF)
    mixed, grad_eout = tie(jnp.concatenate([grad_qkv, grad_outw, small], axis=1), grad_eout)
    tail = own_sum(mixed, 0)
    g_ein, tail = tie(g_ein, tail)
    grad_ein = to_owner(g_ein)
    small = lax.psum(tail[:, 4 * heads_cols :], "tensor")
    total_qkv = tail[:, : 3 * heads_cols].reshape(-1, 3, heads_cols).transpose(1, 0, 2)
    total_outw = tail[:, 3 * heads_cols : 4 * heads_cols]
    dn1, small = tie(dn1, small)
    dn1 = dn1.astype(F32)
    scaled1 = attn_gain * dn1
    grad_tokens = dresid + inv1 * (
        scaled1 - n1 * jnp.mean(scaled1 * n1, axis=-1, keepdims=True)
    )
    return (
        layer_out[None],
        grad_tokens[None],
        small[:, experts],
        total_qkv,
        total_outw,
        small[:, experts + 1],
        small[:, :experts],
        total_shared[:2],
        total_shared[2],
        grad_ein.astype(F32),
        grad_eout.astype(F32),
    )


def solution(mesh):
    return layer(mesh)


def layer(mesh):
    return jax.shard_map(
        shards,
        mesh=mesh,
        in_specs=(
            P("dp", "ctx", None),
            P("dp", None),
            P("dp", "ctx", None),
            P("dp", "ctx", None),
            P(DC),
            P(None, DC, "tensor"),
            P(DC, "tensor"),
            P(DC),
            P(DC, None),
            P(None, DC, "tensor"),
            P(DC, "tensor"),
            P("dp", None, "ctx", "tensor"),
            P("dp", "ctx", "tensor"),
            P("dp", "ctx", None),
        ),
        out_specs=(
            P("dp", "ctx", None),
            P("dp", "ctx", None),
            P(DC),
            P(None, DC, "tensor"),
            P(DC, "tensor"),
            P(DC),
            P(DC, None),
            P(None, DC, "tensor"),
            P(DC, "tensor"),
            P("dp", None, "ctx", "tensor"),
            P("dp", "ctx", "tensor"),
        ),
        check_vma=False,
    )
```
